128 devices in a mesh: tx: 16 (over x, y), ty: 8 (over z, core).
Axes of the slice: x: 4, y: 4, z: 4, core: 2. Of those that a mesh axis runs over, the one named last changes fastest.
Arguments:
- object_field: float32 [2, 8192, 4096], P(None, 'tx', 'ty'), may hold values from -5 to 5
- probe_field: float32 [2, 256, 256], replicated, may hold values from -5 to 5
- amplitudes: float32 [768, 2048, 256], P('tx', 'ty'), may hold values from 0.3 to 3
- scan_blocks: int32 [2048, 2], P(('tx', 'ty')), may hold values from 0 to 63, as said below
- owner_rows: int32 [2048], P(('tx', 'ty')), may hold values from 0 to 15, as said below
Outputs:
- refined_object: float32 [2, 8192, 4096], P(None, 'tx', 'ty')
The draws below stay inside these ranges and needn't reach their ends.
Inputs may be any that keep to these rules, and one draw needn't show every extreme that they name: `scan_blocks`: position p has home device p // 16 in tx-major order; its block row lies within that device's 512 rows divided by 128, its block column within its 512 columns divided by 128. `owner_rows`: of one home device's positions at most 3 share an owner, and in every ty column some home device has exactly 3 positions with the same owner; one owner holds at most 40 positions, and some hold exactly that many.
All inputs are finite; a program needn't handle non-finite values.
Results may differ from the reference program's by a relative error of at most 0.0042.
Values may be sent and summed in bfloat16 or wider, within the bound.
A program may use at most 128 MiB of HBM per device.

```python
import math
import jax
import jax.numpy as jnp
from jax import lax

WIN = 256
BLOCK = 128
TILE_R = 512
TILE_C = 512
POS_DEV = 16
STEPS = 4
MOST = 3
SLOTS = 48
POSITIONS = 2048
NR = 8192
NC = 4096
N_TX = 16
N_TY = 8


def scan_layout(key):
    layout_key = jax.random.fold_in(key, 11)
    subkeys = jax.random.split(layout_key, 4)
    home_count = N_TX * N_TY
    position_ids = jnp.arange(POS_DEV * home_count, dtype=jnp.int32)
    home_row = position_ids // (N_TY * POS_DEV)
    home_col = position_ids // POS_DEV % N_TY
    offset_rows = jax.random.randint(subkeys[0], (POS_DEV * home_count,), 0, TILE_R // BLOCK, dtype=jnp.int32)
    offset_cols = jax.random.randint(subkeys[1], (POS_DEV * home_count,), 0, TILE_C // BLOCK, dtype=jnp.int32)
    blocks = jnp.stack([home_row * (TILE_R // BLOCK) + offset_rows, home_col * (TILE_C // BLOCK) + offset_cols], axis=1).astype(jnp.int32)
    orders = jax.vmap(lambda subkey: jax.random.permutation(subkey, POS_DEV))(jax.random.split(subkeys[2], home_count)).reshape(POS_DEV * home_count).astype(jnp.int32)
    column_orders = jax.vmap(lambda subkey: jax.random.permutation(subkey, N_TX))(jax.random.split(subkeys[3], N_TY)).astype(jnp.int32)
    shifted = home_row + orders
    target = jnp.where(orders < POS_DEV // 2, shifted % N_TX, shifted % (N_TX // 4))
    owners = column_orders[home_col, target]
    return (blocks, owners.astype(jnp.int32))


def draw_scan_blocks(key, part):
    return scan_layout(key)[0]


def draw_owner_rows(key, part):
    return scan_layout(key)[1]


def level_of(own_key, extent, pieces, smallest, largest):
    gain = 1.0
    for dim, blocks in pieces:
        steps = jax.random.uniform(jax.random.fold_in(jax.random.fold_in(own_key, 6), dim), (blocks,), jnp.float32, smallest / len(pieces), largest / len(pieces))
        gain = gain * jnp.repeat(jnp.exp(steps), extent[dim] // blocks).reshape((-1,) + (1,) * (len(extent) - 1 - dim))
    return gain


def gaussian(rng, extent, scale, reach, shards=(), kind=jnp.bfloat16):
    factor_of = level_of(rng, extent, shards, -0.22, 0.18) if shards else 1.0
    values = jax.random.normal(rng, extent, jnp.float32) * scale * factor_of
    return jnp.minimum(jnp.maximum(values, -reach), reach).astype(kind)


def setup_inputs(seed: int = 0) -> dict:
    arg_keys = jax.random.split(jax.random.key(seed), 6)
    object_field = gaussian(arg_keys[0], (2, NR, NC), 0.7, 5.0, ((1, 16), (2, 8)), jnp.float32)
    probe_field = gaussian(arg_keys[1], (2, WIN, WIN), 0.7, 5.0, (), jnp.float32)
    amplitudes = jnp.clip(jnp.exp(math.log(3.0) - 2.3025851 * jax.random.uniform(arg_keys[2], (N_TX * SLOTS, N_TY * WIN, WIN), jnp.float32) ** level_of(arg_keys[2], (N_TX * SLOTS, N_TY * WIN, WIN), ((0, 16), (1, 8)), -0.2, 0.2)), 0.3, 3.0)
    scan_blocks = draw_scan_blocks(jax.random.fold_in(arg_keys[5], 71), 0)
    owner_rows = draw_owner_rows(jax.random.fold_in(arg_keys[5], 71), 0)
    return dict(object_field=object_field, probe_field=probe_field, amplitudes=amplitudes, scan_blocks=scan_blocks, owner_rows=owner_rows)


KAPPA_SQ = 1.0
TIME_STEP = 0.2
AMPLITUDE_FLOOR = 0.5

def dft_tables(window_cells):
    counter = jnp.arange(window_cells, dtype=jnp.int32)
    phases = counter[:, None] * counter[None, :] % window_cells
    angles = phases.astype(jnp.float32) * (2.0 * jnp.pi / window_cells)
    scaling = 1.0 / jnp.sqrt(jnp.asarray(window_cells, jnp.float32))
    return ((jnp.cos(angles) * scaling).astype(jnp.bfloat16), (jnp.sin(angles) * scaling).astype(jnp.bfloat16))

def matmul(first, second):
    return jnp.dot(first, second, preferred_element_type=jnp.float32)

def apply_left(cosine, sine, real_part, imag_part, signum):
    return (matmul(cosine, real_part) + signum * matmul(sine, imag_part), matmul(cosine, imag_part) - signum * matmul(sine, real_part))

def apply_right(cosine, sine, real_part, imag_part, signum):
    return (matmul(real_part, cosine) + signum * matmul(imag_part, sine), matmul(imag_part, cosine) - signum * matmul(real_part, sine))

def position_gradient(window, probe_field, measured, cosine, sine):
    probe_re = probe_field[0]
    probe_im = probe_field[1]
    wave_re = (probe_re * window[0] - probe_im * window[1]).astype(jnp.bfloat16)
    wave_im = (probe_re * window[1] + probe_im * window[0]).astype(jnp.bfloat16)
    half_re, half_im = apply_left(cosine, sine, wave_re, wave_im, 1.0)
    far_re, far_im = apply_right(cosine, sine, half_re.astype(jnp.bfloat16), half_im.astype(jnp.bfloat16), 1.0)
    magnitude = jnp.sqrt(far_re * far_re + far_im * far_im)
    factor = 1.0 - measured / jnp.maximum(magnitude, AMPLITUDE_FLOOR)
    back_re, back_im = apply_left(cosine, sine, (far_re * factor).astype(jnp.bfloat16), (far_im * factor).astype(jnp.bfloat16), -1.0)
    near_re, near_im = apply_right(cosine, sine, back_re.astype(jnp.bfloat16), back_im.astype(jnp.bfloat16), -1.0)
    grad_re = (probe_re * near_re + probe_im * near_im).astype(jnp.bfloat16)
    grad_im = (probe_re * near_im - probe_im * near_re).astype(jnp.bfloat16)
    return jnp.stack([grad_re, grad_im])

def smooth_pass(padded):
    center = padded[:, 1:-1, 1:-1]
    flux_sum = jnp.zeros_like(center)
    for neighbour in (padded[:, :-2, 1:-1], padded[:, 2:, 1:-1], padded[:, 1:-1, :-2], padded[:, 1:-1, 2:]):
        difference = neighbour - center
        weight = 1.0 / (1.0 + (difference[0] * difference[0] + difference[1] * difference[1]) / KAPPA_SQ)
        flux_sum = flux_sum + weight * difference
    return center + TIME_STEP * flux_sum

def reference(object_field, probe_field, amplitudes, scan_blocks, owner_rows):
    cosine, sine = dft_tables(WIN)
    owner_group = owner_rows.reshape(N_TX * N_TY, POS_DEV)
    earlier_mask = jnp.arange(POS_DEV)[None, :] < jnp.arange(POS_DEV)[:, None]
    same_owner = owner_group[:, :, None] == owner_group[:, None, :]
    pair_rank = lax.optimization_barrier(jnp.sum(same_owner & earlier_mask[None], axis=2)).astype(jnp.int32).reshape(POSITIONS)
    position_ids = jnp.arange(POSITIONS, dtype=jnp.int32)
    home_row = position_ids // (N_TY * POS_DEV)
    home_col = position_ids // POS_DEV % N_TY
    slot_row = (owner_rows * SLOTS + home_row * MOST + pair_rank).astype(jnp.int32)
    records = jnp.stack([scan_blocks[:, 0], scan_blocks[:, 1], slot_row, home_col.astype(jnp.int32)], axis=1).astype(jnp.int32)
    padded_object = jnp.pad(object_field, ((0, 0), (0, BLOCK), (0, BLOCK)))
    illumination_window = probe_field[0] * probe_field[0] + probe_field[1] * probe_field[1]
    anchor = jnp.zeros((), jnp.int32)

    def deposit_one(accumulated, record):
        gradient_sum, illumination = accumulated
        start_row = (record[0] * BLOCK).astype(jnp.int32)
        start_col = (record[1] * BLOCK).astype(jnp.int32)
        window = lax.dynamic_slice(padded_object, (anchor, start_row, start_col), (2, WIN, WIN))
        measured = lax.dynamic_slice(amplitudes, (record[2], (record[3] * WIN).astype(jnp.int32), anchor), (1, WIN, WIN))[0]
        gradient = position_gradient(window, probe_field, measured, cosine, sine).astype(jnp.float32)
        region = lax.dynamic_slice(gradient_sum, (anchor, start_row, start_col), (2, WIN, WIN))
        gradient_sum = lax.dynamic_update_slice(gradient_sum, region + gradient, (anchor, start_row, start_col))
        lit_region = lax.dynamic_slice(illumination, (start_row, start_col), (WIN, WIN))
        illumination = lax.dynamic_update_slice(illumination, lit_region + illumination_window, (start_row, start_col))
        return ((gradient_sum, illumination), None)
    initial = (jnp.zeros((2, NR + BLOCK, NC + BLOCK), jnp.float32), jnp.zeros((NR + BLOCK, NC + BLOCK), jnp.float32))
    (gradient_sum, illumination), unused = lax.scan(deposit_one, initial, records)
    updated = object_field - gradient_sum[:, :NR, :NC] / (illumination[:NR, :NC] + 1.0)
    for number in range(STEPS):
        updated = smooth_pass(jnp.pad(updated, ((0, 0), (1, 1), (1, 1))))
    return updated
```

```python
import functools

import jax
import jax.numpy as jnp
import numpy as np
from jax import lax
from jax.experimental import pallas as pl
from jax.experimental.pallas import tpu as pltpu
from jax.sharding import PartitionSpec as P

STEPS = 4


KAPPA_SQ = 1.0
TIME_STEP = 0.2
AMPLITUDE_FLOOR = 0.5


def from_behind(value, axis, steps):
    count = lax.axis_size(axis)
    initial, last = (max(0, -steps), min(count, count - steps))
    return lax.ppermute(value, axis, [(source, source + steps) for source in range(initial, last)])


def extended_2(array, sides, width):
    for axis, dim in sides:
        peers, length = (lax.axis_size(axis), array.shape[dim])
        up = [(i, (i + 1) % peers) for i in range(peers - 1)]
        down = [(j, i) for i, j in up]
        last = lax.slice_in_dim(array, length - width, length, axis=dim)
        initial = lax.slice_in_dim(array, 0, width, axis=dim)
        before = lax.ppermute(last, axis, up)
        after = lax.ppermute(initial, axis, down)
        array = jnp.concatenate([before, array, after], axis=dim)
    return array


def complex_tables(window_cells):
    counter = np.arange(window_cells)
    phases = counter[:, None] * counter[None, :] % window_cells
    angles = phases.astype(np.float32) * np.float32(2.0 * np.pi / window_cells)
    scaling = np.float32(1.0 / np.sqrt(window_cells))
    cosine, sine = (np.cos(angles) * scaling, np.sin(angles) * scaling)
    ahead = np.block([[cosine, sine], [-sine, cosine]])
    conjugate = np.block([[cosine, -sine], [sine, cosine]])
    return jnp.asarray(ahead, jnp.bfloat16), jnp.asarray(conjugate, jnp.bfloat16)


def matmul(first, second):
    return jnp.dot(first, second, preferred_element_type=jnp.float32)


def corner_of(number, spots, cells):
    start_row = pl.multiple_of(number // spots * cells, cells)
    start_col = pl.multiple_of(number % spots * cells, cells)
    return start_row, start_col


def forward_kernel(spots, extended, probe, ahead, conjugate, far_out, phase_out):
    cells = probe.shape[1]
    start_row, start_col = corner_of(pl.program_id(0), spots, cells // 2)
    view = (pl.ds(start_row, cells), pl.ds(start_col, cells))
    window_re, window_im = extended[(0, *view)], extended[(1, *view)]
    probe_re, probe_im = probe[0], probe[1]
    wave_re = (probe_re * window_re - probe_im * window_im).astype(jnp.bfloat16)
    wave_im = (probe_re * window_im + probe_im * window_re).astype(jnp.bfloat16)
    half = matmul(ahead[...], jnp.concatenate([wave_re, wave_im], axis=0)).astype(jnp.bfloat16)
    far = matmul(jnp.concatenate([half[:cells], half[cells:]], axis=1), conjugate[...])
    far_re, far_im = far[:, :cells], far[:, cells:]
    inverse = jnp.minimum(
        lax.rsqrt(far_re * far_re + far_im * far_im), 1.0 / AMPLITUDE_FLOOR
    )
    far_out[0, 0] = far_re.astype(jnp.bfloat16)
    far_out[0, 1] = far_im.astype(jnp.bfloat16)
    phase_out[0, 0] = (far_re * inverse).astype(jnp.bfloat16)
    phase_out[0, 1] = (far_im * inverse).astype(jnp.bfloat16)


def backward_kernel(
    spots, slots, starts, far, phase, arrived, probe, ahead, conjugate, grads, light, measured
):
    cells = probe.shape[1]
    number = pl.program_id(0)

    @pl.when(number == 0)
    def _():
        grads[...] = jnp.zeros_like(grads)
        light[...] = jnp.zeros_like(light)

    first, last = starts[number], starts[number + 1]

    @pl.when(last > first)
    def _():
        measured[...] = arrived[slots[first]].astype(jnp.float32)

        def add_one(index, carry):
            measured[...] += arrived[slots[index]].astype(jnp.float32)
            return carry

        lax.fori_loop(first + 1, last, add_one, 0)
        count = (last - first).astype(jnp.float32)
        total = measured[...]
        residual = [
            (far[0, part].astype(jnp.float32) * count
             - phase[0, part].astype(jnp.float32) * total).astype(jnp.bfloat16)
            for part in range(2)
        ]
        back = matmul(conjugate[...], jnp.concatenate(residual, axis=0)).astype(jnp.bfloat16)
        near = matmul(jnp.concatenate([back[:cells], back[cells:]], axis=1), ahead[...])
        near_re, near_im = near[:, :cells], near[:, cells:]
        probe_re, probe_im = probe[0], probe[1]
        start_row, start_col = corner_of(number, spots, cells // 2)
        view = (pl.ds(start_row, cells), pl.ds(start_col, cells))
        grads[(0, *view)] += probe_re * near_re + probe_im * near_im
        grads[(1, *view)] += probe_re * near_im - probe_im * near_re
        light[view] += count * (probe_re * probe_re + probe_im * probe_im)


def whole(shape):
    return pl.BlockSpec(shape, lambda *_: (0,) * len(shape))


def smooth_pass(padded):
    center = padded[:, 1:-1, 1:-1]
    flux_sum = jnp.zeros_like(center)
    for neighbour in (
        padded[:, :-2, 1:-1],
        padded[:, 2:, 1:-1],
        padded[:, 1:-1, :-2],
        padded[:, 1:-1, 2:],
    ):
        difference = neighbour - center
        weight = 1.0 / (
            1.0 + (difference[0] * difference[0] + difference[1] * difference[1]) / KAPPA_SQ
        )
        flux_sum = flux_sum + weight * difference
    return center + TIME_STEP * flux_sum


def local(object_field, probe_field, amplitudes, scan_blocks, owner_rows):
    tile_rows, tile_cols = object_field.shape[1:]
    window_cells = probe_field.shape[1]
    block_cells = window_cells // 2
    positions_here = owner_rows.shape[0]
    pair_slots = amplitudes.shape[0] // lax.axis_size("tx")
    spots = tile_cols // block_cells
    windows = tile_rows // block_cells * spots
    ext_rows, ext_cols = tile_rows + block_cells, tile_cols + block_cells

    arrived = lax.all_to_all(
        amplitudes.astype(jnp.bfloat16), "tx", split_axis=0, concat_axis=0, tiled=True
    )

    lower_rows = from_behind(object_field[:, :block_cells, :], "tx", -1)
    taller = jnp.concatenate([object_field, lower_rows], axis=1)
    right_cols = from_behind(taller[:, :, :block_cells], "ty", -1)
    extended = jnp.concatenate([taller, right_cols], axis=2)

    order = jnp.arange(positions_here, dtype=jnp.int32)
    earlier = order[None, :] < order[:, None]
    pair_rank = jnp.sum((owner_rows[:, None] == owner_rows[None, :]) & earlier, axis=1)
    slot_index = owner_rows * pair_slots + pair_rank.astype(jnp.int32)
    window_index = (
        (scan_blocks[:, 0] - lax.axis_index("tx") * (tile_rows // block_cells)) * spots
        + scan_blocks[:, 1] - lax.axis_index("ty") * spots
    )
    before = (window_index[None, :] < window_index[:, None]) | (
        (window_index[None, :] == window_index[:, None]) & earlier
    )
    place = jnp.sum(before, axis=1)
    slots = jnp.sum(
        jnp.where(place[None, :] == order[:, None], slot_index[None, :], 0), axis=1
    ).astype(jnp.int32)
    bounds = jnp.arange(windows + 1, dtype=jnp.int32)
    starts = jnp.sum(window_index[None, :] < bounds[:, None], axis=1).astype(jnp.int32)

    ahead, conjugate = complex_tables(window_cells)
    plane = (2, window_cells, window_cells)
    per_window = pl.BlockSpec((1, *plane), lambda number, *_: (number, 0, 0, 0))
    kept = jax.ShapeDtypeStruct((windows, *plane), jnp.bfloat16)
    flops = windows * 16 * window_cells**3
    far, phase = pl.pallas_call(
        functools.partial(forward_kernel, spots),
        grid=(windows,),
        out_shape=(kept, kept),
        in_specs=[whole(extended.shape), whole(plane), whole(ahead.shape), whole(ahead.shape)],
        out_specs=(per_window, per_window),
        cost_estimate=pl.CostEstimate(
            flops=flops, bytes_accessed=12 << 20, transcendentals=windows * window_cells**2
        ),
        name="forward",
    )(extended, probe_field, ahead, conjugate)

    gradient_sum, illumination = pl.pallas_call(
        functools.partial(backward_kernel, spots),
        out_shape=(
            jax.ShapeDtypeStruct((2, ext_rows, ext_cols), jnp.float32),
            jax.ShapeDtypeStruct((ext_rows, ext_cols), jnp.float32),
        ),
        grid_spec=pltpu.PrefetchScalarGridSpec(
            num_scalar_prefetch=2,
            grid=(windows,),
            in_specs=[
                per_window,
                per_window,
                pl.BlockSpec(
                    arrived.shape, lambda *_: (0, 0, 0), pipeline_mode=pl.Buffered(1)
                ),
                whole(plane),
                whole(ahead.shape),
                whole(ahead.shape),
            ],
            out_specs=(whole((2, ext_rows, ext_cols)), whole((ext_rows, ext_cols))),
            scratch_shapes=[pltpu.VMEM((window_cells, window_cells), jnp.float32)],
        ),
        cost_estimate=pl.CostEstimate(flops=flops, bytes_accessed=24 << 20, transcendentals=0),
        name="backward",
    )(slots, starts, far, phase, arrived, probe_field, ahead, conjugate)

    from_above = (
        from_behind(gradient_sum[:, tile_rows:, :].astype(jnp.bfloat16), "tx", 1).astype(
            jnp.float32
        ),
        from_behind(illumination[tile_rows:, :].astype(jnp.bfloat16), "tx", 1).astype(jnp.float32),
    )
    grad_top = gradient_sum[:, :tile_rows, :].at[:, :block_cells, :].add(from_above[0])
    light_top = illumination[:tile_rows, :].at[:block_cells, :].add(from_above[1])
    from_left = (
        from_behind(grad_top[:, :, tile_cols:].astype(jnp.bfloat16), "ty", 1).astype(jnp.float32),
        from_behind(light_top[:, tile_cols:].astype(jnp.bfloat16), "ty", 1).astype(jnp.float32),
    )
    grad_tile = grad_top[:, :, :tile_cols].at[:, :, :block_cells].add(from_left[0])
    light_tile = light_top[:, :tile_cols].at[:, :block_cells].add(from_left[1])
    updated = object_field - grad_tile / (light_tile + 1.0)
    for number in range(STEPS):
        padded = extended_2(updated, (("tx", 1), ("ty", 2)), 1)
        updated = smooth_pass(padded)
    return updated


def solution(mesh):
    in_specs = (
        P(None, "tx", "ty"),
        P(),
        P("tx", "ty", None),
        P(("tx", "ty"), None),
        P(("tx", "ty")),
    )
    out_specs = P(None, "tx", "ty")
    return jax.shard_map(local, mesh=mesh, in_specs=in_specs, out_specs=out_specs, check_vma=False)
```

```python
import functools

import jax
import jax.numpy as jnp
import numpy as np
from jax import lax
from jax.experimental import pallas as pl
from jax.experimental.pallas import tpu as pltpu
from jax.sharding import PartitionSpec as P

STEPS = 4


KAPPA_SQ = 1.0
TIME_STEP = 0.2
AMPLITUDE_FLOOR = 0.5


def from_behind(value, axis, steps):
    count = lax.axis_size(axis)
    initial, last = (max(0, -steps), min(count, count - steps))
    return lax.ppermute(value, axis, [(source, source + steps) for source in range(initial, last)])


def complex_tables(window_cells):
    counter = np.arange(window_cells)
    phases = counter[:, None] * counter[None, :] % window_cells
    angles = phases.astype(np.float32) * np.float32(2.0 * np.pi / window_cells)
    scaling = np.float32(1.0 / np.sqrt(window_cells))
    cosine, sine = (np.cos(angles) * scaling, np.sin(angles) * scaling)
    ahead = np.block([[cosine, sine], [-sine, cosine]])
    conjugate = np.block([[cosine, -sine], [sine, cosine]])
    return jnp.asarray(ahead, jnp.bfloat16), jnp.asarray(conjugate, jnp.bfloat16)


def matmul(first, second):
    return jnp.dot(first, second, preferred_element_type=jnp.float32)


def corner_of(number, spots, cells):
    start_row = pl.multiple_of(number // spots * cells, cells)
    start_col = pl.multiple_of(number % spots * cells, cells)
    return start_row, start_col


def forward_kernel(spots, extended, probe, ahead, conjugate, far_out, phase_out):
    cells = probe.shape[1]
    start_row, start_col = corner_of(pl.program_id(0), spots, cells // 2)
    view = (pl.ds(start_row, cells), pl.ds(start_col, cells))
    window_re, window_im = extended[(0, *view)], extended[(1, *view)]
    probe_re, probe_im = probe[0], probe[1]
    wave_re = (probe_re * window_re - probe_im * window_im).astype(jnp.bfloat16)
    wave_im = (probe_re * window_im + probe_im * window_re).astype(jnp.bfloat16)
    half = matmul(ahead[...], jnp.concatenate([wave_re, wave_im], axis=0)).astype(jnp.bfloat16)
    far = matmul(jnp.concatenate([half[:cells], half[cells:]], axis=1), conjugate[...])
    far_re, far_im = far[:, :cells], far[:, cells:]
    inverse = jnp.minimum(
        lax.rsqrt(far_re * far_re + far_im * far_im), 1.0 / AMPLITUDE_FLOOR
    )
    far_out[0, 0] = far_re.astype(jnp.bfloat16)
    far_out[0, 1] = far_im.astype(jnp.bfloat16)
    phase_out[0, 0] = (far_re * inverse).astype(jnp.bfloat16)
    phase_out[0, 1] = (far_im * inverse).astype(jnp.bfloat16)


def backward_kernel(
    spots, slots, starts, far, phase, arrived, probe, ahead, conjugate, grads, measured
):
    cells = probe.shape[1]
    number = pl.program_id(0)

    @pl.when(number == 0)
    def _():
        grads[...] = jnp.zeros_like(grads)

    first, last = starts[number], starts[number + 1]

    @pl.when(last > first)
    def _():
        measured[...] = arrived[slots[first]].astype(jnp.float32)

        def add_one(index, carry):
            measured[...] += arrived[slots[index]].astype(jnp.float32)
            return carry

        lax.fori_loop(first + 1, last, add_one, 0)
        count = (last - first).astype(jnp.float32)
        total = measured[...]
        residual = [
            (far[0, part].astype(jnp.float32) * count
             - phase[0, part].astype(jnp.float32) * total).astype(jnp.bfloat16)
            for part in range(2)
        ]
        back = matmul(conjugate[...], jnp.concatenate(residual, axis=0)).astype(jnp.bfloat16)
        near = matmul(jnp.concatenate([back[:cells], back[cells:]], axis=1), ahead[...])
        near_re, near_im = near[:, :cells], near[:, cells:]
        probe_re, probe_im = probe[0], probe[1]
        start_row, start_col = corner_of(number, spots, cells // 2)
        view = (pl.ds(start_row, cells), pl.ds(start_col, cells))
        grads[(0, *view)] += probe_re * near_re + probe_im * near_im
        grads[(1, *view)] += probe_re * near_im - probe_im * near_re


def whole(shape):
    return pl.BlockSpec(shape, lambda *_: (0,) * len(shape))


LANES = 128
RIM = 8
MESH = pl.DeviceIdType.MESH
ONWARD = ((1, 0), (0, 1), (1, 1))
AROUND = ((-1, 0), (1, 0), (0, -1), (0, 1), (-1, -1), (-1, 1), (1, -1), (1, 1))


def flux(difference):
    weight = 1.0 / (
        1.0 + (difference[0] * difference[0] + difference[1] * difference[1]) * (1.0 / KAPPA_SQ)
    )
    return weight[None] * difference


def finish_kernel(
    sizes, field, grads, probe, counts, out,
    sent_down, sent_right, sent_corner, got_down, got_right, got_corner, got_counts,
    inverse, column_rims, got_rows, got_columns, got_corners, first, second,
    send_sem, recv_sem, rim_send_sem, rim_recv_sem,
):
    n_tx, n_ty = sizes
    rows, cols = field.shape[1:]
    block = probe.shape[1] // 2
    spots = cols // block
    row, col = lax.axis_index("tx"), lax.axis_index("ty")

    def device(step):
        return (lax.rem(row + step[0] + n_tx, n_tx), lax.rem(col + step[1] + n_ty, n_ty))

    barrier = pltpu.get_barrier_semaphore()
    for step in AROUND:
        pl.semaphore_signal(barrier, inc=1, device_id=device(step), device_id_type=MESH)

    sent_down[...] = grads[:, rows:, :cols].astype(jnp.bfloat16)
    sent_right[...] = grads[:, :rows, cols:].astype(jnp.bfloat16)
    sent_corner[...] = grads[:, rows:, cols:].astype(jnp.bfloat16)
    pl.semaphore_wait(barrier, len(AROUND))

    def send(source, target, sems, number, step):
        return pltpu.make_async_remote_copy(
            src_ref=source,
            dst_ref=target,
            send_sem=sems[0].at[number],
            recv_sem=sems[1].at[number],
            device_id=device(step),
            device_id_type=MESH,
        )

    sums = (send_sem, recv_sem)
    sum_copies = [
        send(source, target, sums, number, ONWARD[number])
        for number, (source, target) in enumerate(
            ((sent_down, got_down), (sent_right, got_right), (sent_corner, got_corner))
        )
    ]
    count_copies = [
        send(counts, got_counts.at[number], sums, 3 + number, step)
        for number, step in enumerate(ONWARD)
    ]
    for copy in count_copies + sum_copies:
        copy.start()

    has_above, has_left = row > 0, col > 0
    has_below, has_right = row < n_tx - 1, col < n_ty - 1
    above, left = has_above.astype(jnp.float32), has_left.astype(jnp.float32)
    for copy in count_copies:
        copy.wait()

    def count_of(block_row, block_col):
        number = block_row % spots * spots + block_col % spots
        if block_row < 0 and block_col < 0:
            return got_counts[2, number : number + 1, :] * (above * left)
        if block_row < 0:
            return got_counts[0, number : number + 1, :] * above
        if block_col < 0:
            return got_counts[1, number : number + 1, :] * left
        return counts[number : number + 1, :]

    for block_row in range(rows // block):
        for block_col in range(spots):
            light = jnp.ones((block, block), jnp.float32)
            for down in range(2):
                for right in range(2):
                    part = (pl.ds(down * block, block), pl.ds(right * block, block))
                    power = probe[(0, *part)] ** 2 + probe[(1, *part)] ** 2
                    light += count_of(block_row - down, block_col - right) * power
            inverse[pl.ds(block_row * block, block), pl.ds(block_col * block, block)] = 1.0 / light

    for copy in sum_copies:
        copy.wait()
    for part in range(2):
        grads[part, :block, :cols] += got_down[part].astype(jnp.float32) * above
        grads[part, :rows, :block] += got_right[part].astype(jnp.float32) * left
        grads[part, :block, :block] += got_corner[part].astype(jnp.float32) * (above * left)
        updated = field[part] - grads[part, :rows, :cols] * inverse[...]
        first[part, pl.ds(2 * RIM, rows), pl.ds(0, cols)] = updated
        column_rims[0, part] = updated[:, :LANES].T[:RIM]
        column_rims[1, part] = updated[:, cols - LANES :].T[LANES - RIM :]

    rims = (rim_send_sem, rim_recv_sem)
    top, bottom = pl.ds(2 * RIM, RIM), pl.ds(2 * RIM + rows - RIM, RIM)
    west, east = pl.ds(0, LANES), pl.ds(cols - LANES, LANES)
    sources = (
        (first.at[:, top, pl.ds(0, cols)], got_rows.at[1]),
        (first.at[:, bottom, pl.ds(0, cols)], got_rows.at[0]),
        (column_rims.at[0], got_columns.at[1]),
        (column_rims.at[1], got_columns.at[0]),
        (first.at[:, top, west], got_corners.at[3]),
        (first.at[:, top, east], got_corners.at[2]),
        (first.at[:, bottom, west], got_corners.at[1]),
        (first.at[:, bottom, east], got_corners.at[0]),
    )
    rim_copies = [
        send(source, target, rims, number, AROUND[number])
        for number, (source, target) in enumerate(sources)
    ]
    for copy in rim_copies:
        copy.start()
    for copy in rim_copies:
        copy.wait()

    lanes = lax.broadcasted_iota(jnp.int32, (RIM, LANES), 1)
    on_right = lanes < jnp.where(has_right, RIM, 0)
    on_left = lanes >= jnp.where(has_left, LANES - RIM, LANES)
    zero = jnp.zeros((), jnp.float32)
    extra = pl.ds(cols, LANES)
    for part in range(2):
        for number, place, exists in ((0, RIM, has_above), (1, 2 * RIM + rows, has_below)):
            corner = jnp.where(
                on_left, got_corners[2 * number, part],
                jnp.where(on_right, got_corners[2 * number + 1, part], zero),
            )
            first[part, pl.ds(place, RIM), pl.ds(0, cols)] = jnp.where(
                exists, got_rows[number, part], zero
            )
            first[part, pl.ds(place, RIM), extra] = jnp.where(exists, corner, zero)
        sides = jnp.concatenate(
            [
                jnp.where(has_right, got_columns[1, part], zero),
                jnp.zeros((LANES - 2 * RIM, rows), jnp.float32),
                jnp.where(has_left, got_columns[0, part], zero),
            ],
            axis=0,
        )
        first[part, pl.ds(2 * RIM, rows), extra] = sides.T

    wide = cols + LANES
    every = lax.broadcasted_iota(jnp.int32, (RIM, wide), 1)
    lane_kept = (every < jnp.where(has_right, cols + RIM, cols)) | (
        every >= jnp.where(has_left, wide - RIM, wide)
    )
    sublane = lax.broadcasted_iota(jnp.int32, (2, RIM, wide), 1)
    chunks = rows // RIM + 2

    def smooth(source, store, start, stop):
        def chunk(number, earlier):
            place = pl.multiple_of((number + 1) * RIM, RIM)
            center = source[:, pl.ds(place, RIM), :]
            below = source[:, pl.ds(pl.multiple_of(place + RIM, RIM), RIM), :]
            lower = jnp.where(
                sublane == RIM - 1,
                pltpu.roll(below, RIM - 1, axis=1),
                pltpu.roll(center, RIM - 1, axis=1),
            )
            down = flux(lower - center)
            up = jnp.where(
                sublane == 0, pltpu.roll(earlier, 1, axis=1), pltpu.roll(down, 1, axis=1)
            )
            right = flux(pltpu.roll(center, wide - 1, axis=2) - center)
            left_flux = pltpu.roll(right, 1, axis=2)
            store(number, place, center + TIME_STEP * ((down - up) + (right - left_flux)))
            return down

        lax.fori_loop(start, stop, chunk, jnp.zeros((2, RIM, wide), jnp.float32))

    def keep(target):
        def store(number, place, value):
            exists = jnp.where(
                number == 0, has_above, jnp.where(number == chunks - 1, has_below, True)
            )
            kept = lane_kept & exists
            target[:, pl.ds(place, RIM), :] = jnp.where(kept[None], value, zero)

        return store

    def give(number, place, value):
        target = pl.multiple_of(place - 2 * RIM, RIM)
        @pl.when(number > 0)
        def _():
            out[:, pl.ds(target, RIM), :] = value[:, :, :cols]

    now, later = first, second
    for _ in range(STEPS - 1):
        smooth(now, keep(later), 0, chunks)
        now, later = later, now
    smooth(now, give, 0, chunks - 1)


def finish(object_field, gradient_sum, probe_field, counts):
    rows, cols = object_field.shape[1:]
    block = probe_field.shape[1] // 2
    sizes = (lax.axis_size("tx"), lax.axis_size("ty"))
    tall, wide = rows + 4 * RIM, cols + LANES
    strips = [(2, block, cols), (2, rows, block), (2, block, block)]
    vmem = pl.BlockSpec(memory_space=pltpu.VMEM)
    return pl.pallas_call(
        functools.partial(finish_kernel, sizes),
        out_shape=jax.ShapeDtypeStruct(object_field.shape, jnp.float32),
        in_specs=[vmem] * 4,
        out_specs=vmem,
        scratch_shapes=[
            *(pltpu.VMEM(strip, jnp.bfloat16) for strip in strips * 2),
            pltpu.VMEM((3, *counts.shape), jnp.float32),
            pltpu.VMEM((rows, cols), jnp.float32),
            pltpu.VMEM((2, 2, RIM, rows), jnp.float32),
            pltpu.VMEM((2, 2, RIM, cols), jnp.float32),
            pltpu.VMEM((2, 2, RIM, rows), jnp.float32),
            pltpu.VMEM((4, 2, RIM, LANES), jnp.float32),
            pltpu.VMEM((2, tall, wide), jnp.float32),
            pltpu.VMEM((2, tall, wide), jnp.float32),
            pltpu.SemaphoreType.DMA((6,)),
            pltpu.SemaphoreType.DMA((6,)),
            pltpu.SemaphoreType.DMA((8,)),
            pltpu.SemaphoreType.DMA((8,)),
        ],
        compiler_params=pltpu.CompilerParams(
            collective_id=0, has_side_effects=True, vmem_limit_bytes=48 << 20
        ),
        name="finish",
    )(object_field, gradient_sum, probe_field, counts)


def local(object_field, probe_field, amplitudes, scan_blocks, owner_rows):
    tile_rows, tile_cols = object_field.shape[1:]
    window_cells = probe_field.shape[1]
    block_cells = window_cells // 2
    positions_here = owner_rows.shape[0]
    pair_slots = amplitudes.shape[0] // lax.axis_size("tx")
    spots = tile_cols // block_cells
    windows = tile_rows // block_cells * spots
    ext_rows, ext_cols = tile_rows + block_cells, tile_cols + block_cells

    lower_rows = from_behind(object_field[:, :block_cells, :], "tx", -1)
    taller = jnp.concatenate([object_field, lower_rows], axis=1)
    right_cols = from_behind(taller[:, :, :block_cells], "ty", -1)
    extended = jnp.concatenate([taller, right_cols], axis=2)
    outgoing, extended = lax.optimization_barrier((amplitudes.astype(jnp.bfloat16), extended))
    arrived = lax.all_to_all(outgoing, "tx", split_axis=0, concat_axis=0, tiled=True)

    order = jnp.arange(positions_here, dtype=jnp.int32)
    earlier = order[None, :] < order[:, None]
    pair_rank = jnp.sum((owner_rows[:, None] == owner_rows[None, :]) & earlier, axis=1)
    slot_index = owner_rows * pair_slots + pair_rank.astype(jnp.int32)
    window_index = (
        (scan_blocks[:, 0] - lax.axis_index("tx") * (tile_rows // block_cells)) * spots
        + scan_blocks[:, 1] - lax.axis_index("ty") * spots
    )
    before = (window_index[None, :] < window_index[:, None]) | (
        (window_index[None, :] == window_index[:, None]) & earlier
    )
    place = jnp.sum(before, axis=1)
    slots = jnp.sum(
        jnp.where(place[None, :] == order[:, None], slot_index[None, :], 0), axis=1
    ).astype(jnp.int32)
    bounds = jnp.arange(windows + 1, dtype=jnp.int32)
    starts = jnp.sum(window_index[None, :] < bounds[:, None], axis=1).astype(jnp.int32)

    ahead, conjugate = complex_tables(window_cells)
    plane = (2, window_cells, window_cells)
    per_window = pl.BlockSpec((1, *plane), lambda number, *_: (number, 0, 0, 0))
    kept = jax.ShapeDtypeStruct((windows, *plane), jnp.bfloat16)
    flops = windows * 16 * window_cells**3
    far, phase = pl.pallas_call(
        functools.partial(forward_kernel, spots),
        grid=(windows,),
        out_shape=(kept, kept),
        in_specs=[whole(extended.shape), whole(plane), whole(ahead.shape), whole(ahead.shape)],
        out_specs=(per_window, per_window),
        cost_estimate=pl.CostEstimate(
            flops=flops, bytes_accessed=12 << 20, transcendentals=windows * window_cells**2
        ),
        name="forward",
    )(extended, probe_field, ahead, conjugate)

    gradient_sum = pl.pallas_call(
        functools.partial(backward_kernel, spots),
        out_shape=jax.ShapeDtypeStruct((2, ext_rows, ext_cols), jnp.float32),
        grid_spec=pltpu.PrefetchScalarGridSpec(
            num_scalar_prefetch=2,
            grid=(windows,),
            in_specs=[
                per_window,
                per_window,
                pl.BlockSpec(
                    arrived.shape, lambda *_: (0, 0, 0), pipeline_mode=pl.Buffered(1)
                ),
                whole(plane),
                whole(ahead.shape),
                whole(ahead.shape),
            ],
            out_specs=whole((2, ext_rows, ext_cols)),
            scratch_shapes=[pltpu.VMEM((window_cells, window_cells), jnp.float32)],
        ),
        cost_estimate=pl.CostEstimate(flops=flops, bytes_accessed=24 << 20, transcendentals=0),
        name="backward",
    )(slots, starts, far, phase, arrived, probe_field, ahead, conjugate)

    counts = (starts[1:] - starts[:-1]).astype(jnp.float32)
    counts = jnp.broadcast_to(counts[:, None], (windows, LANES))
    return finish(object_field, gradient_sum, probe_field, counts)


def solution(mesh):
    in_specs = (
        P(None, "tx", "ty"),
        P(),
        P("tx", "ty", None),
        P(("tx", "ty"), None),
        P(("tx", "ty")),
    )
    out_specs = P(None, "tx", "ty")
    return jax.shard_map(local, mesh=mesh, in_specs=in_specs, out_specs=out_specs, check_vma=False)
```

```python
import functools

import jax
import jax.numpy as jnp
import numpy as np
from jax import lax
from jax.experimental import pallas as pl
from jax.experimental.pallas import tpu as pltpu
from jax.sharding import PartitionSpec as P

STEPS = 4


KAPPA_SQ = 1.0
TIME_STEP = 0.2
AMPLITUDE_FLOOR = 0.5


def complex_tables(window_cells):
    counter = np.arange(window_cells)
    phases = counter[:, None] * counter[None, :] % window_cells
    angles = phases.astype(np.float32) * np.float32(2.0 * np.pi / window_cells)
    scaling = np.float32(1.0 / np.sqrt(window_cells))
    cosine, sine = (np.cos(angles) * scaling, np.sin(angles) * scaling)
    ahead = np.block([[cosine, sine], [-sine, cosine]])
    conjugate = np.block([[cosine, -sine], [sine, cosine]])
    return jnp.asarray(ahead, jnp.bfloat16), jnp.asarray(conjugate, jnp.bfloat16)


def matmul(first, second):
    return jnp.dot(first, second, preferred_element_type=jnp.float32)


LANES = 128
RIM = 8
MESH = pl.DeviceIdType.MESH
ONWARD = ((1, 0), (0, 1), (1, 1))
AROUND = ((-1, 0), (1, 0), (0, -1), (0, 1), (-1, -1), (-1, 1), (1, -1), (1, 1))


def flux(difference):
    weight = 1.0 / (
        1.0 + (difference[0] * difference[0] + difference[1] * difference[1]) * (1.0 / KAPPA_SQ)
    )
    return weight[None] * difference


def finish_kernel(
    sizes, field, grads, probe, counts, out,
    sent_down, sent_right, sent_corner, got_down, got_right, got_corner, got_counts,
    inverse, column_rims, got_rows, got_columns, got_corners, first, second,
    send_sem, recv_sem, rim_send_sem, rim_recv_sem,
):
    n_tx, n_ty = sizes
    rows, cols = field.shape[1:]
    block = probe.shape[1] // 2
    spots = cols // block
    row, col = lax.axis_index("tx"), lax.axis_index("ty")

    def device(step):
        return (lax.rem(row + step[0] + n_tx, n_tx), lax.rem(col + step[1] + n_ty, n_ty))

    barrier = pltpu.get_barrier_semaphore()
    for step in AROUND:
        pl.semaphore_signal(barrier, inc=1, device_id=device(step), device_id_type=MESH)

    sent_down[...] = grads[:, rows:, :cols].astype(jnp.bfloat16)
    sent_right[...] = grads[:, :rows, cols:].astype(jnp.bfloat16)
    sent_corner[...] = grads[:, rows:, cols:].astype(jnp.bfloat16)
    pl.semaphore_wait(barrier, len(AROUND))

    def send(source, target, sems, number, step):
        return pltpu.make_async_remote_copy(
            src_ref=source,
            dst_ref=target,
            send_sem=sems[0].at[number],
            recv_sem=sems[1].at[number],
            device_id=device(step),
            device_id_type=MESH,
        )

    sums = (send_sem, recv_sem)
    sum_copies = [
        send(source, target, sums, number, ONWARD[number])
        for number, (source, target) in enumerate(
            ((sent_down, got_down), (sent_right, got_right), (sent_corner, got_corner))
        )
    ]
    count_copies = [
        send(counts, got_counts.at[number], sums, 3 + number, step)
        for number, step in enumerate(ONWARD)
    ]
    for copy in count_copies + sum_copies:
        copy.start()

    has_above, has_left = row > 0, col > 0
    has_below, has_right = row < n_tx - 1, col < n_ty - 1
    above, left = has_above.astype(jnp.float32), has_left.astype(jnp.float32)
    for copy in count_copies:
        copy.wait()

    def count_of(block_row, block_col):
        number = block_row % spots * spots + block_col % spots
        if block_row < 0 and block_col < 0:
            return got_counts[2, number : number + 1, :] * (above * left)
        if block_row < 0:
            return got_counts[0, number : number + 1, :] * above
        if block_col < 0:
            return got_counts[1, number : number + 1, :] * left
        return counts[number : number + 1, :]

    for block_row in range(rows // block):
        for block_col in range(spots):
            light = jnp.ones((block, block), jnp.float32)
            for down in range(2):
                for right in range(2):
                    part = (pl.ds(down * block, block), pl.ds(right * block, block))
                    power = probe[(0, *part)] ** 2 + probe[(1, *part)] ** 2
                    light += count_of(block_row - down, block_col - right) * power
            inverse[pl.ds(block_row * block, block), pl.ds(block_col * block, block)] = 1.0 / light

    for copy in sum_copies:
        copy.wait()
    for part in range(2):
        grads[part, :block, :cols] += got_down[part].astype(jnp.float32) * above
        grads[part, :rows, :block] += got_right[part].astype(jnp.float32) * left
        grads[part, :block, :block] += got_corner[part].astype(jnp.float32) * (above * left)
        updated = field[part] - grads[part, :rows, :cols] * inverse[...]
        first[part, pl.ds(2 * RIM, rows), pl.ds(0, cols)] = updated
        column_rims[0, part] = updated[:, :LANES].T[:RIM]
        column_rims[1, part] = updated[:, cols - LANES :].T[LANES - RIM :]

    rims = (rim_send_sem, rim_recv_sem)
    top, bottom = pl.ds(2 * RIM, RIM), pl.ds(2 * RIM + rows - RIM, RIM)
    west, east = pl.ds(0, LANES), pl.ds(cols - LANES, LANES)
    sources = (
        (first.at[:, top, pl.ds(0, cols)], got_rows.at[1]),
        (first.at[:, bottom, pl.ds(0, cols)], got_rows.at[0]),
        (column_rims.at[0], got_columns.at[1]),
        (column_rims.at[1], got_columns.at[0]),
        (first.at[:, top, west], got_corners.at[3]),
        (first.at[:, top, east], got_corners.at[2]),
        (first.at[:, bottom, west], got_corners.at[1]),
        (first.at[:, bottom, east], got_corners.at[0]),
    )
    rim_copies = [
        send(source, target, rims, number, AROUND[number])
        for number, (source, target) in enumerate(sources)
    ]
    for copy in rim_copies:
        copy.start()
    for copy in rim_copies:
        copy.wait()

    lanes = lax.broadcasted_iota(jnp.int32, (RIM, LANES), 1)
    on_right = lanes < jnp.where(has_right, RIM, 0)
    on_left = lanes >= jnp.where(has_left, LANES - RIM, LANES)
    zero = jnp.zeros((), jnp.float32)
    extra = pl.ds(cols, LANES)
    for part in range(2):
        for number, place, exists in ((0, RIM, has_above), (1, 2 * RIM + rows, has_below)):
            corner = jnp.where(
                on_left, got_corners[2 * number, part],
                jnp.where(on_right, got_corners[2 * number + 1, part], zero),
            )
            first[part, pl.ds(place, RIM), pl.ds(0, cols)] = jnp.where(
                exists, got_rows[number, part], zero
            )
            first[part, pl.ds(place, RIM), extra] = jnp.where(exists, corner, zero)
        sides = jnp.concatenate(
            [
                jnp.where(has_right, got_columns[1, part], zero),
                jnp.zeros((LANES - 2 * RIM, rows), jnp.float32),
                jnp.where(has_left, got_columns[0, part], zero),
            ],
            axis=0,
        )
        first[part, pl.ds(2 * RIM, rows), extra] = sides.T

    wide = cols + LANES
    every = lax.broadcasted_iota(jnp.int32, (RIM, wide), 1)
    lane_kept = (every < jnp.where(has_right, cols + RIM, cols)) | (
        every >= jnp.where(has_left, wide - RIM, wide)
    )
    sublane = lax.broadcasted_iota(jnp.int32, (2, RIM, wide), 1)
    chunks = rows // RIM + 2

    def smooth(source, store, start, stop):
        def chunk(number, earlier):
            place = pl.multiple_of((number + 1) * RIM, RIM)
            center = source[:, pl.ds(place, RIM), :]
            below = source[:, pl.ds(pl.multiple_of(place + RIM, RIM), RIM), :]
            lower = jnp.where(
                sublane == RIM - 1,
                pltpu.roll(below, RIM - 1, axis=1),
                pltpu.roll(center, RIM - 1, axis=1),
            )
            down = flux(lower - center)
            up = jnp.where(
                sublane == 0, pltpu.roll(earlier, 1, axis=1), pltpu.roll(down, 1, axis=1)
            )
            right = flux(pltpu.roll(center, wide - 1, axis=2) - center)
            left_flux = pltpu.roll(right, 1, axis=2)
            store(number, place, center + TIME_STEP * ((down - up) + (right - left_flux)))
            return down

        lax.fori_loop(start, stop, chunk, jnp.zeros((2, RIM, wide), jnp.float32))

    def keep(target):
        def store(number, place, value):
            exists = jnp.where(
                number == 0, has_above, jnp.where(number == chunks - 1, has_below, True)
            )
            kept = lane_kept & exists
            target[:, pl.ds(place, RIM), :] = jnp.where(kept[None], value, zero)

        return store

    def give(number, place, value):
        target = pl.multiple_of(place - 2 * RIM, RIM)
        @pl.when(number > 0)
        def _():
            out[:, pl.ds(target, RIM), :] = value[:, :, :cols]

    now, later = first, second
    for _ in range(STEPS - 1):
        smooth(now, keep(later), 0, chunks)
        now, later = later, now
    smooth(now, give, 0, chunks - 1)


def finish(object_field, gradient_sum, probe_field, counts):
    rows, cols = object_field.shape[1:]
    block = probe_field.shape[1] // 2
    sizes = (lax.axis_size("tx"), lax.axis_size("ty"))
    tall, wide = rows + 4 * RIM, cols + LANES
    strips = [(2, block, cols), (2, rows, block), (2, block, block)]
    vmem = pl.BlockSpec(memory_space=pltpu.VMEM)
    return pl.pallas_call(
        functools.partial(finish_kernel, sizes),
        out_shape=jax.ShapeDtypeStruct(object_field.shape, jnp.float32),
        in_specs=[vmem] * 4,
        out_specs=vmem,
        scratch_shapes=[
            *(pltpu.VMEM(strip, jnp.bfloat16) for strip in strips * 2),
            pltpu.VMEM((3, *counts.shape), jnp.float32),
            pltpu.VMEM((rows, cols), jnp.float32),
            pltpu.VMEM((2, 2, RIM, rows), jnp.float32),
            pltpu.VMEM((2, 2, RIM, cols), jnp.float32),
            pltpu.VMEM((2, 2, RIM, rows), jnp.float32),
            pltpu.VMEM((4, 2, RIM, LANES), jnp.float32),
            pltpu.VMEM((2, tall, wide), jnp.float32),
            pltpu.VMEM((2, tall, wide), jnp.float32),
            pltpu.SemaphoreType.DMA((6,)),
            pltpu.SemaphoreType.DMA((6,)),
            pltpu.SemaphoreType.DMA((8,)),
            pltpu.SemaphoreType.DMA((8,)),
        ],
        compiler_params=pltpu.CompilerParams(
            collective_id=0, has_side_effects=True, vmem_limit_bytes=48 << 20
        ),
        name="finish",
    )(object_field, gradient_sum, probe_field, counts)


SIDE = 4
STAGES = 4
TAKEN = tuple(
    sorted(
        ((dx, dy) for dx in range(SIDE) for dy in range(SIDE)),
        key=lambda step: (step == (0, 0), 2 not in step, 0 in step),
    )
)
NEARBY = ((1, 0), (-1, 0), (0, 1), (0, -1), (1, 1), (-1, -1))


def gather_kernel(
    sizes, slots, same, ends, counts, field, amplitudes, probe, ahead, conjugate, grads,
    extended, sent_rows, got_rows, staged, sent, arrived, held, passed, passed_again,
    far, phase, sums, stage_sem, field_sem, own_sem, halo_send, halo_recv, send_sem, recv_sem,
):
    n_tx, n_ty = sizes
    cells = probe.shape[1]
    block = cells // 2
    rows, cols = extended.shape[1] - block, extended.shape[2] - block
    spots = cols // block
    windows = rows // block * spots
    row, col = lax.axis_index("tx"), lax.axis_index("ty")
    place = (row // SIDE, lax.rem(row, SIDE))

    def around(step):
        return (lax.rem(row + step[0] + n_tx, n_tx), lax.rem(col + step[1] + n_ty, n_ty))

    def owner_at(half, first, second):
        first, second = lax.rem(first + SIDE, SIDE), lax.rem(second + SIDE, SIDE)
        return first * SIDE + second if half == 0 else second * SIDE + first

    def load(number):
        dx, dy = TAKEN[number]
        home = owner_at(0, place[0] + dx, place[1] + dy)
        slot = number % STAGES
        return pltpu.make_async_copy(
            amplitudes.at[home], staged.at[slot], stage_sem.at[slot]
        )

    take_field = pltpu.make_async_copy(
        field, extended.at[:, pl.ds(0, rows), pl.ds(0, cols)], field_sem
    )
    take_field.start()
    for number in range(STAGES):
        load(number).start()

    barrier = pltpu.get_barrier_semaphore()
    partners = [around(step) for step in NEARBY] + [
        (owner_at(half, place[half] + step, place[1 - half]), col)
        for half in range(2)
        for step in (1, -1)
    ]
    for partner in partners:
        pl.semaphore_signal(barrier, inc=1, device_id=partner, device_id_type=MESH)

    def remote(source, target, sems, partner):
        return pltpu.make_async_remote_copy(
            src_ref=source,
            dst_ref=target,
            send_sem=sems[0],
            recv_sem=sems[1],
            device_id=partner,
            device_id_type=MESH,
        )

    def piece(half, kind, first, second):
        a, b = place[half], place[1 - half]
        lines = pl.ds(half * block, block)
        ring = 0 if kind < 4 else 1
        number = kind * SIDE + (second if ring == 0 else first)
        sems = (send_sem.at[half, number], recv_sem.at[half, number])
        if ring == 0:
            step = 1 if kind == 0 or (kind > 1 and second < 2) else -1
            partner = owner_at(half, a + step, b)
            if kind == 3:
                source, owner = passed.at[half, second], owner_at(half, a - step, b)
            else:
                offset = (1, -1, 2)[kind]
                source = sent.at[owner_at(half, a + offset, b + second), :, lines]
                owner = row
            if kind == 2:
                target = passed.at[half, second]
            elif second == 0:
                target = arrived.at[owner, :, lines]
            else:
                target = held.at[half, (0, 2, 2, 1)[kind], second - 1]
        else:
            step = 1 if kind == 4 or (kind > 5 and first < 2) else -1
            partner = owner_at(half, a, b + step)
            offset = (1, 3, 2)[kind - 4] if kind < 7 else 0
            if kind == 7:
                source = passed_again.at[half, first]
                owner = owner_at(half, a - first, b - step)
            else:
                source = (
                    sent.at[owner_at(half, a, b + offset), :, lines]
                    if first == 0
                    else held.at[half, first - 1, offset - 1]
                )
                owner = owner_at(half, a - first, b)
            target = (
                passed_again.at[half, first] if kind == 6 else arrived.at[owner, :, lines]
            )
        return remote(source, target, sems, (partner, col))

    take_field.wait()
    sent_rows[...] = extended[:, :block, :cols].astype(jnp.bfloat16)
    pl.semaphore_wait(barrier, len(partners))

    corner = (pl.ds(rows, block), pl.ds(cols, block))
    halos = [
        remote(sent_rows, got_rows, (halo_send.at[0], halo_recv.at[0]), around((-1, 0))),
        remote(
            extended.at[:, pl.ds(0, rows), pl.ds(0, block)],
            extended.at[:, pl.ds(0, rows), pl.ds(cols, block)],
            (halo_send.at[1], halo_recv.at[1]), around((0, -1)),
        ),
        remote(
            extended.at[:, pl.ds(0, block), pl.ds(0, block)],
            extended.at[(slice(None), *corner)],
            (halo_send.at[2], halo_recv.at[2]), around((-1, -1)),
        ),
    ]

    for number, (dx, dy) in enumerate(TAKEN):
        slot = number % STAGES
        home = owner_at(0, place[0] + dx, place[1] + dy)
        load(number).wait()

        def cast(index, carry):
            sent[home, index] = staged[slot, index].astype(jnp.bfloat16)
            return carry

        lax.fori_loop(0, sent.shape[1], cast, 0)
        if number + STAGES < len(TAKEN):
            load(number + STAGES).start()
        for half, (first, second) in enumerate(((dx, dy), (dy, dx))):
            if first:
                piece(half, (0, 2, 1)[first - 1], None, second).start()
        if number == 6:
            for copy in halos:
                copy.start()

    own = pltpu.make_async_copy(sent.at[row], arrived.at[row], own_sem)
    own.start()

    def forward(number):
        start_row = pl.multiple_of(number // spots * block, block)
        start_col = pl.multiple_of(lax.rem(number, spots) * block, block)
        view = (pl.ds(start_row, cells), pl.ds(start_col, cells))
        window_re, window_im = extended[(0, *view)], extended[(1, *view)]
        probe_re, probe_im = probe[0], probe[1]
        wave_re = (probe_re * window_re - probe_im * window_im).astype(jnp.bfloat16)
        wave_im = (probe_re * window_im + probe_im * window_re).astype(jnp.bfloat16)
        half = matmul(ahead[...], jnp.concatenate([wave_re, wave_im], axis=0)).astype(
            jnp.bfloat16
        )
        waves = matmul(jnp.concatenate([half[:cells], half[cells:]], axis=1), conjugate[...])
        far_re, far_im = waves[:, :cells], waves[:, cells:]
        inverse = jnp.minimum(
            lax.rsqrt(far_re * far_re + far_im * far_im), 1.0 / AMPLITUDE_FLOOR
        )
        far[number, 0] = far_re.astype(jnp.bfloat16)
        far[number, 1] = far_im.astype(jnp.bfloat16)
        phase[number, 0] = (far_re * inverse).astype(jnp.bfloat16)
        phase[number, 1] = (far_im * inverse).astype(jnp.bfloat16)

    def relay_first():
        for second in range(SIDE):
            for half in range(2):
                piece(half, 2, None, second).wait_recv()
                piece(half, 3, None, second).start()
        for kind in (6, 4, 5):
            for half in range(2):
                piece(half, kind, 0, None).start()

    def turn(first, second):
        arrival = (0, 3, 1)[first - 1]
        kind = {1: 4, 2: 6, 3: 5}[second]
        for half in range(2):
            piece(half, arrival, None, second).wait_recv()
            piece(half, kind, first, None).start()

    def relay_second(first):
        for half in range(2):
            piece(half, 6, first, None).wait_recv()
            piece(half, 7, first, None).start()

    def take_halos():
        for copy in halos:
            copy.wait()

        for part in range(2):
            extended[part, pl.ds(rows, block), pl.ds(0, cols)] = jnp.where(
                row < n_tx - 1, got_rows[part].astype(jnp.float32), 0.0
            )

        @pl.when(col == n_ty - 1)
        def _():
            extended[:, :, pl.ds(cols, block)] = jnp.zeros_like(extended[:, :, cols:])

        @pl.when(row == n_tx - 1)
        def _():
            extended[(slice(None), *corner)] = jnp.zeros((2, block, block), jnp.float32)

    inner = spots - 1
    steps = {
        3: [relay_first],
        5: [functools.partial(turn, 1, 2)],
        7: [functools.partial(turn, 3, 2), take_halos],
        9: [functools.partial(turn, 1, 1)],
        11: [functools.partial(turn, 3, 1)],
        13: [functools.partial(turn, 1, 3)],
        14: [functools.partial(turn, 3, 3)],
    }

    def forward_step(index, carry):
        edge = index - inner * inner
        inside = index < inner * inner
        at_row = jnp.where(inside, index // inner, jnp.where(edge < spots, inner, edge - spots))
        at_col = jnp.where(inside, lax.rem(index, inner), jnp.where(edge < spots, edge, inner))
        forward(at_row * spots + at_col)
        for when, work in steps.items():

            @pl.when(index == when)
            def _(work=work):
                for one in work:
                    one()

        return carry

    lax.fori_loop(0, windows, forward_step, 0)
    for second in (2, 1, 3):
        turn(2, second)
    grads[...] = jnp.zeros_like(grads)
    for first in (0, 1, 3, 2):
        relay_second(first)

    own.wait()
    for half in range(2):
        for kind in (0, 1, 3):
            piece(half, kind, None, 0).wait_recv()
        for kind in (4, 5, 7):
            for first in range(SIDE):
                piece(half, kind, first, None).wait_recv()

    def add_up(index, carry):
        slot = slots[index]
        plane = arrived[slot // arrived.shape[1], lax.rem(slot, arrived.shape[1])]
        before = jnp.where(same[index] > 0, sums[jnp.maximum(index - 1, 0)], 0.0)
        sums[index] = before + plane.astype(jnp.float32)
        return carry

    lax.fori_loop(0, sums.shape[0], add_up, 0)

    def backward(number, carry):
        count = counts[number]
        total = sums[ends[number]] * jnp.minimum(count, 1.0)
        residual = [
            (
                far[number, part].astype(jnp.float32) * count
                - phase[number, part].astype(jnp.float32) * total
            ).astype(jnp.bfloat16)
            for part in range(2)
        ]
        back = matmul(conjugate[...], jnp.concatenate(residual, axis=0)).astype(jnp.bfloat16)
        near = matmul(jnp.concatenate([back[:cells], back[cells:]], axis=1), ahead[...])
        near_re, near_im = near[:, :cells], near[:, cells:]
        probe_re, probe_im = probe[0], probe[1]
        start_row = pl.multiple_of(number // spots * block, block)
        start_col = pl.multiple_of(lax.rem(number, spots) * block, block)
        view = (pl.ds(start_row, cells), pl.ds(start_col, cells))
        grads[(0, *view)] += probe_re * near_re + probe_im * near_im
        grads[(1, *view)] += probe_re * near_im - probe_im * near_re
        return carry

    lax.fori_loop(0, windows, backward, 0)
    for half in range(2):
        for kind in range(4):
            for second in range(SIDE):
                piece(half, kind, None, second).wait_send()
        for kind in range(4, 8):
            for first in range(SIDE):
                piece(half, kind, first, None).wait_send()


def gather(object_field, probe_field, amplitudes, tables, scalars):
    rows, cols = object_field.shape[1:]
    cells = probe_field.shape[1]
    block = cells // 2
    windows = rows // block * (cols // block)
    groups = lax.axis_size("tx")
    slots = amplitudes.shape[0] // groups
    sizes = (groups, lax.axis_size("ty"))
    assert groups == SIDE * SIDE
    vmem = pl.BlockSpec(memory_space=pltpu.VMEM)
    smem = pl.BlockSpec(memory_space=pltpu.SMEM)
    anywhere = pl.BlockSpec(memory_space=pl.ANY)
    narrow, wide = jnp.bfloat16, jnp.float32
    own = (groups, slots, cells, cells)
    part = (slots, block, cells)
    return pl.pallas_call(
        functools.partial(gather_kernel, sizes),
        out_shape=jax.ShapeDtypeStruct((2, rows + block, cols + block), wide),
        in_specs=[smem] * 4 + [anywhere] * 2 + [vmem] * 3,
        out_specs=vmem,
        scratch_shapes=[
            pltpu.VMEM((2, rows + block, cols + block), wide),
            pltpu.VMEM((2, block, cols), narrow),
            pltpu.VMEM((2, block, cols), narrow),
            pltpu.VMEM((STAGES, slots, cells, cells), wide),
            pltpu.VMEM(own, narrow),
            pltpu.VMEM(own, narrow),
            pltpu.VMEM((2, SIDE - 1, SIDE - 1, *part), narrow),
            pltpu.VMEM((2, SIDE, *part), narrow),
            pltpu.VMEM((2, SIDE, *part), narrow),
            pltpu.VMEM((windows, 2, cells, cells), narrow),
            pltpu.VMEM((windows, 2, cells, cells), narrow),
            pltpu.VMEM((scalars[0].shape[0], cells, cells), wide),
            pltpu.SemaphoreType.DMA((STAGES,)),
            pltpu.SemaphoreType.DMA,
            pltpu.SemaphoreType.DMA,
            pltpu.SemaphoreType.DMA((3,)),
            pltpu.SemaphoreType.DMA((3,)),
            pltpu.SemaphoreType.DMA((2, 8 * SIDE)),
            pltpu.SemaphoreType.DMA((2, 8 * SIDE)),
        ],
        compiler_params=pltpu.CompilerParams(
            collective_id=1, has_side_effects=True, vmem_limit_bytes=60 << 20
        ),
        name="gather",
    )(
        *scalars, object_field, amplitudes.reshape(own), probe_field, *tables
    )


def local(object_field, probe_field, amplitudes, scan_blocks, owner_rows):
    tile_rows, tile_cols = object_field.shape[1:]
    window_cells = probe_field.shape[1]
    block_cells = window_cells // 2
    positions_here = owner_rows.shape[0]
    pair_slots = amplitudes.shape[0] // lax.axis_size("tx")
    spots = tile_cols // block_cells
    windows = tile_rows // block_cells * spots

    order = jnp.arange(positions_here, dtype=jnp.int32)
    earlier = order[None, :] < order[:, None]
    pair_rank = jnp.sum((owner_rows[:, None] == owner_rows[None, :]) & earlier, axis=1)
    slot_index = owner_rows * pair_slots + pair_rank.astype(jnp.int32)
    window_index = (
        (scan_blocks[:, 0] - lax.axis_index("tx") * (tile_rows // block_cells)) * spots
        + scan_blocks[:, 1] - lax.axis_index("ty") * spots
    )
    before = (window_index[None, :] < window_index[:, None]) | (
        (window_index[None, :] == window_index[:, None]) & earlier
    )
    place = jnp.sum(before, axis=1)
    slots = jnp.sum(
        jnp.where(place[None, :] == order[:, None], slot_index[None, :], 0), axis=1
    ).astype(jnp.int32)
    bounds = jnp.arange(windows, dtype=jnp.int32)
    counts = jnp.sum(window_index[None, :] == bounds[:, None], axis=1).astype(jnp.float32)
    ends = jnp.sum(window_index[None, :] <= bounds[:, None], axis=1).astype(jnp.int32)
    follows = (window_index[None, :] == window_index[:, None]) & earlier
    same = jnp.sum(
        jnp.where(place[None, :] == order[:, None], jnp.any(follows, axis=1)[None, :], False),
        axis=1,
    ).astype(jnp.int32)
    scalars = (slots, same, jnp.maximum(ends - 1, 0), counts)
    gradient_sum = gather(
        object_field, probe_field, amplitudes, complex_tables(window_cells), scalars
    )
    counts = jnp.broadcast_to(counts[:, None], (windows, LANES))
    return finish(object_field, gradient_sum, probe_field, counts)


def solution(mesh):
    in_specs = (
        P(None, "tx", "ty"),
        P(),
        P("tx", "ty", None),
        P(("tx", "ty"), None),
        P(("tx", "ty")),
    )
    out_specs = P(None, "tx", "ty")
    return jax.shard_map(local, mesh=mesh, in_specs=in_specs, out_specs=out_specs, check_vma=False)
```

```python
import functools

import jax
import jax.numpy as jnp
import numpy as np
from jax import lax
from jax.experimental import pallas as pl
from jax.experimental.pallas import tpu as pltpu
from jax.sharding import PartitionSpec as P

STEPS = 4


KAPPA_SQ = 1.0
TIME_STEP = 0.2
AMPLITUDE_FLOOR = 0.5


def complex_tables(window_cells):
    counter = np.arange(window_cells)
    phases = counter[:, None] * counter[None, :] % window_cells
    angles = phases.astype(np.float32) * np.float32(2.0 * np.pi / window_cells)
    scaling = np.float32(1.0 / np.sqrt(window_cells))
    cosine, sine = (np.cos(angles) * scaling, np.sin(angles) * scaling)
    ahead = np.block([[cosine, sine], [-sine, cosine]])
    conjugate = np.block([[cosine, -sine], [sine, cosine]])
    return jnp.asarray(ahead, jnp.bfloat16), jnp.asarray(conjugate, jnp.bfloat16)


def matmul(first, second):
    return jnp.dot(first, second, preferred_element_type=jnp.float32)


LANES = 128
RIM = 8
UNROLL = 6
MESH = pl.DeviceIdType.MESH
ONWARD = ((1, 0), (0, 1), (1, 1))
AROUND = ((-1, 0), (1, 0), (0, -1), (0, 1), (-1, -1), (-1, 1), (1, -1), (1, 1))


def flux(real, imag):
    weight = 1.0 / (1.0 + (real * real + imag * imag) * (1.0 / KAPPA_SQ))
    return weight * real, weight * imag


SIDE = 4
STAGES = 4
TAKEN = tuple(
    sorted(
        ((dx, dy) for dx in range(SIDE) for dy in range(SIDE)),
        key=lambda step: (step == (0, 0), 2 not in step, 0 in step),
    )
)


def step_kernel(
    sizes, slots, same, ends, counts, field, amplitudes, probe, ahead, conjugate, wide_counts, out,
    extended, sent_rows, got_rows, staged, sent, arrived, held, passed, passed_again,
    far, phase, sums, grads, inverse, got_counts,
    sent_down, sent_right, sent_corner, got_down, got_right, got_corner,
    column_rims, got_tops, got_columns, got_corners, first_field, second_field,
    stage_sem, field_sem, own_sem, halo_send, halo_recv, send_sem, recv_sem,
    sum_send, sum_recv, rim_send, rim_recv,
):
    n_tx, n_ty = sizes
    cells = probe.shape[1]
    block = cells // 2
    rows, cols = extended.shape[1] - block, extended.shape[2] - block
    spots = cols // block
    windows = rows // block * spots
    row, col = lax.axis_index("tx"), lax.axis_index("ty")
    place = (row // SIDE, lax.rem(row, SIDE))

    def around(step):
        return (lax.rem(row + step[0] + n_tx, n_tx), lax.rem(col + step[1] + n_ty, n_ty))

    def owner_at(half, first, second):
        first, second = lax.rem(first + SIDE, SIDE), lax.rem(second + SIDE, SIDE)
        return first * SIDE + second if half == 0 else second * SIDE + first

    def load(number):
        dx, dy = TAKEN[number]
        home = owner_at(0, place[0] + dx, place[1] + dy)
        slot = number % STAGES
        return pltpu.make_async_copy(
            amplitudes.at[home], staged.at[slot], stage_sem.at[slot]
        )

    take_field = pltpu.make_async_copy(
        field, extended.at[:, pl.ds(0, rows), pl.ds(0, cols)], field_sem
    )
    take_field.start()
    for number in range(STAGES):
        load(number).start()

    barrier = pltpu.get_barrier_semaphore()
    partners = [around(step) for step in AROUND] + [
        (owner_at(half, place[half] + step, place[1 - half]), col)
        for half in range(2)
        for step in (1, -1)
    ]
    for partner in partners:
        pl.semaphore_signal(barrier, inc=1, device_id=partner, device_id_type=MESH)

    def remote(source, target, sems, partner):
        return pltpu.make_async_remote_copy(
            src_ref=source,
            dst_ref=target,
            send_sem=sems[0],
            recv_sem=sems[1],
            device_id=partner,
            device_id_type=MESH,
        )

    def piece(half, kind, first, second):
        a, b = place[half], place[1 - half]
        lines = pl.ds(half * block, block)
        ring = 0 if kind < 4 else 1
        number = kind * SIDE + (second if ring == 0 else first)
        sems = (send_sem.at[half, number], recv_sem.at[half, number])
        if ring == 0:
            step = 1 if kind == 0 or (kind > 1 and second < 2) else -1
            partner = owner_at(half, a + step, b)
            if kind == 3:
                source, owner = passed.at[half, second], owner_at(half, a - step, b)
            else:
                offset = (1, -1, 2)[kind]
                source = sent.at[owner_at(half, a + offset, b + second), :, lines]
                owner = row
            if kind == 2:
                target = passed.at[half, second]
            elif second == 0:
                target = arrived.at[owner, :, lines]
            else:
                target = held.at[half, (0, 2, 2, 1)[kind], second - 1]
        else:
            step = 1 if kind == 4 or (kind > 5 and first < 2) else -1
            partner = owner_at(half, a, b + step)
            offset = (1, 3, 2)[kind - 4] if kind < 7 else 0
            if kind == 7:
                source = passed_again.at[half, first]
                owner = owner_at(half, a - first, b - step)
            else:
                source = (
                    sent.at[owner_at(half, a, b + offset), :, lines]
                    if first == 0
                    else held.at[half, first - 1, offset - 1]
                )
                owner = owner_at(half, a - first, b)
            target = (
                passed_again.at[half, first] if kind == 6 else arrived.at[owner, :, lines]
            )
        return remote(source, target, sems, (partner, col))

    take_field.wait()
    sent_rows[...] = extended[:, :block, :cols].astype(jnp.bfloat16)
    pl.semaphore_wait(barrier, len(partners))

    corner = (pl.ds(rows, block), pl.ds(cols, block))
    halos = [
        remote(sent_rows, got_rows, (halo_send.at[0], halo_recv.at[0]), around((-1, 0))),
        remote(
            extended.at[:, pl.ds(0, rows), pl.ds(0, block)],
            extended.at[:, pl.ds(0, rows), pl.ds(cols, block)],
            (halo_send.at[1], halo_recv.at[1]), around((0, -1)),
        ),
        remote(
            extended.at[:, pl.ds(0, block), pl.ds(0, block)],
            extended.at[(slice(None), *corner)],
            (halo_send.at[2], halo_recv.at[2]), around((-1, -1)),
        ),
    ]

    halos += [
        remote(
            wide_counts, got_counts.at[number],
            (halo_send.at[3 + number], halo_recv.at[3 + number]), around(step),
        )
        for number, step in enumerate(ONWARD)
    ]

    for number, (dx, dy) in enumerate(TAKEN):
        slot = number % STAGES
        home = owner_at(0, place[0] + dx, place[1] + dy)
        load(number).wait()

        def cast(index, carry):
            sent[home, index] = staged[slot, index].astype(jnp.bfloat16)
            return carry

        lax.fori_loop(0, sent.shape[1], cast, 0)
        if number + STAGES < len(TAKEN):
            load(number + STAGES).start()
        for half, (first, second) in enumerate(((dx, dy), (dy, dx))):
            if first:
                piece(half, (0, 2, 1)[first - 1], None, second).start()
        if number == 6:
            for copy in halos:
                copy.start()

    own = pltpu.make_async_copy(sent.at[row], arrived.at[row], own_sem)
    own.start()

    def forward(number):
        start_row = pl.multiple_of(number // spots * block, block)
        start_col = pl.multiple_of(lax.rem(number, spots) * block, block)
        view = (pl.ds(start_row, cells), pl.ds(start_col, cells))
        window_re, window_im = extended[(0, *view)], extended[(1, *view)]
        probe_re, probe_im = probe[0], probe[1]
        wave_re = (probe_re * window_re - probe_im * window_im).astype(jnp.bfloat16)
        wave_im = (probe_re * window_im + probe_im * window_re).astype(jnp.bfloat16)
        half = matmul(ahead[...], jnp.concatenate([wave_re, wave_im], axis=0)).astype(
            jnp.bfloat16
        )
        waves = matmul(jnp.concatenate([half[:cells], half[cells:]], axis=1), conjugate[...])
        far_re, far_im = waves[:, :cells], waves[:, cells:]
        inverse = jnp.minimum(
            lax.rsqrt(far_re * far_re + far_im * far_im), 1.0 / AMPLITUDE_FLOOR
        )
        far[number, 0] = far_re.astype(jnp.bfloat16)
        far[number, 1] = far_im.astype(jnp.bfloat16)
        phase[number, 0] = (far_re * inverse).astype(jnp.bfloat16)
        phase[number, 1] = (far_im * inverse).astype(jnp.bfloat16)

    def relay_first():
        for second in range(SIDE):
            for half in range(2):
                piece(half, 2, None, second).wait_recv()
                piece(half, 3, None, second).start()
        for kind in (6, 4, 5):
            for half in range(2):
                piece(half, kind, 0, None).start()

    def turn(first, second):
        arrival = (0, 3, 1)[first - 1]
        kind = {1: 4, 2: 6, 3: 5}[second]
        for half in range(2):
            piece(half, arrival, None, second).wait_recv()
            piece(half, kind, first, None).start()

    def relay_second(first):
        for half in range(2):
            piece(half, 6, first, None).wait_recv()
            piece(half, 7, first, None).start()

    def take_halos():
        for copy in halos:
            copy.wait()

        for part in range(2):
            extended[part, pl.ds(rows, block), pl.ds(0, cols)] = jnp.where(
                row < n_tx - 1, got_rows[part].astype(jnp.float32), 0.0
            )

        @pl.when(col == n_ty - 1)
        def _():
            extended[:, :, pl.ds(cols, block)] = jnp.zeros_like(extended[:, :, cols:])

        @pl.when(row == n_tx - 1)
        def _():
            extended[(slice(None), *corner)] = jnp.zeros((2, block, block), jnp.float32)

    above, left = (row > 0).astype(jnp.float32), (col > 0).astype(jnp.float32)

    def count_of(block_row, block_col):
        number = block_row % spots * spots + block_col % spots
        if block_row < 0 and block_col < 0:
            return got_counts[2, number : number + 1, :] * (above * left)
        if block_row < 0:
            return got_counts[0, number : number + 1, :] * above
        if block_col < 0:
            return got_counts[1, number : number + 1, :] * left
        return wide_counts[number : number + 1, :]

    def light_up():
        for block_row in range(rows // block):
            for block_col in range(spots):
                light = jnp.ones((block, block), jnp.float32)
                for down in range(2):
                    for right in range(2):
                        part = (pl.ds(down * block, block), pl.ds(right * block, block))
                        power = probe[(0, *part)] ** 2 + probe[(1, *part)] ** 2
                        light += count_of(block_row - down, block_col - right) * power
                spot = (pl.ds(block_row * block, block), pl.ds(block_col * block, block))
                inverse[spot] = 1.0 / light

    inner = spots - 1
    steps = {
        3: [relay_first],
        5: [functools.partial(turn, 1, 2)],
        7: [functools.partial(turn, 3, 2), take_halos],
        9: [functools.partial(turn, 1, 1)],
        11: [functools.partial(turn, 3, 1)],
        13: [functools.partial(turn, 1, 3)],
        14: [functools.partial(turn, 3, 3)],
    }

    def forward_step(index, carry):
        edge = index - inner * inner
        inside = index < inner * inner
        at_row = jnp.where(inside, index // inner, jnp.where(edge < spots, inner, edge - spots))
        at_col = jnp.where(inside, lax.rem(index, inner), jnp.where(edge < spots, edge, inner))
        forward(at_row * spots + at_col)
        for when, work in steps.items():

            @pl.when(index == when)
            def _(work=work):
                for one in work:
                    one()

        return carry

    lax.fori_loop(0, windows, forward_step, 0)
    for second in (2, 1, 3):
        turn(2, second)
    grads[...] = jnp.zeros_like(grads)
    for first in (0, 1, 3):
        relay_second(first)
    light_up()
    relay_second(2)

    own.wait()
    for half in range(2):
        for kind in (0, 1, 3):
            piece(half, kind, None, 0).wait_recv()
        for kind in (4, 5, 7):
            for first in range(SIDE):
                piece(half, kind, first, None).wait_recv()

    def add_up(index, carry):
        slot = slots[index]
        plane = arrived[slot // arrived.shape[1], lax.rem(slot, arrived.shape[1])]
        before = jnp.where(same[index] > 0, sums[jnp.maximum(index - 1, 0)], 0.0)
        sums[index] = before + plane.astype(jnp.float32)
        return carry

    lax.fori_loop(0, sums.shape[0], add_up, 0)

    sum_copies = [
        remote(source, target, (sum_send.at[number], sum_recv.at[number]), around(ONWARD[number]))
        for number, (source, target) in enumerate(
            ((sent_down, got_down), (sent_right, got_right), (sent_corner, got_corner))
        )
    ]

    def backward(index, carry):
        interior = index - 2 * spots + 1
        edge = interior < 0
        at_row = jnp.where(
            edge, jnp.where(index < spots, inner, index - spots), interior // inner
        )
        at_col = jnp.where(
            edge, jnp.where(index < spots, index, inner), lax.rem(interior, inner)
        )
        number = at_row * spots + at_col

        @pl.when(index == 2 * spots - 1)
        def _():
            sent_down[...] = grads[:, rows:, :cols].astype(jnp.bfloat16)
            sent_right[...] = grads[:, :rows, cols:].astype(jnp.bfloat16)
            sent_corner[...] = grads[:, rows:, cols:].astype(jnp.bfloat16)
            for copy in sum_copies:
                copy.start()

        count = counts[number]
        total = sums[ends[number]] * jnp.minimum(count, 1.0)
        residual = [
            (
                far[number, part].astype(jnp.float32) * count
                - phase[number, part].astype(jnp.float32) * total
            ).astype(jnp.bfloat16)
            for part in range(2)
        ]
        back = matmul(conjugate[...], jnp.concatenate(residual, axis=0)).astype(jnp.bfloat16)
        near = matmul(jnp.concatenate([back[:cells], back[cells:]], axis=1), ahead[...])
        near_re, near_im = near[:, :cells], near[:, cells:]
        probe_re, probe_im = probe[0], probe[1]
        view = (
            pl.ds(pl.multiple_of(at_row * block, block), cells),
            pl.ds(pl.multiple_of(at_col * block, block), cells),
        )
        grads[(0, *view)] += probe_re * near_re + probe_im * near_im
        grads[(1, *view)] += probe_re * near_im - probe_im * near_re
        return carry

    lax.fori_loop(0, windows, backward, 0)
    strips = cols // LANES
    for copy in sum_copies:
        copy.wait()
    for part in range(2):
        grads[part, :block, :cols] += got_down[part].astype(jnp.float32) * above
        grads[part, :rows, :block] += got_right[part].astype(jnp.float32) * left
        grads[part, :block, :block] += got_corner[part].astype(jnp.float32) * (above * left)
        for strip in range(strips):
            lanes = pl.ds(strip * LANES, LANES)
            updated = (
                extended[part, pl.ds(0, rows), lanes]
                - grads[part, pl.ds(0, rows), lanes] * inverse[:, lanes]
            )
            first_field[part, strip, pl.ds(2 * RIM, rows), :] = updated
            if strip == 0:
                column_rims[0, part] = updated.T[:RIM]
            if strip == strips - 1:
                column_rims[1, part] = updated.T[LANES - RIM :]

    top, bottom = pl.ds(2 * RIM, RIM), pl.ds(2 * RIM + rows - RIM, RIM)
    main = pl.ds(0, strips)
    rim_copies = [
        remote(source, target, (rim_send.at[number], rim_recv.at[number]), around(AROUND[number]))
        for number, (source, target) in enumerate(
            (
                (first_field.at[:, main, top], got_tops.at[1]),
                (first_field.at[:, main, bottom], got_tops.at[0]),
                (column_rims.at[0], got_columns.at[1]),
                (column_rims.at[1], got_columns.at[0]),
                (first_field.at[:, 0, top], got_corners.at[3]),
                (first_field.at[:, strips - 1, top], got_corners.at[2]),
                (first_field.at[:, 0, bottom], got_corners.at[1]),
                (first_field.at[:, strips - 1, bottom], got_corners.at[0]),
            )
        )
    ]
    for copy in rim_copies:
        copy.start()
    for copy in rim_copies:
        copy.wait()

    has_above, has_left = row > 0, col > 0
    has_below, has_right = row < n_tx - 1, col < n_ty - 1
    lane = lax.broadcasted_iota(jnp.int32, (RIM, LANES), 1)
    sublane = lax.broadcasted_iota(jnp.int32, (RIM, LANES), 0)
    on_right = lane < jnp.where(has_right, RIM, 0)
    on_left = lane >= jnp.where(has_left, LANES - RIM, LANES)
    beside = on_right | on_left
    ends_of_tile = ((0, RIM, has_above), (1, 2 * RIM + rows, has_below))
    for part in range(2):
        for number, start, exists in ends_of_tile:
            corner_cells = jnp.where(
                on_left, got_corners[2 * number, part],
                jnp.where(on_right, got_corners[2 * number + 1, part], 0.0),
            )
            spot = pl.ds(start, RIM)
            for strip in range(strips):
                first_field[part, strip, spot, :] = jnp.where(
                    exists, got_tops[number, part, strip], 0.0
                )
            first_field[part, strips, spot, :] = jnp.where(exists, corner_cells, 0.0)
        sides = jnp.concatenate(
            [
                jnp.where(has_right, got_columns[1, part], 0.0),
                jnp.zeros((LANES - 2 * RIM, rows), jnp.float32),
                jnp.where(has_left, got_columns[0, part], 0.0),
            ],
            axis=0,
        )
        first_field[part, strips, pl.ds(2 * RIM, rows), :] = sides.T

    everywhere = [(part, strip) for strip in range(strips + 1) for part in range(2)]
    blank = jnp.zeros((RIM, LANES), jnp.float32)

    def smooth(source, store, start, stop):
        def shifted(values, amount, edge):
            turned = {key: pltpu.roll(value, amount, axis=1) for key, value in values.items()}
            step = 1 if edge else -1
            return {
                (part, strip): jnp.where(
                    lane == edge, turned[part, (strip + step) % (strips + 1)], turned[part, strip]
                )
                for part, strip in everywhere
            }

        def fluxes(ahead_of, center):
            found = {}
            for strip in range(strips + 1):
                found[0, strip], found[1, strip] = flux(
                    *(ahead_of[part, strip] - center[part, strip] for part in range(2))
                )
            return found

        def chunk(number, earlier):
            start_row = pl.multiple_of((number + 1) * RIM, RIM)
            center, lower = (
                {
                    (part, strip): source[part, strip, pl.ds(start_row + offset, RIM), :]
                    for part, strip in everywhere
                }
                for offset in (0, 1)
            )
            down = fluxes(lower, center)
            right = fluxes(shifted(center, LANES - 1, LANES - 1), center)
            before = shifted(right, 1, 0)
            for at, key in enumerate(everywhere):
                up = jnp.where(
                    sublane == 0,
                    pltpu.roll(earlier[at], 1, axis=0),
                    pltpu.roll(down[key], 1, axis=0),
                )
                value = center[key] + TIME_STEP * ((down[key] - up) + (right[key] - before[key]))
                store(start_row, *key, value)
            return [down[key] for key in everywhere]

        lax.fori_loop(start, stop, chunk, [blank] * len(everywhere), unroll=UNROLL)

    def keep(target):
        def store(start_row, part, strip, value):
            if strip == strips:
                value = jnp.where(beside, value, 0.0)
            target[part, strip, pl.ds(start_row, RIM), :] = value

        return store

    def give(start_row, part, strip, value):
        if strip < strips:
            target = pl.multiple_of(jnp.maximum(start_row - 2 * RIM, 0), RIM)
            out[part, pl.ds(target, RIM), pl.ds(strip * LANES, LANES)] = value

    chunks = rows // RIM + 2
    now, later = first_field, second_field
    for _ in range(STEPS - 1):
        smooth(now, keep(later), 0, chunks)
        for _, start, exists in ends_of_tile:

            @pl.when(jnp.logical_not(exists))
            def _(start=start, later=later):
                later[:, :, pl.ds(start, RIM), :] = jnp.zeros(
                    (2, strips + 1, RIM, LANES), jnp.float32
                )

        now, later = later, now
    smooth(now, give, 0, chunks - 1)

    for half in range(2):
        for kind in range(4):
            for second in range(SIDE):
                piece(half, kind, None, second).wait_send()
        for kind in range(4, 8):
            for first in range(SIDE):
                piece(half, kind, first, None).wait_send()


def whole_step(object_field, probe_field, amplitudes, tables, scalars, wide_counts):
    rows, cols = object_field.shape[1:]
    cells = probe_field.shape[1]
    block = cells // 2
    windows = rows // block * (cols // block)
    groups = lax.axis_size("tx")
    slots = amplitudes.shape[0] // groups
    sizes = (groups, lax.axis_size("ty"))
    assert groups == SIDE * SIDE
    vmem = pl.BlockSpec(memory_space=pltpu.VMEM)
    smem = pl.BlockSpec(memory_space=pltpu.SMEM)
    anywhere = pl.BlockSpec(memory_space=pl.ANY)
    narrow, wide = jnp.bfloat16, jnp.float32
    own = (groups, slots, cells, cells)
    part = (slots, block, cells)
    strips = [(2, block, cols), (2, rows, block), (2, block, block)]
    smoothed = (2, cols // LANES + 1, rows + 4 * RIM, LANES)
    return pl.pallas_call(
        functools.partial(step_kernel, sizes),
        out_shape=jax.ShapeDtypeStruct(object_field.shape, wide),
        in_specs=[smem] * 4 + [anywhere] * 2 + [vmem] * 4,
        out_specs=vmem,
        scratch_shapes=[
            pltpu.VMEM((2, rows + block, cols + block), wide),
            pltpu.VMEM((2, block, cols), narrow),
            pltpu.VMEM((2, block, cols), narrow),
            pltpu.VMEM((STAGES, slots, cells, cells), wide),
            pltpu.VMEM(own, narrow),
            pltpu.VMEM(own, narrow),
            pltpu.VMEM((2, SIDE - 1, SIDE - 1, *part), narrow),
            pltpu.VMEM((2, SIDE, *part), narrow),
            pltpu.VMEM((2, SIDE, *part), narrow),
            pltpu.VMEM((windows, 2, cells, cells), narrow),
            pltpu.VMEM((windows, 2, cells, cells), narrow),
            pltpu.VMEM((scalars[0].shape[0], cells, cells), wide),
            pltpu.VMEM((2, rows + block, cols + block), wide),
            pltpu.VMEM((rows, cols), wide),
            pltpu.VMEM((3, *wide_counts.shape), wide),
            *(pltpu.VMEM(strip, narrow) for strip in strips * 2),
            pltpu.VMEM((2, 2, RIM, rows), wide),
            pltpu.VMEM((2, 2, cols // LANES, RIM, LANES), wide),
            pltpu.VMEM((2, 2, RIM, rows), wide),
            pltpu.VMEM((4, 2, RIM, LANES), wide),
            pltpu.VMEM(smoothed, wide),
            pltpu.VMEM(smoothed, wide),
            pltpu.SemaphoreType.DMA((STAGES,)),
            pltpu.SemaphoreType.DMA,
            pltpu.SemaphoreType.DMA,
            pltpu.SemaphoreType.DMA((6,)),
            pltpu.SemaphoreType.DMA((6,)),
            pltpu.SemaphoreType.DMA((2, 8 * SIDE)),
            pltpu.SemaphoreType.DMA((2, 8 * SIDE)),
            pltpu.SemaphoreType.DMA((3,)),
            pltpu.SemaphoreType.DMA((3,)),
            pltpu.SemaphoreType.DMA((8,)),
            pltpu.SemaphoreType.DMA((8,)),
        ],
        compiler_params=pltpu.CompilerParams(
            collective_id=1, has_side_effects=True, vmem_limit_bytes=60 << 20
        ),
        name="step",
    )(
        *scalars, object_field, amplitudes.reshape(own), probe_field, *tables, wide_counts
    )


def local(object_field, probe_field, amplitudes, scan_blocks, owner_rows):
    tile_rows, tile_cols = object_field.shape[1:]
    window_cells = probe_field.shape[1]
    block_cells = window_cells // 2
    positions_here = owner_rows.shape[0]
    pair_slots = amplitudes.shape[0] // lax.axis_size("tx")
    spots = tile_cols // block_cells
    windows = tile_rows // block_cells * spots

    order = jnp.arange(positions_here, dtype=jnp.int32)
    earlier = order[None, :] < order[:, None]
    pair_rank = jnp.sum((owner_rows[:, None] == owner_rows[None, :]) & earlier, axis=1)
    slot_index = owner_rows * pair_slots + pair_rank.astype(jnp.int32)
    window_index = (
        (scan_blocks[:, 0] - lax.axis_index("tx") * (tile_rows // block_cells)) * spots
        + scan_blocks[:, 1] - lax.axis_index("ty") * spots
    )
    before = (window_index[None, :] < window_index[:, None]) | (
        (window_index[None, :] == window_index[:, None]) & earlier
    )
    place = jnp.sum(before, axis=1)
    slots = jnp.sum(
        jnp.where(place[None, :] == order[:, None], slot_index[None, :], 0), axis=1
    ).astype(jnp.int32)
    bounds = jnp.arange(windows, dtype=jnp.int32)
    counts = jnp.sum(window_index[None, :] == bounds[:, None], axis=1).astype(jnp.float32)
    ends = jnp.sum(window_index[None, :] <= bounds[:, None], axis=1).astype(jnp.int32)
    follows = (window_index[None, :] == window_index[:, None]) & earlier
    same = jnp.sum(
        jnp.where(place[None, :] == order[:, None], jnp.any(follows, axis=1)[None, :], False),
        axis=1,
    ).astype(jnp.int32)
    scalars = (slots, same, jnp.maximum(ends - 1, 0), counts)
    wide_counts = jnp.broadcast_to(counts[:, None], (windows, LANES))
    tables = complex_tables(window_cells)
    return whole_step(object_field, probe_field, amplitudes, tables, scalars, wide_counts)


def solution(mesh):
    in_specs = (
        P(None, "tx", "ty"),
        P(),
        P("tx", "ty", None),
        P(("tx", "ty"), None),
        P(("tx", "ty")),
    )
    out_specs = P(None, "tx", "ty")
    return jax.shard_map(local, mesh=mesh, in_specs=in_specs, out_specs=out_specs, check_vma=False)
```

```python
import functools

import jax
import jax.numpy as jnp
import numpy as np
from jax import lax
from jax.experimental import pallas as pl
from jax.experimental.pallas import tpu as pltpu
from jax.sharding import PartitionSpec as P

STEPS = 4
ROUNDS = 2


KAPPA_SQ = 1.0
TIME_STEP = 0.2
AMPLITUDE_FLOOR = 0.5


def complex_tables(window_cells):
    counter = np.arange(window_cells)
    phases = counter[:, None] * counter[None, :] % window_cells
    angles = phases.astype(np.float32) * np.float32(2.0 * np.pi / window_cells)
    scaling = np.float32(1.0 / np.sqrt(window_cells))
    cosine, sine = (np.cos(angles) * scaling, np.sin(angles) * scaling)
    ahead = np.block([[cosine, sine], [-sine, cosine]])
    conjugate = np.block([[cosine, -sine], [sine, cosine]])
    lines = np.arange(2 * window_cells).reshape(2, 2, ROUNDS, -1)
    split = np.stack([conjugate[:, lines[:, :, number].reshape(-1)] for number in range(ROUNDS)])
    return tuple(jnp.asarray(table, jnp.bfloat16) for table in (ahead, conjugate, split))


def matmul(first, second):
    return jnp.dot(first, second, preferred_element_type=jnp.float32)


LANES = 128
RIM = 8
UNROLL = 6
GRANT = 55
MESH = pl.DeviceIdType.MESH
ONWARD = ((1, 0), (0, 1), (1, 1))
AROUND = ((-1, 0), (1, 0), (0, -1), (0, 1), (-1, -1), (-1, 1), (1, -1), (1, 1))


def flux(real, imag):
    weight = 1.0 / (1.0 + (real * real + imag * imag) * (1.0 / KAPPA_SQ))
    return weight * real, weight * imag


SIDE = 4
STAGES = 4
TAKEN = tuple(
    sorted(
        ((dx, dy) for dx in range(SIDE) for dy in range(SIDE)),
        key=lambda step: (step == (0, 0), 2 not in step, 0 in step),
    )
)


def step_kernel(
    sizes, scan_blocks, owners, field, amplitudes, probe, ahead, conjugate, split, out,
    slots, same, ends, counts, places, spots_of, slots_of, follows, wide_counts,
    extended, sent_rows, got_rows, staged, sent, arrived_first, arrived_second,
    held, passed, passed_again,
    far, phase, sums, grads, inverse, got_counts,
    sent_down, sent_right, sent_corner, got_down, got_right, got_corner,
    column_rims, got_tops, got_columns, got_corners, first_field, second_field,
    stage_sem, field_sem, own_sem, halo_send, halo_recv, send_sem, recv_sem,
    sum_send, sum_recv, rim_send, rim_recv,
):
    n_tx, n_ty = sizes
    cells = probe.shape[1]
    block = cells // 2
    rows, cols = extended.shape[1] - block, extended.shape[2] - block
    spots = cols // block
    windows = rows // block * spots
    row, col = lax.axis_index("tx"), lax.axis_index("ty")
    place = (row // SIDE, lax.rem(row, SIDE))

    def around(step):
        return (lax.rem(row + step[0] + n_tx, n_tx), lax.rem(col + step[1] + n_ty, n_ty))

    def owner_at(half, first, second):
        first, second = lax.rem(first + SIDE, SIDE), lax.rem(second + SIDE, SIDE)
        return first * SIDE + second if half == 0 else second * SIDE + first

    def load(number):
        dx, dy = TAKEN[number]
        home = owner_at(0, place[0] + dx, place[1] + dy)
        slot = number % STAGES
        return pltpu.make_async_copy(
            amplitudes.at[home], staged.at[slot], stage_sem.at[slot]
        )

    take_field = pltpu.make_async_copy(
        field, extended.at[:, pl.ds(0, rows), pl.ds(0, cols)], field_sem
    )
    take_field.start()
    for number in range(STAGES):
        load(number).start()

    barrier = pltpu.get_barrier_semaphore()
    partners = [around(step) for step in AROUND] + [
        (owner_at(half, place[half] + step, place[1 - half]), col)
        for half in range(2)
        for step in (1, -1)
    ]
    for partner in partners:
        pl.semaphore_signal(barrier, inc=1, device_id=partner, device_id_type=MESH)

    def remote(source, target, sems, partner):
        return pltpu.make_async_remote_copy(
            src_ref=source,
            dst_ref=target,
            send_sem=sems[0],
            recv_sem=sems[1],
            device_id=partner,
            device_id_type=MESH,
        )

    depth = block // ROUNDS
    arrived = (arrived_first, arrived_second)
    pair_slots = sent.shape[1]

    def piece(half, kind, first, second, turn_of):
        a, b = place[half], place[1 - half]
        inside = pl.ds(turn_of * depth, depth)
        lines = pl.ds(half * block + turn_of * depth, depth)
        landing = pl.ds(half * depth, depth)
        ring = 0 if kind < 4 else 1
        number = kind * SIDE + (second if ring == 0 else first)
        sems = (send_sem.at[turn_of, half, number], recv_sem.at[turn_of, half, number])
        if ring == 0:
            step = 1 if kind == 0 or (kind > 1 and second < 2) else -1
            partner = owner_at(half, a + step, b)
            if kind == 3:
                source, owner = passed.at[half, second, :, inside], owner_at(half, a - step, b)
            else:
                offset = (1, -1, 2)[kind]
                source = sent.at[owner_at(half, a + offset, b + second), :, lines]
                owner = row
            if kind == 2:
                target = passed.at[half, second, :, inside]
            elif second == 0:
                target = arrived[turn_of].at[owner, :, landing]
            else:
                target = held.at[half, (0, 2, 2, 1)[kind], second - 1, :, inside]
        else:
            step = 1 if kind == 4 or (kind > 5 and first < 2) else -1
            partner = owner_at(half, a, b + step)
            offset = (1, 3, 2)[kind - 4] if kind < 7 else 0
            if kind == 7:
                source = passed_again.at[half, first, :, inside]
                owner = owner_at(half, a - first, b - step)
            else:
                source = (
                    sent.at[owner_at(half, a, b + offset), :, lines]
                    if first == 0
                    else held.at[half, first - 1, offset - 1, :, inside]
                )
                owner = owner_at(half, a - first, b)
            target = (
                passed_again.at[half, first, :, inside]
                if kind == 6
                else arrived[turn_of].at[owner, :, landing]
            )
        return remote(source, target, sems, (partner, col))

    take_field.wait()
    sent_rows[...] = extended[:, :block, :cols].astype(jnp.bfloat16)
    pl.semaphore_wait(barrier, len(partners))

    corner = (pl.ds(rows, block), pl.ds(cols, block))
    halos = [
        remote(sent_rows, got_rows, (halo_send.at[0], halo_recv.at[0]), around((-1, 0))),
        remote(
            extended.at[:, pl.ds(0, rows), pl.ds(0, block)],
            extended.at[:, pl.ds(0, rows), pl.ds(cols, block)],
            (halo_send.at[1], halo_recv.at[1]), around((0, -1)),
        ),
        remote(
            extended.at[:, pl.ds(0, block), pl.ds(0, block)],
            extended.at[(slice(None), *corner)],
            (halo_send.at[2], halo_recv.at[2]), around((-1, -1)),
        ),
    ]

    count_copies = [
        remote(
            wide_counts, got_counts.at[number],
            (halo_send.at[3 + number], halo_recv.at[3 + number]), around(step),
        )
        for number, step in enumerate(ONWARD)
    ]

    for number, (dx, dy) in enumerate(TAKEN):
        slot = number % STAGES
        home = owner_at(0, place[0] + dx, place[1] + dy)
        load(number).wait()

        def cast(index, carry):
            sent[home, index] = staged[slot, index].astype(jnp.bfloat16)
            return carry

        lax.fori_loop(0, sent.shape[1], cast, 0)
        if number + STAGES < len(TAKEN):
            load(number + STAGES).start()
        for half, (first, second) in enumerate(((dx, dy), (dy, dx))):
            if first:
                piece(half, (0, 2, 1)[first - 1], None, second, 0).start()
        if number == 6:
            for copy in halos:
                copy.start()

    own_copies = [
        pltpu.make_async_copy(
            sent.at[row, :, pl.ds(half * block + turn_of * depth, depth)],
            arrived[turn_of].at[row, :, pl.ds(half * depth, depth)],
            own_sem.at[turn_of, half],
        )
        for turn_of in range(ROUNDS)
        for half in range(2)
    ]
    for copy in own_copies:
        copy.start()

    def forward(number):
        start_row = pl.multiple_of(number // spots * block, block)
        start_col = pl.multiple_of(lax.rem(number, spots) * block, block)
        view = (pl.ds(start_row, cells), pl.ds(start_col, cells))
        window_re, window_im = extended[(0, *view)], extended[(1, *view)]
        probe_re, probe_im = probe[0], probe[1]
        wave_re = (probe_re * window_re - probe_im * window_im).astype(jnp.bfloat16)
        wave_im = (probe_re * window_im + probe_im * window_re).astype(jnp.bfloat16)
        half = matmul(ahead[...], jnp.concatenate([wave_re, wave_im], axis=0)).astype(
            jnp.bfloat16
        )
        waves = matmul(jnp.concatenate([half[:cells], half[cells:]], axis=1), conjugate[...])
        far_re, far_im = waves[:, :cells], waves[:, cells:]
        inverse = jnp.minimum(
            lax.rsqrt(far_re * far_re + far_im * far_im), 1.0 / AMPLITUDE_FLOOR
        )
        far[number, 0] = far_re.astype(jnp.bfloat16)
        far[number, 1] = far_im.astype(jnp.bfloat16)
        phase[number, 0] = (far_re * inverse).astype(jnp.bfloat16)
        phase[number, 1] = (far_im * inverse).astype(jnp.bfloat16)

    def send_far():
        for second in range(SIDE):
            for half in range(2):
                piece(half, 2, None, second, 1).start()

    def send_near():
        for second in (2, 1, 3, 0):
            for kind in range(2):
                for half in range(2):
                    piece(half, kind, None, second, 1).start()

    def relay_first(turn_of):
        for second in range(SIDE):
            for half in range(2):
                piece(half, 2, None, second, turn_of).wait_recv()
                piece(half, 3, None, second, turn_of).start()
        for kind in (6, 4, 5):
            for half in range(2):
                piece(half, kind, 0, None, turn_of).start()

    def turn(first, second, turn_of):
        arrival = (0, 3, 1)[first - 1]
        kind = {1: 4, 2: 6, 3: 5}[second]
        for half in range(2):
            piece(half, arrival, None, second, turn_of).wait_recv()
            piece(half, kind, first, None, turn_of).start()

    def relay_second(first, turn_of):
        for half in range(2):
            piece(half, 6, first, None, turn_of).wait_recv()
            piece(half, 7, first, None, turn_of).start()

    def work_out_tables():
        total = range(owners.shape[0])

        def spot_of(at, carry):
            spots_of[at] = (
                (scan_blocks[0, at] - row * (rows // block)) * spots
                + scan_blocks[1, at] - col * spots
            )
            return carry

        def place_of(at, carry):
            rank, ahead_of, matches = (jnp.zeros((), jnp.int32) for _ in range(3))
            for other in total:
                earlier = other < at
                rank += jnp.where((owners[other] == owners[at]) & earlier, 1, 0)
                ahead_of += jnp.where(spots_of[other] < spots_of[at], 1, 0)
                matches += jnp.where((spots_of[other] == spots_of[at]) & earlier, 1, 0)
            places[at] = ahead_of + matches
            follows[at] = jnp.minimum(matches, 1)
            slots_of[at] = owners[at] * pair_slots + rank
            return carry

        def sorted_at(at, carry):
            slot, joins = (jnp.zeros((), jnp.int32) for _ in range(2))
            for other in total:
                slot += jnp.where(places[other] == at, slots_of[other], 0)
                joins += jnp.where(places[other] == at, follows[other], 0)
            slots[at] = slot
            same[at] = joins
            return carry

        def count_at(at, carry):
            count, up_to = (jnp.zeros((), jnp.int32) for _ in range(2))
            for other in total:
                count += jnp.where(spots_of[other] == at, 1, 0)
                up_to += jnp.where(spots_of[other] <= at, 1, 0)
            counts[at] = count.astype(jnp.float32)
            ends[at] = jnp.maximum(up_to - 1, 0)
            return carry

        lax.fori_loop(0, len(total), spot_of, 0)
        lax.fori_loop(0, len(total), place_of, 0)
        lax.fori_loop(0, len(total), sorted_at, 0)
        lax.fori_loop(0, windows, count_at, 0)
        for number in range(windows):
            wide_counts[number : number + 1, :] = jnp.full((1, LANES), counts[number])
        for copy in count_copies:
            copy.start()

    def take_halos():
        for copy in halos:
            copy.wait()

        for part in range(2):
            extended[part, pl.ds(rows, block), pl.ds(0, cols)] = jnp.where(
                row < n_tx - 1, got_rows[part].astype(jnp.float32), 0.0
            )

        @pl.when(col == n_ty - 1)
        def _():
            extended[:, :, pl.ds(cols, block)] = jnp.zeros_like(extended[:, :, cols:])

        @pl.when(row == n_tx - 1)
        def _():
            extended[(slice(None), *corner)] = jnp.zeros((2, block, block), jnp.float32)

    above, left = (row > 0).astype(jnp.float32), (col > 0).astype(jnp.float32)

    def count_of(block_row, block_col):
        number = block_row % spots * spots + block_col % spots
        if block_row < 0 and block_col < 0:
            return got_counts[2, number : number + 1, :] * (above * left)
        if block_row < 0:
            return got_counts[0, number : number + 1, :] * above
        if block_col < 0:
            return got_counts[1, number : number + 1, :] * left
        return wide_counts[number : number + 1, :]

    def light_up():
        for block_row in range(rows // block):
            for block_col in range(spots):
                light = jnp.ones((block, block), jnp.float32)
                for down in range(2):
                    for right in range(2):
                        part = (pl.ds(down * block, block), pl.ds(right * block, block))
                        power = probe[(0, *part)] ** 2 + probe[(1, *part)] ** 2
                        light += count_of(block_row - down, block_col - right) * power
                spot = (pl.ds(block_row * block, block), pl.ds(block_col * block, block))
                inverse[spot] = 1.0 / light

    inner = spots - 1
    steps = {
        3: [functools.partial(relay_first, 0)],
        5: [functools.partial(turn, 1, 2, 0)],
        6: [send_far],
        7: [functools.partial(turn, 3, 2, 0), take_halos],
        8: [send_near],
        9: [functools.partial(turn, 1, 1, 0)],
        10: [functools.partial(turn, 3, 1, 0)],
        11: [functools.partial(turn, 1, 3, 0)],
        12: [functools.partial(turn, 3, 3, 0)],
        13: [functools.partial(relay_first, 1)],
        14: [functools.partial(turn, 2, 2, 0)],
    }

    def forward_step(index, carry):
        edge = index - inner * inner
        inside = index < inner * inner
        at_row = jnp.where(inside, index // inner, jnp.where(edge < spots, inner, edge - spots))
        at_col = jnp.where(inside, lax.rem(index, inner), jnp.where(edge < spots, edge, inner))
        forward(at_row * spots + at_col)
        for when, work in steps.items():

            @pl.when(index == when)
            def _(work=work):
                for one in work:
                    one()

        return carry

    lax.fori_loop(0, windows, forward_step, 0)
    work_out_tables()
    for second in (1, 3):
        turn(2, second, 0)
    for first in (0, 1, 3, 2):
        relay_second(first, 0)
    for second in (2, 1, 3):
        for first in (1, 3):
            turn(first, second, 1)
    grads[...] = jnp.zeros_like(grads)
    for second in (2, 1, 3):
        turn(2, second, 1)
    for copy in count_copies:
        copy.wait()
    light_up()
    for copy in own_copies:
        copy.wait()

    sum_copies = [
        remote(source, target, (sum_send.at[number], sum_recv.at[number]), around(ONWARD[number]))
        for number, (source, target) in enumerate(
            ((sent_down, got_down), (sent_right, got_right), (sent_corner, got_corner))
        )
    ]

    def round_lines(turn_of):
        return [
            pl.ds(pl.multiple_of(half * block + turn_of * depth, depth), depth)
            for half in range(2)
        ]

    def add_up(turn_of, index, carry):
        slot = slots[index]
        owner, rank = slot // pair_slots, lax.rem(slot, pair_slots)
        for half, lines in enumerate(round_lines(turn_of)):
            before = jnp.where(same[index] > 0, sums[jnp.maximum(index - 1, 0), lines], 0.0)
            plane = arrived[turn_of][owner, rank, pl.ds(half * depth, depth)]
            sums[index, lines] = before + plane.astype(jnp.float32)
        return carry

    def take_round(turn_of):
        for half in range(2):
            for kind in (0, 1, 3):
                piece(half, kind, None, 0, turn_of).wait_recv()
            for kind in (4, 5, 7):
                for first in range(SIDE):
                    piece(half, kind, first, None, turn_of).wait_recv()
        lax.fori_loop(0, sums.shape[0], functools.partial(add_up, turn_of), 0)

    def backward(step, carry):
        turn_of, index = step // windows, lax.rem(step, windows)

        for number in range(ROUNDS):

            @pl.when(step == number * windows)
            def _(number=number):
                take_round(number)

        for when, first in ((2, 0), (4, 1), (7, 3), (10, 2)):

            @pl.when(step == when)
            def _(first=first):
                relay_second(first, 1)

        interior = index - 2 * spots + 1
        edge = interior < 0
        at_row = jnp.where(
            edge, jnp.where(index < spots, inner, index - spots), interior // inner
        )
        at_col = jnp.where(
            edge, jnp.where(index < spots, index, inner), lax.rem(interior, inner)
        )
        number = at_row * spots + at_col

        @pl.when(step == windows + 2 * spots - 1)
        def _():
            sent_down[...] = grads[:, rows:, :cols].astype(jnp.bfloat16)
            sent_right[...] = grads[:, :rows, cols:].astype(jnp.bfloat16)
            sent_corner[...] = grads[:, rows:, cols:].astype(jnp.bfloat16)
            for copy in sum_copies:
                copy.start()

        count = counts[number]
        used = jnp.minimum(count, 1.0)
        last = ends[number]
        parts = []
        for part in range(2):
            pieces = [
                far[number, part, lines].astype(jnp.float32) * count
                - phase[number, part, lines].astype(jnp.float32) * (sums[last, lines] * used)
                for lines in round_lines(turn_of)
            ]
            parts.append(jnp.concatenate(pieces, axis=0).astype(jnp.bfloat16))
        across = matmul(jnp.concatenate(parts, axis=1), ahead[...]).astype(jnp.bfloat16)
        near = matmul(
            split[turn_of], jnp.concatenate([across[:, :cells], across[:, cells:]], axis=0)
        )
        near_re, near_im = near[:cells], near[cells:]
        probe_re, probe_im = probe[0], probe[1]
        view = (
            pl.ds(pl.multiple_of(at_row * block, block), cells),
            pl.ds(pl.multiple_of(at_col * block, block), cells),
        )
        grads[(0, *view)] += probe_re * near_re + probe_im * near_im
        grads[(1, *view)] += probe_re * near_im - probe_im * near_re
        return carry

    lax.fori_loop(0, ROUNDS * windows, backward, 0)
    strips = cols // LANES
    for copy in sum_copies:
        copy.wait()
    for part in range(2):
        grads[part, :block, :cols] += got_down[part].astype(jnp.float32) * above
        grads[part, :rows, :block] += got_right[part].astype(jnp.float32) * left
        grads[part, :block, :block] += got_corner[part].astype(jnp.float32) * (above * left)
        for strip in range(strips):
            lanes = pl.ds(strip * LANES, LANES)
            updated = (
                extended[part, pl.ds(0, rows), lanes]
                - grads[part, pl.ds(0, rows), lanes] * inverse[:, lanes]
            )
            first_field[part, strip, pl.ds(2 * RIM, rows), :] = updated
            if strip == 0:
                column_rims[0, part] = updated.T[:RIM]
            if strip == strips - 1:
                column_rims[1, part] = updated.T[LANES - RIM :]

    top, bottom = pl.ds(2 * RIM, RIM), pl.ds(2 * RIM + rows - RIM, RIM)
    main = pl.ds(0, strips)
    rim_copies = [
        remote(source, target, (rim_send.at[number], rim_recv.at[number]), around(AROUND[number]))
        for number, (source, target) in enumerate(
            (
                (first_field.at[:, main, top], got_tops.at[1]),
                (first_field.at[:, main, bottom], got_tops.at[0]),
                (column_rims.at[0], got_columns.at[1]),
                (column_rims.at[1], got_columns.at[0]),
                (first_field.at[:, 0, top], got_corners.at[3]),
                (first_field.at[:, strips - 1, top], got_corners.at[2]),
                (first_field.at[:, 0, bottom], got_corners.at[1]),
                (first_field.at[:, strips - 1, bottom], got_corners.at[0]),
            )
        )
    ]
    for copy in rim_copies:
        copy.start()
    for copy in rim_copies:
        copy.wait()

    has_above, has_left = row > 0, col > 0
    has_below, has_right = row < n_tx - 1, col < n_ty - 1
    lane = lax.broadcasted_iota(jnp.int32, (RIM, LANES), 1)
    sublane = lax.broadcasted_iota(jnp.int32, (RIM, LANES), 0)
    on_right = lane < jnp.where(has_right, RIM, 0)
    on_left = lane >= jnp.where(has_left, LANES - RIM, LANES)
    beside = on_right | on_left
    ends_of_tile = ((0, RIM, has_above), (1, 2 * RIM + rows, has_below))
    for part in range(2):
        for number, start, exists in ends_of_tile:
            corner_cells = jnp.where(
                on_left, got_corners[2 * number, part],
                jnp.where(on_right, got_corners[2 * number + 1, part], 0.0),
            )
            spot = pl.ds(start, RIM)
            for strip in range(strips):
                first_field[part, strip, spot, :] = jnp.where(
                    exists, got_tops[number, part, strip], 0.0
                )
            first_field[part, strips, spot, :] = jnp.where(exists, corner_cells, 0.0)
        sides = jnp.concatenate(
            [
                jnp.where(has_right, got_columns[1, part], 0.0),
                jnp.zeros((LANES - 2 * RIM, rows), jnp.float32),
                jnp.where(has_left, got_columns[0, part], 0.0),
            ],
            axis=0,
        )
        first_field[part, strips, pl.ds(2 * RIM, rows), :] = sides.T

    everywhere = [(part, strip) for strip in range(strips + 1) for part in range(2)]
    blank = jnp.zeros((RIM, LANES), jnp.float32)

    def smooth(source, store, start, stop):
        def shifted(values, amount, edge):
            turned = {key: pltpu.roll(value, amount, axis=1) for key, value in values.items()}
            step = 1 if edge else -1
            return {
                (part, strip): jnp.where(
                    lane == edge, turned[part, (strip + step) % (strips + 1)], turned[part, strip]
                )
                for part, strip in everywhere
            }

        def fluxes(ahead_of, center):
            found = {}
            for strip in range(strips + 1):
                found[0, strip], found[1, strip] = flux(
                    *(ahead_of[part, strip] - center[part, strip] for part in range(2))
                )
            return found

        def chunk(number, earlier):
            start_row = pl.multiple_of((number + 1) * RIM, RIM)
            center, lower = (
                {
                    (part, strip): source[part, strip, pl.ds(start_row + offset, RIM), :]
                    for part, strip in everywhere
                }
                for offset in (0, 1)
            )
            down = fluxes(lower, center)
            right = fluxes(shifted(center, LANES - 1, LANES - 1), center)
            before = shifted(right, 1, 0)
            for at, key in enumerate(everywhere):
                up = jnp.where(
                    sublane == 0,
                    pltpu.roll(earlier[at], 1, axis=0),
                    pltpu.roll(down[key], 1, axis=0),
                )
                value = center[key] + TIME_STEP * ((down[key] - up) + (right[key] - before[key]))
                store(start_row, *key, value)
            return [down[key] for key in everywhere]

        lax.fori_loop(start, stop, chunk, [blank] * len(everywhere), unroll=UNROLL)

    def keep(target):
        def store(start_row, part, strip, value):
            if strip == strips:
                value = jnp.where(beside, value, 0.0)
            target[part, strip, pl.ds(start_row, RIM), :] = value

        return store

    def give(start_row, part, strip, value):
        if strip < strips:
            target = pl.multiple_of(jnp.maximum(start_row - 2 * RIM, 0), RIM)
            out[part, pl.ds(target, RIM), pl.ds(strip * LANES, LANES)] = value

    chunks = rows // RIM + 2
    now, later = first_field, second_field
    for _ in range(STEPS - 1):
        smooth(now, keep(later), 0, chunks)
        for _, start, exists in ends_of_tile:

            @pl.when(jnp.logical_not(exists))
            def _(start=start, later=later):
                later[:, :, pl.ds(start, RIM), :] = jnp.zeros(
                    (2, strips + 1, RIM, LANES), jnp.float32
                )

        now, later = later, now
    smooth(now, give, 0, chunks - 1)

    for turn_of in range(ROUNDS):
        for half in range(2):
            for kind in range(4):
                for second in range(SIDE):
                    piece(half, kind, None, second, turn_of).wait_send()
            for kind in range(4, 8):
                for first in range(SIDE):
                    piece(half, kind, first, None, turn_of).wait_send()


def whole_step(object_field, probe_field, amplitudes, scan_blocks, owner_rows):
    rows, cols = object_field.shape[1:]
    cells = probe_field.shape[1]
    block = cells // 2
    windows = rows // block * (cols // block)
    groups = lax.axis_size("tx")
    slots = amplitudes.shape[0] // groups
    sizes = (groups, lax.axis_size("ty"))
    positions = owner_rows.shape[0]
    assert groups == SIDE * SIDE
    vmem = pl.BlockSpec(memory_space=pltpu.VMEM)
    smem = pl.BlockSpec(memory_space=pltpu.SMEM)
    anywhere = pl.BlockSpec(memory_space=pl.ANY)
    narrow, wide = jnp.bfloat16, jnp.float32
    own = (groups, slots, cells, cells)
    part = (slots, block, cells)
    strips = [(2, block, cols), (2, rows, block), (2, block, block)]
    smoothed = (2, cols // LANES + 1, rows + 4 * RIM, LANES)
    return pl.pallas_call(
        functools.partial(step_kernel, sizes),
        out_shape=jax.ShapeDtypeStruct(object_field.shape, wide),
        in_specs=[smem] * 2 + [anywhere] * 2 + [vmem] * 4,
        out_specs=vmem,
        scratch_shapes=[
            *(
                pltpu.SMEM((length,), kind)
                for length, kind in (
                    (positions, jnp.int32), (positions, jnp.int32), (windows, jnp.int32),
                    (windows, wide), *((positions, jnp.int32) for _ in range(4)),
                )
            ),
            pltpu.VMEM((windows, LANES), wide),
            pltpu.VMEM((2, rows + block, cols + block), wide),
            pltpu.VMEM((2, block, cols), narrow),
            pltpu.VMEM((2, block, cols), narrow),
            pltpu.VMEM((STAGES, slots, cells, cells), wide),
            pltpu.VMEM(own, narrow),
            *(pltpu.VMEM((groups, slots, cells // ROUNDS, cells), narrow) for _ in range(ROUNDS)),
            pltpu.VMEM((2, SIDE - 1, SIDE - 1, *part), narrow),
            pltpu.VMEM((2, SIDE, *part), narrow),
            pltpu.VMEM((2, SIDE, *part), narrow),
            pltpu.VMEM((windows, 2, cells, cells), narrow),
            pltpu.VMEM((windows, 2, cells, cells), narrow),
            pltpu.VMEM((positions, cells, cells), wide),
            pltpu.VMEM((2, rows + block, cols + block), wide),
            pltpu.VMEM((rows, cols), wide),
            pltpu.VMEM((3, windows, LANES), wide),
            *(pltpu.VMEM(strip, narrow) for strip in strips * 2),
            pltpu.VMEM((2, 2, RIM, rows), wide),
            pltpu.VMEM((2, 2, cols // LANES, RIM, LANES), wide),
            pltpu.VMEM((2, 2, RIM, rows), wide),
            pltpu.VMEM((4, 2, RIM, LANES), wide),
            pltpu.VMEM(smoothed, wide),
            pltpu.VMEM(smoothed, wide),
            pltpu.SemaphoreType.DMA((STAGES,)),
            pltpu.SemaphoreType.DMA,
            pltpu.SemaphoreType.DMA((ROUNDS, 2)),
            pltpu.SemaphoreType.DMA((6,)),
            pltpu.SemaphoreType.DMA((6,)),
            pltpu.SemaphoreType.DMA((ROUNDS, 2, 8 * SIDE)),
            pltpu.SemaphoreType.DMA((ROUNDS, 2, 8 * SIDE)),
            pltpu.SemaphoreType.DMA((3,)),
            pltpu.SemaphoreType.DMA((3,)),
            pltpu.SemaphoreType.DMA((8,)),
            pltpu.SemaphoreType.DMA((8,)),
        ],
        compiler_params=pltpu.CompilerParams(
            collective_id=1, has_side_effects=True, vmem_limit_bytes=GRANT << 20
        ),
        name="step",
    )(
        scan_blocks.T, owner_rows, object_field, amplitudes.reshape(own), probe_field,
        *complex_tables(cells)
    )


def solution(mesh):
    in_specs = (
        P(None, "tx", "ty"),
        P(),
        P("tx", "ty", None),
        P(("tx", "ty"), None),
        P(("tx", "ty")),
    )
    out_specs = P(None, "tx", "ty")
    return jax.shard_map(whole_step, mesh=mesh, in_specs=in_specs, out_specs=out_specs, check_vma=False)
```

```python
import functools

import jax
import jax.numpy as jnp
import numpy as np
from jax import lax
from jax.experimental import pallas as pl
from jax.experimental.pallas import tpu as pltpu
from jax.sharding import PartitionSpec as P

STEPS = 4
ROUNDS = 2


KAPPA_SQ = 1.0
TIME_STEP = 0.2
AMPLITUDE_FLOOR = 0.5


def complex_tables(window_cells):
    counter = np.arange(window_cells)
    phases = counter[:, None] * counter[None, :] % window_cells
    angles = phases.astype(np.float32) * np.float32(2.0 * np.pi / window_cells)
    scaling = np.float32(1.0 / np.sqrt(window_cells))
    cosine, sine = (np.cos(angles) * scaling, np.sin(angles) * scaling)
    ahead = np.block([[cosine, sine], [-sine, cosine]])
    conjugate = np.block([[cosine, -sine], [sine, cosine]])
    lines = np.arange(2 * window_cells).reshape(2, 2, ROUNDS, -1)
    split = np.stack([conjugate[:, lines[:, :, number].reshape(-1)] for number in range(ROUNDS)])
    return tuple(jnp.asarray(table, jnp.bfloat16) for table in (ahead, conjugate, split))


def matmul(first, second):
    return jnp.dot(first, second, preferred_element_type=jnp.float32)


LANES = 128
RIM = 8
UNROLL = 6
GRANT = 49
MESH = pl.DeviceIdType.MESH
ONWARD = ((1, 0), (0, 1), (1, 1))
AROUND = ((-1, 0), (1, 0), (0, -1), (0, 1), (-1, -1), (-1, 1), (1, -1), (1, 1))


def flux(real, imag):
    weight = 1.0 / (1.0 + (real * real + imag * imag) * (1.0 / KAPPA_SQ))
    return weight * real, weight * imag


SIDE = 4
STAGES = 2
TAKEN = tuple(
    sorted(
        ((dx, dy) for dx in range(SIDE) for dy in range(SIDE)),
        key=lambda step: (step == (0, 0), 2 not in step, 0 in step),
    )
)


def step_kernel(
    sizes, scan_blocks, owners, field, amplitudes, probe_given, ahead_given, conjugate_given,
    split_given, out, probe, ahead, conjugate, split,
    slots, same, ends, counts, places, spots_of, slots_of, follows, wide_counts,
    extended, sent_rows, got_rows, staged, sent, arrived_first, arrived_second,
    held, passed, passed_again,
    far, phase, sums, grads, inverse, got_counts,
    sent_right, sent_corner, got_down, got_right, got_corner,
    column_rims, got_tops, got_columns, got_corners, first_field, second_field,
    stage_sem, field_sem, table_sem, own_sem, halo_send, halo_recv, send_sem, recv_sem,
    sum_send, sum_recv, rim_send, rim_recv,
):
    n_tx, n_ty = sizes
    cells = probe.shape[1]
    block = cells // 2
    rows, cols = extended.shape[1] - block, extended.shape[2] - block
    spots = cols // block
    windows = rows // block * spots
    row, col = lax.axis_index("tx"), lax.axis_index("ty")
    place = (row // SIDE, lax.rem(row, SIDE))

    def around(step):
        return (lax.rem(row + step[0] + n_tx, n_tx), lax.rem(col + step[1] + n_ty, n_ty))

    def owner_at(half, first, second):
        first, second = lax.rem(first + SIDE, SIDE), lax.rem(second + SIDE, SIDE)
        return first * SIDE + second if half == 0 else second * SIDE + first

    def load(number):
        dx, dy = TAKEN[number]
        home = owner_at(0, place[0] + dx, place[1] + dy)
        slot = number % STAGES
        return pltpu.make_async_copy(
            amplitudes.at[home], staged.at[slot], stage_sem.at[slot]
        )

    take_field = pltpu.make_async_copy(
        field, extended.at[:, pl.ds(0, rows), pl.ds(0, cols)], field_sem
    )
    take_tables = [
        pltpu.make_async_copy(source, target, table_sem.at[number])
        for number, (source, target) in enumerate(
            (
                (probe_given, probe), (ahead_given, ahead), (conjugate_given, conjugate),
                (split_given, split),
            )
        )
    ]
    for number in range(STAGES):
        load(number).start()
    take_field.start()

    barrier = pltpu.get_barrier_semaphore()
    partners = [around(step) for step in AROUND] + [
        (owner_at(half, place[half] + step, place[1 - half]), col)
        for half in range(2)
        for step in (1, -1)
    ]
    for partner in partners:
        pl.semaphore_signal(barrier, inc=1, device_id=partner, device_id_type=MESH)

    def remote(source, target, sems, partner):
        return pltpu.make_async_remote_copy(
            src_ref=source,
            dst_ref=target,
            send_sem=sems[0],
            recv_sem=sems[1],
            device_id=partner,
            device_id_type=MESH,
        )

    depth = block // ROUNDS
    arrived = (arrived_first, arrived_second)
    pair_slots = sent.shape[1]

    def piece(half, kind, first, second, turn_of):
        a, b = place[half], place[1 - half]
        inside = pl.ds(turn_of * depth, depth)
        lines = pl.ds(half * block + turn_of * depth, depth)
        landing = pl.ds(half * depth, depth)
        ring = 0 if kind < 4 else 1
        number = kind * SIDE + (second if ring == 0 else first)
        sems = (send_sem.at[turn_of, half, number], recv_sem.at[turn_of, half, number])
        if ring == 0:
            upward = 3 if (half, turn_of) == (1, 0) else 2
            step = 1 if kind == 0 or (kind > 1 and second < upward) else -1
            partner = owner_at(half, a + step, b)
            if kind == 3:
                source, owner = passed.at[half, second, :, inside], owner_at(half, a - step, b)
            else:
                offset = (1, -1, 2)[kind]
                source = sent.at[owner_at(half, a + offset, b + second), :, lines]
                owner = row
            if kind == 2:
                target = passed.at[half, second, :, inside]
            elif second == 0:
                target = arrived[turn_of].at[owner, :, landing]
            else:
                target = held.at[half, (0, 2, 2, 1)[kind], second - 1, :, inside]
        else:
            step = 1 if kind == 4 or (kind > 5 and first < 2) else -1
            partner = owner_at(half, a, b + step)
            offset = (1, 3, 2)[kind - 4] if kind < 7 else 0
            if kind == 7:
                source = passed_again.at[half, first, :, inside]
                owner = owner_at(half, a - first, b - step)
            else:
                source = (
                    sent.at[owner_at(half, a, b + offset), :, lines]
                    if first == 0
                    else held.at[half, first - 1, offset - 1, :, inside]
                )
                owner = owner_at(half, a - first, b)
            target = (
                passed_again.at[half, first, :, inside]
                if kind == 6
                else arrived[turn_of].at[owner, :, landing]
            )
        return remote(source, target, sems, (partner, col))

    corner = (pl.ds(rows, block), pl.ds(cols, block))
    halos = [
        remote(sent_rows, got_rows, (halo_send.at[0], halo_recv.at[0]), around((-1, 0))),
        remote(
            extended.at[:, pl.ds(0, rows), pl.ds(0, block)],
            extended.at[:, pl.ds(0, rows), pl.ds(cols, block)],
            (halo_send.at[1], halo_recv.at[1]), around((0, -1)),
        ),
        remote(
            extended.at[:, pl.ds(0, block), pl.ds(0, block)],
            extended.at[(slice(None), *corner)],
            (halo_send.at[2], halo_recv.at[2]), around((-1, -1)),
        ),
    ]

    count_copies = [
        remote(
            wide_counts, got_counts.at[number],
            (halo_send.at[3 + number], halo_recv.at[3 + number]), around(step),
        )
        for number, step in enumerate(ONWARD)
    ]

    for number, (dx, dy) in enumerate(TAKEN):
        slot = number % STAGES
        home = owner_at(0, place[0] + dx, place[1] + dy)
        load(number).wait()

        def cast(index, carry):
            sent[home, index] = staged[slot, index].astype(jnp.bfloat16)
            return carry

        lax.fori_loop(0, sent.shape[1], cast, 0)
        if number == 0:
            pl.semaphore_wait(barrier, len(partners))
        if number + STAGES < len(TAKEN):
            load(number + STAGES).start()
        for half, (first, second) in enumerate(((dx, dy), (dy, dx))):
            if first:
                piece(half, (0, 2, 1)[first - 1], None, second, 0).start()
        if number == 4:
            for copy in take_tables:
                copy.start()
            take_field.wait()
            sent_rows[...] = extended[:, :block, :cols].astype(jnp.bfloat16)
        if number == 6:
            for copy in halos:
                copy.start()

    own_copies = [
        pltpu.make_async_copy(
            sent.at[row, :, pl.ds(half * block + turn_of * depth, depth)],
            arrived[turn_of].at[row, :, pl.ds(half * depth, depth)],
            own_sem.at[turn_of, half],
        )
        for turn_of in range(ROUNDS)
        for half in range(2)
    ]
    for copy in own_copies:
        copy.start()

    def forward(number):
        start_row = pl.multiple_of(number // spots * block, block)
        start_col = pl.multiple_of(lax.rem(number, spots) * block, block)
        view = (pl.ds(start_row, cells), pl.ds(start_col, cells))
        window_re, window_im = extended[(0, *view)], extended[(1, *view)]
        probe_re, probe_im = probe[0], probe[1]
        wave_re = (probe_re * window_re - probe_im * window_im).astype(jnp.bfloat16)
        wave_im = (probe_re * window_im + probe_im * window_re).astype(jnp.bfloat16)
        half = matmul(ahead[...], jnp.concatenate([wave_re, wave_im], axis=0)).astype(
            jnp.bfloat16
        )
        waves = matmul(jnp.concatenate([half[:cells], half[cells:]], axis=1), conjugate[...])
        far_re, far_im = waves[:, :cells], waves[:, cells:]
        inverse = jnp.minimum(
            lax.rsqrt(far_re * far_re + far_im * far_im), 1.0 / AMPLITUDE_FLOOR
        )
        far[number, 0] = far_re.astype(jnp.bfloat16)
        far[number, 1] = far_im.astype(jnp.bfloat16)
        phase[number, 0] = (far_re * inverse).astype(jnp.bfloat16)
        phase[number, 1] = (far_im * inverse).astype(jnp.bfloat16)

    def send_far():
        for second in range(SIDE):
            for half in range(2):
                piece(half, 2, None, second, 1).start()

    def send_near():
        for second in (2, 1, 3, 0):
            for kind in range(2):
                for half in range(2):
                    piece(half, kind, None, second, 1).start()

    def relay_first(turn_of):
        for second in range(SIDE):
            for half in range(2):
                piece(half, 2, None, second, turn_of).wait_recv()
                piece(half, 3, None, second, turn_of).start()
        for kind in (6, 4, 5):
            for half in range(2):
                piece(half, kind, 0, None, turn_of).start()

    def turn(first, second, turn_of):
        arrival = (0, 3, 1)[first - 1]
        kind = {1: 4, 2: 6, 3: 5}[second]
        for half in range(2):
            piece(half, arrival, None, second, turn_of).wait_recv()
            piece(half, kind, first, None, turn_of).start()

    def relay_second(first, turn_of):
        for half in range(2):
            piece(half, 6, first, None, turn_of).wait_recv()
            piece(half, 7, first, None, turn_of).start()

    def work_out_tables():
        total = range(owners.shape[0])

        def spot_of(at, carry):
            spots_of[at] = (
                (scan_blocks[0, at] - row * (rows // block)) * spots
                + scan_blocks[1, at] - col * spots
            )
            return carry

        def place_of(at, carry):
            rank, ahead_of, matches = (jnp.zeros((), jnp.int32) for _ in range(3))
            for other in total:
                earlier = other < at
                rank += jnp.where((owners[other] == owners[at]) & earlier, 1, 0)
                ahead_of += jnp.where(spots_of[other] < spots_of[at], 1, 0)
                matches += jnp.where((spots_of[other] == spots_of[at]) & earlier, 1, 0)
            places[at] = ahead_of + matches
            follows[at] = jnp.minimum(matches, 1)
            slots_of[at] = owners[at] * pair_slots + rank
            return carry

        def sorted_at(at, carry):
            slot, joins = (jnp.zeros((), jnp.int32) for _ in range(2))
            for other in total:
                slot += jnp.where(places[other] == at, slots_of[other], 0)
                joins += jnp.where(places[other] == at, follows[other], 0)
            slots[at] = slot
            same[at] = joins
            return carry

        def count_at(at, carry):
            count, up_to = (jnp.zeros((), jnp.int32) for _ in range(2))
            for other in total:
                count += jnp.where(spots_of[other] == at, 1, 0)
                up_to += jnp.where(spots_of[other] <= at, 1, 0)
            counts[at] = count.astype(jnp.float32)
            ends[at] = jnp.maximum(up_to - 1, 0)
            return carry

        lax.fori_loop(0, len(total), spot_of, 0)
        lax.fori_loop(0, len(total), place_of, 0)
        lax.fori_loop(0, len(total), sorted_at, 0)
        lax.fori_loop(0, windows, count_at, 0)
        for number in range(windows):
            wide_counts[number : number + 1, :] = jnp.full((1, LANES), counts[number])
        for copy in count_copies:
            copy.start()

    def take_halos():
        for copy in halos:
            copy.wait()

        for part in range(2):
            extended[part, pl.ds(rows, block), pl.ds(0, cols)] = jnp.where(
                row < n_tx - 1, got_rows[part].astype(jnp.float32), 0.0
            )

        @pl.when(col == n_ty - 1)
        def _():
            extended[:, :, pl.ds(cols, block)] = jnp.zeros_like(extended[:, :, cols:])

        @pl.when(row == n_tx - 1)
        def _():
            extended[(slice(None), *corner)] = jnp.zeros((2, block, block), jnp.float32)

    above, left = (row > 0).astype(jnp.float32), (col > 0).astype(jnp.float32)

    def count_of(block_row, block_col):
        number = block_row % spots * spots + block_col % spots
        if block_row < 0 and block_col < 0:
            return got_counts[2, number : number + 1, :] * (above * left)
        if block_row < 0:
            return got_counts[0, number : number + 1, :] * above
        if block_col < 0:
            return got_counts[1, number : number + 1, :] * left
        return wide_counts[number : number + 1, :]

    def light_up():
        for block_row in range(rows // block):
            for block_col in range(spots):
                light = jnp.ones((block, block), jnp.float32)
                for down in range(2):
                    for right in range(2):
                        part = (pl.ds(down * block, block), pl.ds(right * block, block))
                        power = probe[(0, *part)] ** 2 + probe[(1, *part)] ** 2
                        light += count_of(block_row - down, block_col - right) * power
                spot = (pl.ds(block_row * block, block), pl.ds(block_col * block, block))
                inverse[spot] = 1.0 / light

    inner = spots - 1
    steps = {
        3: [functools.partial(relay_first, 0)],
        5: [functools.partial(turn, 1, 2, 0)],
        6: [send_far],
        7: [functools.partial(turn, 3, 2, 0), take_halos],
        8: [send_near],
        9: [functools.partial(turn, 1, 1, 0)],
        10: [functools.partial(turn, 3, 1, 0)],
        11: [functools.partial(turn, 1, 3, 0)],
        12: [functools.partial(turn, 3, 3, 0)],
        13: [functools.partial(relay_first, 1)],
        14: [functools.partial(turn, 2, 2, 0)],
    }

    for copy in take_tables:
        copy.wait()

    def forward_step(index, carry):
        edge = index - inner * inner
        inside = index < inner * inner
        at_row = jnp.where(inside, index // inner, jnp.where(edge < spots, inner, edge - spots))
        at_col = jnp.where(inside, lax.rem(index, inner), jnp.where(edge < spots, edge, inner))
        forward(at_row * spots + at_col)
        for when, work in steps.items():

            @pl.when(index == when)
            def _(work=work):
                for one in work:
                    one()

        return carry

    lax.fori_loop(0, windows, forward_step, 0)
    work_out_tables()
    for second in (1, 3):
        turn(2, second, 0)
    for first in (0, 1, 3, 2):
        relay_second(first, 0)
    for second in (2, 1, 3):
        for first in (1, 3):
            turn(first, second, 1)
    grads[...] = jnp.zeros_like(grads)
    for second in (2, 1, 3):
        turn(2, second, 1)
    for copy in count_copies:
        copy.wait()
    light_up()
    for copy in own_copies:
        copy.wait()

    sum_copies = [
        remote(source, target, (sum_send.at[number], sum_recv.at[number]), around(ONWARD[number]))
        for number, (source, target) in enumerate(
            ((sent_rows, got_down), (sent_right, got_right), (sent_corner, got_corner))
        )
    ]

    def round_lines(turn_of):
        return [
            pl.ds(pl.multiple_of(half * block + turn_of * depth, depth), depth)
            for half in range(2)
        ]

    def add_up(turn_of, index, carry):
        slot = slots[index]
        owner, rank = slot // pair_slots, lax.rem(slot, pair_slots)
        for half, lines in enumerate(round_lines(turn_of)):
            before = jnp.where(same[index] > 0, sums[jnp.maximum(index - 1, 0), lines], 0.0)
            plane = arrived[turn_of][owner, rank, pl.ds(half * depth, depth)]
            sums[index, lines] = before + plane.astype(jnp.float32)
        return carry

    def take_round(turn_of):
        for half in range(2):
            for kind in (0, 1, 3):
                piece(half, kind, None, 0, turn_of).wait_recv()
            for kind in (4, 5, 7):
                for first in range(SIDE):
                    piece(half, kind, first, None, turn_of).wait_recv()
        lax.fori_loop(0, sums.shape[0], functools.partial(add_up, turn_of), 0)

    def backward(step, carry):
        turn_of, index = step // windows, lax.rem(step, windows)

        for number in range(ROUNDS):

            @pl.when(step == number * windows)
            def _(number=number):
                take_round(number)

        for when, first in ((2, 0), (4, 1), (7, 3), (10, 2)):

            @pl.when(step == when)
            def _(first=first):
                relay_second(first, 1)

        interior = index - 2 * spots + 1
        edge = interior < 0
        at_row = jnp.where(
            edge, jnp.where(index < spots, inner, index - spots), interior // inner
        )
        at_col = jnp.where(
            edge, jnp.where(index < spots, index, inner), lax.rem(interior, inner)
        )
        number = at_row * spots + at_col

        @pl.when(step == windows + spots)
        def _():
            sent_rows[...] = grads[:, rows:, :cols].astype(jnp.bfloat16)
            sent_corner[...] = grads[:, rows:, cols:].astype(jnp.bfloat16)
            sum_copies[2].start()
            sum_copies[0].start()

        @pl.when(step == windows + 2 * spots - 1)
        def _():
            sent_right[...] = grads[:, :rows, cols:].astype(jnp.bfloat16)
            sum_copies[1].start()

        count = counts[number]
        used = jnp.minimum(count, 1.0)
        last = ends[number]
        parts = []
        for part in range(2):
            pieces = [
                far[number, part, lines].astype(jnp.float32) * count
                - phase[number, part, lines].astype(jnp.float32) * (sums[last, lines] * used)
                for lines in round_lines(turn_of)
            ]
            parts.append(jnp.concatenate(pieces, axis=0).astype(jnp.bfloat16))
        across = matmul(jnp.concatenate(parts, axis=1), ahead[...]).astype(jnp.bfloat16)
        near = matmul(
            split[turn_of], jnp.concatenate([across[:, :cells], across[:, cells:]], axis=0)
        )
        near_re, near_im = near[:cells], near[cells:]
        probe_re, probe_im = probe[0], probe[1]
        view = (
            pl.ds(pl.multiple_of(at_row * block, block), cells),
            pl.ds(pl.multiple_of(at_col * block, block), cells),
        )
        grads[(0, *view)] += probe_re * near_re + probe_im * near_im
        grads[(1, *view)] += probe_re * near_im - probe_im * near_re
        return carry

    lax.fori_loop(0, ROUNDS * windows, backward, 0)
    strips = cols // LANES
    for copy in sum_copies:
        copy.wait()
    for part in range(2):
        grads[part, :block, :cols] += got_down[part].astype(jnp.float32) * above
        grads[part, :rows, :block] += got_right[part].astype(jnp.float32) * left
        grads[part, :block, :block] += got_corner[part].astype(jnp.float32) * (above * left)
        for strip in range(strips):
            lanes = pl.ds(strip * LANES, LANES)
            updated = (
                extended[part, pl.ds(0, rows), lanes]
                - grads[part, pl.ds(0, rows), lanes] * inverse[:, lanes]
            )
            first_field[part, strip, pl.ds(2 * RIM, rows), :] = updated
            if strip == 0:
                column_rims[0, part] = updated.T[:RIM]
            if strip == strips - 1:
                column_rims[1, part] = updated.T[LANES - RIM :]

    top, bottom = pl.ds(2 * RIM, RIM), pl.ds(2 * RIM + rows - RIM, RIM)
    main = pl.ds(0, strips)
    rim_copies = [
        remote(source, target, (rim_send.at[number], rim_recv.at[number]), around(AROUND[number]))
        for number, (source, target) in enumerate(
            (
                (first_field.at[:, main, top], got_tops.at[1]),
                (first_field.at[:, main, bottom], got_tops.at[0]),
                (column_rims.at[0], got_columns.at[1]),
                (column_rims.at[1], got_columns.at[0]),
                (first_field.at[:, 0, top], got_corners.at[3]),
                (first_field.at[:, strips - 1, top], got_corners.at[2]),
                (first_field.at[:, 0, bottom], got_corners.at[1]),
                (first_field.at[:, strips - 1, bottom], got_corners.at[0]),
            )
        )
    ]
    for copy in rim_copies:
        copy.start()
    for copy in rim_copies:
        copy.wait()

    has_above, has_left = row > 0, col > 0
    has_below, has_right = row < n_tx - 1, col < n_ty - 1
    lane = lax.broadcasted_iota(jnp.int32, (RIM, LANES), 1)
    sublane = lax.broadcasted_iota(jnp.int32, (RIM, LANES), 0)
    on_right = lane < jnp.where(has_right, RIM, 0)
    on_left = lane >= jnp.where(has_left, LANES - RIM, LANES)
    beside = on_right | on_left
    ends_of_tile = ((0, RIM, has_above), (1, 2 * RIM + rows, has_below))
    for part in range(2):
        for number, start, exists in ends_of_tile:
            corner_cells = jnp.where(
                on_left, got_corners[2 * number, part],
                jnp.where(on_right, got_corners[2 * number + 1, part], 0.0),
            )
            spot = pl.ds(start, RIM)
            for strip in range(strips):
                first_field[part, strip, spot, :] = jnp.where(
                    exists, got_tops[number, part, strip], 0.0
                )
            first_field[part, strips, spot, :] = jnp.where(exists, corner_cells, 0.0)
        sides = jnp.concatenate(
            [
                jnp.where(has_right, got_columns[1, part], 0.0),
                jnp.zeros((LANES - 2 * RIM, rows), jnp.float32),
                jnp.where(has_left, got_columns[0, part], 0.0),
            ],
            axis=0,
        )
        first_field[part, strips, pl.ds(2 * RIM, rows), :] = sides.T

    everywhere = [(part, strip) for strip in range(strips + 1) for part in range(2)]
    blank = jnp.zeros((RIM, LANES), jnp.float32)

    def smooth(source, store, start, stop):
        def shifted(values, amount, edge):
            turned = {key: pltpu.roll(value, amount, axis=1) for key, value in values.items()}
            step = 1 if edge else -1
            return {
                (part, strip): jnp.where(
                    lane == edge, turned[part, (strip + step) % (strips + 1)], turned[part, strip]
                )
                for part, strip in everywhere
            }

        def fluxes(ahead_of, center):
            found = {}
            for strip in range(strips + 1):
                found[0, strip], found[1, strip] = flux(
                    *(ahead_of[part, strip] - center[part, strip] for part in range(2))
                )
            return found

        def chunk(number, earlier):
            start_row = pl.multiple_of((number + 1) * RIM, RIM)
            center, lower = (
                {
                    (part, strip): source[part, strip, pl.ds(start_row + offset, RIM), :]
                    for part, strip in everywhere
                }
                for offset in (0, 1)
            )
            down = fluxes(lower, center)
            right = fluxes(shifted(center, LANES - 1, LANES - 1), center)
            before = shifted(right, 1, 0)
            for at, key in enumerate(everywhere):
                up = jnp.where(
                    sublane == 0,
                    pltpu.roll(earlier[at], 1, axis=0),
                    pltpu.roll(down[key], 1, axis=0),
                )
                value = center[key] + TIME_STEP * ((down[key] - up) + (right[key] - before[key]))
                store(start_row, *key, value)
            return [down[key] for key in everywhere]

        lax.fori_loop(start, stop, chunk, [blank] * len(everywhere), unroll=UNROLL)

    def keep(target):
        def store(start_row, part, strip, value):
            if strip == strips:
                value = jnp.where(beside, value, 0.0)
            target[part, strip, pl.ds(start_row, RIM), :] = value

        return store

    def give(start_row, part, strip, value):
        if strip < strips:
            target = pl.multiple_of(jnp.maximum(start_row - 2 * RIM, 0), RIM)
            out[part, pl.ds(target, RIM), pl.ds(strip * LANES, LANES)] = value

    chunks = rows // RIM + 2
    now, later = first_field, second_field
    for _ in range(STEPS - 1):
        smooth(now, keep(later), 0, chunks)
        for _, start, exists in ends_of_tile:

            @pl.when(jnp.logical_not(exists))
            def _(start=start, later=later):
                later[:, :, pl.ds(start, RIM), :] = jnp.zeros(
                    (2, strips + 1, RIM, LANES), jnp.float32
                )

        now, later = later, now
    smooth(now, give, 0, chunks - 1)

    for turn_of in range(ROUNDS):
        for half in range(2):
            for kind in range(4):
                for second in range(SIDE):
                    piece(half, kind, None, second, turn_of).wait_send()
            for kind in range(4, 8):
                for first in range(SIDE):
                    piece(half, kind, first, None, turn_of).wait_send()


def whole_step(object_field, probe_field, amplitudes, scan_blocks, owner_rows):
    rows, cols = object_field.shape[1:]
    cells = probe_field.shape[1]
    block = cells // 2
    windows = rows // block * (cols // block)
    groups = lax.axis_size("tx")
    slots = amplitudes.shape[0] // groups
    sizes = (groups, lax.axis_size("ty"))
    positions = owner_rows.shape[0]
    tables = complex_tables(cells)
    assert groups == SIDE * SIDE
    vmem = pl.BlockSpec(memory_space=pltpu.VMEM)
    smem = pl.BlockSpec(memory_space=pltpu.SMEM)
    anywhere = pl.BlockSpec(memory_space=pltpu.HBM)
    narrow, wide = jnp.bfloat16, jnp.float32
    own = (groups, slots, cells, cells)
    part = (slots, block, cells)
    strips = [(2, block, cols), (2, rows, block), (2, block, block)]
    smoothed = (2, cols // LANES + 1, rows + 4 * RIM, LANES)
    return pl.pallas_call(
        functools.partial(step_kernel, sizes),
        out_shape=jax.ShapeDtypeStruct(object_field.shape, wide),
        in_specs=[smem] * 2 + [anywhere] * 6,
        out_specs=vmem,
        scratch_shapes=[
            pltpu.VMEM(probe_field.shape, wide),
            *(pltpu.VMEM(table.shape, narrow) for table in tables),
            *(
                pltpu.SMEM((length,), kind)
                for length, kind in (
                    (positions, jnp.int32), (positions, jnp.int32), (windows, jnp.int32),
                    (windows, wide), *((positions, jnp.int32) for _ in range(4)),
                )
            ),
            pltpu.VMEM((windows, LANES), wide),
            pltpu.VMEM((2, rows + block, cols + block), wide),
            pltpu.VMEM((2, block, cols), narrow),
            pltpu.VMEM((2, block, cols), narrow),
            pltpu.VMEM((STAGES, slots, cells, cells), wide),
            pltpu.VMEM(own, narrow),
            *(pltpu.VMEM((groups, slots, cells // ROUNDS, cells), narrow) for _ in range(ROUNDS)),
            pltpu.VMEM((2, SIDE - 1, SIDE - 1, *part), narrow),
            pltpu.VMEM((2, SIDE, *part), narrow),
            pltpu.VMEM((2, SIDE, *part), narrow),
            pltpu.VMEM((windows, 2, cells, cells), narrow),
            pltpu.VMEM((windows, 2, cells, cells), narrow),
            pltpu.VMEM((positions, cells, cells), wide),
            pltpu.VMEM((2, rows + block, cols + block), wide),
            pltpu.VMEM((rows, cols), wide),
            pltpu.VMEM((3, windows, LANES), wide),
            *(pltpu.VMEM(strip, narrow) for strip in strips[1:] + strips),
            pltpu.VMEM((2, 2, RIM, rows), wide),
            pltpu.VMEM((2, 2, cols // LANES, RIM, LANES), wide),
            pltpu.VMEM((2, 2, RIM, rows), wide),
            pltpu.VMEM((4, 2, RIM, LANES), wide),
            pltpu.VMEM(smoothed, wide),
            pltpu.VMEM(smoothed, wide),
            pltpu.SemaphoreType.DMA((STAGES,)),
            pltpu.SemaphoreType.DMA,
            pltpu.SemaphoreType.DMA((4,)),
            pltpu.SemaphoreType.DMA((ROUNDS, 2)),
            pltpu.SemaphoreType.DMA((6,)),
            pltpu.SemaphoreType.DMA((6,)),
            pltpu.SemaphoreType.DMA((ROUNDS, 2, 8 * SIDE)),
            pltpu.SemaphoreType.DMA((ROUNDS, 2, 8 * SIDE)),
            pltpu.SemaphoreType.DMA((3,)),
            pltpu.SemaphoreType.DMA((3,)),
            pltpu.SemaphoreType.DMA((8,)),
            pltpu.SemaphoreType.DMA((8,)),
        ],
        compiler_params=pltpu.CompilerParams(
            collective_id=1, has_side_effects=True, vmem_limit_bytes=GRANT << 20
        ),
        name="step",
    )(
        scan_blocks.T, owner_rows, object_field, amplitudes.reshape(own), probe_field,
        *tables
    )


def solution(mesh):
    in_specs = (
        P(None, "tx", "ty"),
        P(),
        P("tx", "ty", None),
        P(("tx", "ty"), None),
        P(("tx", "ty")),
    )
    out_specs = P(None, "tx", "ty")
    return jax.shard_map(whole_step, mesh=mesh, in_specs=in_specs, out_specs=out_specs, check_vma=False)
```

```python
import functools

import jax
import jax.numpy as jnp
import numpy as np
from jax import lax
from jax.experimental import pallas as pl
from jax.experimental.pallas import tpu as pltpu
from jax.sharding import PartitionSpec as P

STEPS = 4
ROUNDS = 2


KAPPA_SQ = 1.0
TIME_STEP = 0.2
AMPLITUDE_FLOOR = 0.5


def complex_tables(window_cells):
    counter = np.arange(window_cells)
    phases = counter[:, None] * counter[None, :] % window_cells
    angles = phases.astype(np.float32) * np.float32(2.0 * np.pi / window_cells)
    scaling = np.float32(1.0 / np.sqrt(window_cells))
    cosine, sine = (np.cos(angles) * scaling, np.sin(angles) * scaling)
    ahead = np.block([[cosine, sine], [-sine, cosine]])
    conjugate = np.block([[cosine, -sine], [sine, cosine]])
    lines = np.arange(2 * window_cells).reshape(2, 2, ROUNDS, -1)
    split = np.stack([conjugate[:, lines[:, :, number].reshape(-1)] for number in range(ROUNDS)])
    return tuple(jnp.asarray(table, jnp.bfloat16) for table in (ahead, conjugate, split))


def matmul(first, second):
    return jnp.dot(first, second, preferred_element_type=jnp.float32)


LANES = 128
RIM = 8
UNROLL = 6
GRANT = 55
MESH = pl.DeviceIdType.MESH
ONWARD = ((1, 0), (0, 1), (1, 1))
AROUND = ((-1, 0), (1, 0), (0, -1), (0, 1), (-1, -1), (-1, 1), (1, -1), (1, 1))


def flux(real, imag):
    weight = 1.0 / (1.0 + (real * real + imag * imag) * (1.0 / KAPPA_SQ))
    return weight * real, weight * imag


SIDE = 4
STAGES = 3
TAKEN = tuple(
    sorted(
        ((dx, dy) for dx in range(SIDE) for dy in range(SIDE)),
        key=lambda step: (step == (0, 0), 2 not in step, 0 in step),
    )
)


def step_kernel(
    sizes, scan_blocks, owners, field, amplitudes, probe_given, ahead_given, conjugate_given,
    split_given, out, probe, ahead, conjugate, split,
    slots, same, ends, counts, places, spots_of, slots_of, follows, wide_counts,
    extended, sent_rows, got_rows, staged, sent, arrived_first, arrived_second,
    held, passed, passed_again,
    far, phase, sums, grads, inverse, got_counts,
    sent_right, sent_corner, got_down, got_right, got_corner,
    column_rims, got_tops, got_columns, got_corners, first_field, second_field,
    stage_sem, field_sem, table_sem, own_sem, halo_send, halo_recv, send_sem, recv_sem,
    sum_send, sum_recv, rim_send, rim_recv,
):
    n_tx, n_ty = sizes
    cells = probe.shape[1]
    block = cells // 2
    rows, cols = extended.shape[1] - block, extended.shape[2] - block
    spots = cols // block
    windows = rows // block * spots
    row, col = lax.axis_index("tx"), lax.axis_index("ty")
    place = (row // SIDE, lax.rem(row, SIDE))

    def around(step):
        return (lax.rem(row + step[0] + n_tx, n_tx), lax.rem(col + step[1] + n_ty, n_ty))

    def owner_at(half, first, second):
        first, second = lax.rem(first + SIDE, SIDE), lax.rem(second + SIDE, SIDE)
        return first * SIDE + second if half == 0 else second * SIDE + first

    def load(number):
        dx, dy = TAKEN[number]
        home = owner_at(0, place[0] + dx, place[1] + dy)
        slot = number % STAGES
        return pltpu.make_async_copy(
            amplitudes.at[home], staged.at[slot], stage_sem.at[slot]
        )

    take_field = pltpu.make_async_copy(
        field, extended.at[:, pl.ds(0, rows), pl.ds(0, cols)], field_sem
    )
    take_tables = [
        pltpu.make_async_copy(source, target, table_sem.at[number])
        for number, (source, target) in enumerate(
            (
                (probe_given, probe), (ahead_given, ahead), (conjugate_given, conjugate),
                (split_given, split),
            )
        )
    ]
    for number in range(STAGES):
        load(number).start()
    take_field.start()

    barrier = pltpu.get_barrier_semaphore()
    partners = [around(step) for step in AROUND] + [
        (owner_at(half, place[half] + step, place[1 - half]), col)
        for half in range(2)
        for step in (1, -1)
    ]
    for partner in partners:
        pl.semaphore_signal(barrier, inc=1, device_id=partner, device_id_type=MESH)

    def remote(source, target, sems, partner):
        return pltpu.make_async_remote_copy(
            src_ref=source,
            dst_ref=target,
            send_sem=sems[0],
            recv_sem=sems[1],
            device_id=partner,
            device_id_type=MESH,
        )

    depth = block // ROUNDS
    arrived = (arrived_first, arrived_second)
    pair_slots = sent.shape[1]

    def piece(half, kind, first, second, turn_of):
        a, b = place[half], place[1 - half]
        inside = pl.ds(turn_of * depth, depth)
        lines = pl.ds(half * block + turn_of * depth, depth)
        landing = pl.ds(half * depth, depth)
        ring = 0 if kind < 4 else 1
        number = kind * SIDE + (second if ring == 0 else first)
        sems = (send_sem.at[turn_of, half, number], recv_sem.at[turn_of, half, number])
        if ring == 0:
            upward = 3 if (half, turn_of) == (1, 0) else 2
            step = 1 if kind == 0 or (kind > 1 and second < upward) else -1
            partner = owner_at(half, a + step, b)
            if kind == 3:
                source, owner = passed.at[half, second, :, inside], owner_at(half, a - step, b)
            else:
                offset = (1, -1, 2)[kind]
                source = sent.at[owner_at(half, a + offset, b + second), :, lines]
                owner = row
            if kind == 2:
                target = passed.at[half, second, :, inside]
            elif second == 0:
                target = arrived[turn_of].at[owner, :, landing]
            else:
                target = held.at[half, (0, 2, 2, 1)[kind], second - 1, :, inside]
        else:
            step = 1 if kind == 4 or (kind > 5 and first < 2) else -1
            partner = owner_at(half, a, b + step)
            offset = (1, 3, 2)[kind - 4] if kind < 7 else 0
            if kind == 7:
                source = passed_again.at[half, first, :, inside]
                owner = owner_at(half, a - first, b - step)
            else:
                source = (
                    sent.at[owner_at(half, a, b + offset), :, lines]
                    if first == 0
                    else held.at[half, first - 1, offset - 1, :, inside]
                )
                owner = owner_at(half, a - first, b)
            target = (
                passed_again.at[half, first, :, inside]
                if kind == 6
                else arrived[turn_of].at[owner, :, landing]
            )
        return remote(source, target, sems, (partner, col))

    corner = (pl.ds(rows, block), pl.ds(cols, block))
    halos = [
        remote(sent_rows, got_rows, (halo_send.at[0], halo_recv.at[0]), around((-1, 0))),
        remote(
            extended.at[:, pl.ds(0, rows), pl.ds(0, block)],
            extended.at[:, pl.ds(0, rows), pl.ds(cols, block)],
            (halo_send.at[1], halo_recv.at[1]), around((0, -1)),
        ),
        remote(
            extended.at[:, pl.ds(0, block), pl.ds(0, block)],
            extended.at[(slice(None), *corner)],
            (halo_send.at[2], halo_recv.at[2]), around((-1, -1)),
        ),
    ]

    count_copies = [
        remote(
            wide_counts, got_counts.at[number],
            (halo_send.at[3 + number], halo_recv.at[3 + number]), around(step),
        )
        for number, step in enumerate(ONWARD)
    ]

    for number, (dx, dy) in enumerate(TAKEN):
        slot = number % STAGES
        home = owner_at(0, place[0] + dx, place[1] + dy)
        load(number).wait()

        def cast(index, carry):
            sent[home, index] = staged[slot, index].astype(jnp.bfloat16)
            return carry

        lax.fori_loop(0, sent.shape[1], cast, 0)
        if number == 0:
            pl.semaphore_wait(barrier, len(partners))
        if number + STAGES < len(TAKEN):
            load(number + STAGES).start()
        for half, (first, second) in enumerate(((dx, dy), (dy, dx))):
            if first:
                piece(half, (0, 2, 1)[first - 1], None, second, 0).start()
        if number == 4:
            for copy in take_tables:
                copy.start()
            take_field.wait()
            sent_rows[...] = extended[:, :block, :cols].astype(jnp.bfloat16)
        if number == 6:
            for copy in halos:
                copy.start()

    own_copies = [
        pltpu.make_async_copy(
            sent.at[row, :, pl.ds(half * block + turn_of * depth, depth)],
            arrived[turn_of].at[row, :, pl.ds(half * depth, depth)],
            own_sem.at[turn_of, half],
        )
        for turn_of in range(ROUNDS)
        for half in range(2)
    ]
    for copy in own_copies:
        copy.start()

    def forward(number):
        start_row = pl.multiple_of(number // spots * block, block)
        start_col = pl.multiple_of(lax.rem(number, spots) * block, block)
        view = (pl.ds(start_row, cells), pl.ds(start_col, cells))
        window_re, window_im = extended[(0, *view)], extended[(1, *view)]
        probe_re, probe_im = probe[0], probe[1]
        wave_re = (probe_re * window_re - probe_im * window_im).astype(jnp.bfloat16)
        wave_im = (probe_re * window_im + probe_im * window_re).astype(jnp.bfloat16)
        half = matmul(ahead[...], jnp.concatenate([wave_re, wave_im], axis=0)).astype(
            jnp.bfloat16
        )
        waves = matmul(jnp.concatenate([half[:cells], half[cells:]], axis=1), conjugate[...])
        far_re, far_im = waves[:, :cells], waves[:, cells:]
        inverse = jnp.minimum(
            lax.rsqrt(far_re * far_re + far_im * far_im), 1.0 / AMPLITUDE_FLOOR
        )
        far[number, 0] = far_re.astype(jnp.bfloat16)
        far[number, 1] = far_im.astype(jnp.bfloat16)
        phase[number, 0] = (far_re * inverse).astype(jnp.bfloat16)
        phase[number, 1] = (far_im * inverse).astype(jnp.bfloat16)

    def send_far():
        for second in range(SIDE):
            for half in range(2):
                piece(half, 2, None, second, 1).start()

    def send_near():
        for second in (2, 1, 3):
            for kind in range(2):
                for half in range(2):
                    piece(half, kind, None, second, 1).start()

    def send_last():
        for half in range(2):
            for kind in range(2):
                piece(half, kind, None, 0, 1).start()
            for kind in (4, 5):
                piece(half, kind, 0, None, 1).start()

    def relay_first(turn_of):
        for second in range(SIDE):
            for half in range(2):
                piece(half, 2, None, second, turn_of).wait_recv()
                piece(half, 3, None, second, turn_of).start()
        for kind in (6,) if turn_of == ROUNDS - 1 else (6, 4, 5):
            for half in range(2):
                piece(half, kind, 0, None, turn_of).start()

    def turn(first, second, turn_of):
        arrival = (0, 3, 1)[first - 1]
        kind = {1: 4, 2: 6, 3: 5}[second]
        for half in range(2):
            piece(half, arrival, None, second, turn_of).wait_recv()
            piece(half, kind, first, None, turn_of).start()

    def relay_second(first, turn_of):
        for half in range(2):
            piece(half, 6, first, None, turn_of).wait_recv()
            piece(half, 7, first, None, turn_of).start()

    def work_out_tables():
        total = range(owners.shape[0])

        def spot_of(at, carry):
            spots_of[at] = (
                (scan_blocks[0, at] - row * (rows // block)) * spots
                + scan_blocks[1, at] - col * spots
            )
            return carry

        def place_of(at, carry):
            rank, ahead_of, matches = (jnp.zeros((), jnp.int32) for _ in range(3))
            for other in total:
                earlier = other < at
                rank += jnp.where((owners[other] == owners[at]) & earlier, 1, 0)
                ahead_of += jnp.where(spots_of[other] < spots_of[at], 1, 0)
                matches += jnp.where((spots_of[other] == spots_of[at]) & earlier, 1, 0)
            places[at] = ahead_of + matches
            follows[at] = jnp.minimum(matches, 1)
            slots_of[at] = owners[at] * pair_slots + rank
            return carry

        def sorted_at(at, carry):
            slot, joins = (jnp.zeros((), jnp.int32) for _ in range(2))
            for other in total:
                slot += jnp.where(places[other] == at, slots_of[other], 0)
                joins += jnp.where(places[other] == at, follows[other], 0)
            slots[at] = slot
            same[at] = joins
            return carry

        def count_at(at, carry):
            count, up_to = (jnp.zeros((), jnp.int32) for _ in range(2))
            for other in total:
                count += jnp.where(spots_of[other] == at, 1, 0)
                up_to += jnp.where(spots_of[other] <= at, 1, 0)
            counts[at] = count.astype(jnp.float32)
            ends[at] = jnp.maximum(up_to - 1, 0)
            return carry

        lax.fori_loop(0, len(total), spot_of, 0)
        lax.fori_loop(0, len(total), place_of, 0)
        lax.fori_loop(0, len(total), sorted_at, 0)
        lax.fori_loop(0, windows, count_at, 0)
        for number in range(windows):
            wide_counts[number : number + 1, :] = jnp.full((1, LANES), counts[number])
        for copy in count_copies:
            copy.start()

    def take_halos():
        for copy in halos:
            copy.wait()

        for part in range(2):
            extended[part, pl.ds(rows, block), pl.ds(0, cols)] = jnp.where(
                row < n_tx - 1, got_rows[part].astype(jnp.float32), 0.0
            )

        @pl.when(col == n_ty - 1)
        def _():
            extended[:, :, pl.ds(cols, block)] = jnp.zeros_like(extended[:, :, cols:])

        @pl.when(row == n_tx - 1)
        def _():
            extended[(slice(None), *corner)] = jnp.zeros((2, block, block), jnp.float32)

    above, left = (row > 0).astype(jnp.float32), (col > 0).astype(jnp.float32)

    def count_of(block_row, block_col):
        number = block_row % spots * spots + block_col % spots
        if block_row < 0 and block_col < 0:
            return got_counts[2, number : number + 1, :] * (above * left)
        if block_row < 0:
            return got_counts[0, number : number + 1, :] * above
        if block_col < 0:
            return got_counts[1, number : number + 1, :] * left
        return wide_counts[number : number + 1, :]

    def light_up():
        for block_row in range(rows // block):
            for block_col in range(spots):
                light = jnp.ones((block, block), jnp.float32)
                for down in range(2):
                    for right in range(2):
                        part = (pl.ds(down * block, block), pl.ds(right * block, block))
                        power = probe[(0, *part)] ** 2 + probe[(1, *part)] ** 2
                        light += count_of(block_row - down, block_col - right) * power
                spot = (pl.ds(block_row * block, block), pl.ds(block_col * block, block))
                inverse[spot] = 1.0 / light

    inner = spots - 1
    steps = {
        3: [functools.partial(relay_first, 0)],
        5: [functools.partial(turn, 1, 2, 0)],
        6: [send_far],
        7: [functools.partial(turn, 3, 2, 0), take_halos],
        8: [send_near],
        9: [functools.partial(turn, 1, 1, 0)],
        10: [functools.partial(turn, 3, 1, 0)],
        11: [functools.partial(turn, 1, 3, 0)],
        12: [functools.partial(turn, 3, 3, 0)],
        13: [functools.partial(relay_first, 1)],
        14: [functools.partial(turn, 2, 2, 0)],
    }

    for copy in take_tables:
        copy.wait()

    def forward_step(index, carry):
        edge = index - inner * inner
        inside = index < inner * inner
        at_row = jnp.where(inside, index // inner, jnp.where(edge < spots, inner, edge - spots))
        at_col = jnp.where(inside, lax.rem(index, inner), jnp.where(edge < spots, edge, inner))
        forward(at_row * spots + at_col)
        for when, work in steps.items():

            @pl.when(index == when)
            def _(work=work):
                for one in work:
                    one()

        return carry

    lax.fori_loop(0, windows, forward_step, 0)
    work_out_tables()
    for second in (1, 3):
        turn(2, second, 0)
    for first in (0, 1, 3, 2):
        relay_second(first, 0)
    for second in (2, 1, 3):
        for first in (1, 3):
            turn(first, second, 1)
    grads[...] = jnp.zeros_like(grads)
    for second in (2, 1, 3):
        turn(2, second, 1)
    send_last()
    for copy in count_copies:
        copy.wait()
    light_up()
    for copy in own_copies:
        copy.wait()

    sum_copies = [
        remote(source, target, (sum_send.at[number], sum_recv.at[number]), around(ONWARD[number]))
        for number, (source, target) in enumerate(
            ((sent_rows, got_down), (sent_right, got_right), (sent_corner, got_corner))
        )
    ]

    def round_lines(turn_of):
        return [
            pl.ds(pl.multiple_of(half * block + turn_of * depth, depth), depth)
            for half in range(2)
        ]

    def add_up(turn_of, index, carry):
        slot = slots[index]
        owner, rank = slot // pair_slots, lax.rem(slot, pair_slots)
        for half, lines in enumerate(round_lines(turn_of)):
            before = jnp.where(same[index] > 0, sums[jnp.maximum(index - 1, 0), lines], 0.0)
            plane = arrived[turn_of][owner, rank, pl.ds(half * depth, depth)]
            sums[index, lines] = before + plane.astype(jnp.float32)
        return carry

    def take_round(turn_of):
        for half in range(2):
            for kind in (0, 1, 3):
                piece(half, kind, None, 0, turn_of).wait_recv()
            for kind in (4, 5, 7):
                for first in range(SIDE):
                    piece(half, kind, first, None, turn_of).wait_recv()
        lax.fori_loop(0, sums.shape[0], functools.partial(add_up, turn_of), 0)

    def backward(step, carry):
        turn_of, index = step // windows, lax.rem(step, windows)

        for number in range(ROUNDS):

            @pl.when(step == number * windows)
            def _(number=number):
                take_round(number)

        for when, first in ((2, 0), (4, 1), (7, 3), (10, 2)):

            @pl.when(step == when)
            def _(first=first):
                relay_second(first, 1)

        interior = index - 2 * spots + 1
        edge = interior < 0
        at_row = jnp.where(
            edge, jnp.where(index < spots, inner, index - spots), interior // inner
        )
        at_col = jnp.where(
            edge, jnp.where(index < spots, index, inner), lax.rem(interior, inner)
        )
        number = at_row * spots + at_col

        @pl.when(step == windows + spots)
        def _():
            sent_rows[...] = grads[:, rows:, :cols].astype(jnp.bfloat16)
            sent_corner[...] = grads[:, rows:, cols:].astype(jnp.bfloat16)
            sum_copies[2].start()
            sum_copies[0].start()

        @pl.when(step == windows + 2 * spots - 1)
        def _():
            sent_right[...] = grads[:, :rows, cols:].astype(jnp.bfloat16)
            sum_copies[1].start()

        count = counts[number]
        used = jnp.minimum(count, 1.0)
        last = ends[number]
        parts = []
        for part in range(2):
            pieces = [
                far[number, part, lines].astype(jnp.float32) * count
                - phase[number, part, lines].astype(jnp.float32) * (sums[last, lines] * used)
                for lines in round_lines(turn_of)
            ]
            parts.append(jnp.concatenate(pieces, axis=0).astype(jnp.bfloat16))
        across = matmul(jnp.concatenate(parts, axis=1), ahead[...]).astype(jnp.bfloat16)
        near = matmul(
            split[turn_of], jnp.concatenate([across[:, :cells], across[:, cells:]], axis=0)
        )
        near_re, near_im = near[:cells], near[cells:]
        probe_re, probe_im = probe[0], probe[1]
        view = (
            pl.ds(pl.multiple_of(at_row * block, block), cells),
            pl.ds(pl.multiple_of(at_col * block, block), cells),
        )
        grads[(0, *view)] += probe_re * near_re + probe_im * near_im
        grads[(1, *view)] += probe_re * near_im - probe_im * near_re
        return carry

    lax.fori_loop(0, ROUNDS * windows, backward, 0)
    strips = cols // LANES

    def refresh(part, strip, start, count):
        lines, lanes = pl.ds(start, count), pl.ds(strip * LANES, LANES)
        updated = (
            extended[part, lines, lanes] - grads[part, lines, lanes] * inverse[lines, lanes]
        )
        first_field[part, strip, pl.ds(2 * RIM + start, count), :] = updated
        return updated

    for copy in sum_copies:
        copy.wait()
    for part in range(2):
        grads[part, :block, :cols] += got_down[part].astype(jnp.float32) * above
        grads[part, :rows, :block] += got_right[part].astype(jnp.float32) * left
        grads[part, :block, :block] += got_corner[part].astype(jnp.float32) * (above * left)
        column_rims[0, part] = refresh(part, 0, 0, rows).T[:RIM]
        column_rims[1, part] = refresh(part, strips - 1, 0, rows).T[LANES - RIM :]
        for strip in range(1, strips - 1):
            for start in (0, rows - RIM):
                refresh(part, strip, start, RIM)

    top, bottom = pl.ds(2 * RIM, RIM), pl.ds(2 * RIM + rows - RIM, RIM)
    main = pl.ds(0, strips)
    rim_copies = [
        remote(source, target, (rim_send.at[number], rim_recv.at[number]), around(AROUND[number]))
        for number, (source, target) in enumerate(
            (
                (first_field.at[:, main, top], got_tops.at[1]),
                (first_field.at[:, main, bottom], got_tops.at[0]),
                (column_rims.at[0], got_columns.at[1]),
                (column_rims.at[1], got_columns.at[0]),
                (first_field.at[:, 0, top], got_corners.at[3]),
                (first_field.at[:, strips - 1, top], got_corners.at[2]),
                (first_field.at[:, 0, bottom], got_corners.at[1]),
                (first_field.at[:, strips - 1, bottom], got_corners.at[0]),
            )
        )
    ]
    for copy in rim_copies:
        copy.start()
    for part in range(2):
        for strip in range(1, strips - 1):
            refresh(part, strip, RIM, rows - 2 * RIM)
    for copy in rim_copies:
        copy.wait()

    has_above, has_left = row > 0, col > 0
    has_below, has_right = row < n_tx - 1, col < n_ty - 1
    lane = lax.broadcasted_iota(jnp.int32, (RIM, LANES), 1)
    sublane = lax.broadcasted_iota(jnp.int32, (RIM, LANES), 0)
    on_right = lane < jnp.where(has_right, RIM, 0)
    on_left = lane >= jnp.where(has_left, LANES - RIM, LANES)
    beside = on_right | on_left
    ends_of_tile = ((0, RIM, has_above), (1, 2 * RIM + rows, has_below))
    for part in range(2):
        for number, start, exists in ends_of_tile:
            corner_cells = jnp.where(
                on_left, got_corners[2 * number, part],
                jnp.where(on_right, got_corners[2 * number + 1, part], 0.0),
            )
            spot = pl.ds(start, RIM)
            for strip in range(strips):
                first_field[part, strip, spot, :] = jnp.where(
                    exists, got_tops[number, part, strip], 0.0
                )
            first_field[part, strips, spot, :] = jnp.where(exists, corner_cells, 0.0)
        sides = jnp.concatenate(
            [
                jnp.where(has_right, got_columns[1, part], 0.0),
                jnp.zeros((LANES - 2 * RIM, rows), jnp.float32),
                jnp.where(has_left, got_columns[0, part], 0.0),
            ],
            axis=0,
        )
        first_field[part, strips, pl.ds(2 * RIM, rows), :] = sides.T

    everywhere = [(part, strip) for strip in range(strips + 1) for part in range(2)]
    blank = jnp.zeros((RIM, LANES), jnp.float32)

    def smooth(source, store, start, stop):
        def shifted(values, amount, edge):
            turned = {key: pltpu.roll(value, amount, axis=1) for key, value in values.items()}
            step = 1 if edge else -1
            return {
                (part, strip): jnp.where(
                    lane == edge, turned[part, (strip + step) % (strips + 1)], turned[part, strip]
                )
                for part, strip in everywhere
            }

        def fluxes(ahead_of, center):
            found = {}
            for strip in range(strips + 1):
                found[0, strip], found[1, strip] = flux(
                    *(ahead_of[part, strip] - center[part, strip] for part in range(2))
                )
            return found

        def chunk(number, earlier):
            start_row = pl.multiple_of((number + 1) * RIM, RIM)
            center, lower = (
                {
                    (part, strip): source[part, strip, pl.ds(start_row + offset, RIM), :]
                    for part, strip in everywhere
                }
                for offset in (0, 1)
            )
            down = fluxes(lower, center)
            right = fluxes(shifted(center, LANES - 1, LANES - 1), center)
            before = shifted(right, 1, 0)
            for at, key in enumerate(everywhere):
                up = jnp.where(
                    sublane == 0,
                    pltpu.roll(earlier[at], 1, axis=0),
                    pltpu.roll(down[key], 1, axis=0),
                )
                value = center[key] + TIME_STEP * ((down[key] - up) + (right[key] - before[key]))
                store(start_row, *key, value)
            return [down[key] for key in everywhere]

        lax.fori_loop(start, stop, chunk, [blank] * len(everywhere), unroll=UNROLL)

    def keep(target):
        def store(start_row, part, strip, value):
            if strip == strips:
                value = jnp.where(beside, value, 0.0)
            target[part, strip, pl.ds(start_row, RIM), :] = value

        return store

    def give(start_row, part, strip, value):
        if strip < strips:
            target = pl.multiple_of(jnp.maximum(start_row - 2 * RIM, 0), RIM)
            out[part, pl.ds(target, RIM), pl.ds(strip * LANES, LANES)] = value

    chunks = rows // RIM + 2
    now, later = first_field, second_field
    for _ in range(STEPS - 1):
        smooth(now, keep(later), 0, chunks)
        for _, start, exists in ends_of_tile:

            @pl.when(jnp.logical_not(exists))
            def _(start=start, later=later):
                later[:, :, pl.ds(start, RIM), :] = jnp.zeros(
                    (2, strips + 1, RIM, LANES), jnp.float32
                )

        now, later = later, now
    smooth(now, give, 0, chunks - 1)

    for turn_of in range(ROUNDS):
        for half in range(2):
            for kind in range(4):
                for second in range(SIDE):
                    piece(half, kind, None, second, turn_of).wait_send()
            for kind in range(4, 8):
                for first in range(SIDE):
                    piece(half, kind, first, None, turn_of).wait_send()


def whole_step(object_field, probe_field, amplitudes, scan_blocks, owner_rows):
    rows, cols = object_field.shape[1:]
    cells = probe_field.shape[1]
    block = cells // 2
    windows = rows // block * (cols // block)
    groups = lax.axis_size("tx")
    slots = amplitudes.shape[0] // groups
    sizes = (groups, lax.axis_size("ty"))
    positions = owner_rows.shape[0]
    tables = complex_tables(cells)
    assert groups == SIDE * SIDE
    vmem = pl.BlockSpec(memory_space=pltpu.VMEM)
    smem = pl.BlockSpec(memory_space=pltpu.SMEM)
    anywhere = pl.BlockSpec(memory_space=pltpu.HBM)
    narrow, wide = jnp.bfloat16, jnp.float32
    own = (groups, slots, cells, cells)
    part = (slots, block, cells)
    strips = [(2, block, cols), (2, rows, block), (2, block, block)]
    smoothed = (2, cols // LANES + 1, rows + 4 * RIM, LANES)
    return pl.pallas_call(
        functools.partial(step_kernel, sizes),
        out_shape=jax.ShapeDtypeStruct(object_field.shape, wide),
        in_specs=[smem] * 2 + [anywhere] * 6,
        out_specs=vmem,
        scratch_shapes=[
            pltpu.VMEM(probe_field.shape, wide),
            *(pltpu.VMEM(table.shape, narrow) for table in tables),
            *(
                pltpu.SMEM((length,), kind)
                for length, kind in (
                    (positions, jnp.int32), (positions, jnp.int32), (windows, jnp.int32),
                    (windows, wide), *((positions, jnp.int32) for _ in range(4)),
                )
            ),
            pltpu.VMEM((windows, LANES), wide),
            pltpu.VMEM((2, rows + block, cols + block), wide),
            pltpu.VMEM((2, block, cols), narrow),
            pltpu.VMEM((2, block, cols), narrow),
            pltpu.VMEM((STAGES, slots, cells, cells), wide),
            pltpu.VMEM(own, narrow),
            *(pltpu.VMEM((groups, slots, cells // ROUNDS, cells), narrow) for _ in range(ROUNDS)),
            pltpu.VMEM((2, SIDE - 1, SIDE - 1, *part), narrow),
            pltpu.VMEM((2, SIDE, *part), narrow),
            pltpu.VMEM((2, SIDE, *part), narrow),
            pltpu.VMEM((windows, 2, cells, cells), narrow),
            pltpu.VMEM((windows, 2, cells, cells), narrow),
            pltpu.VMEM((positions, cells, cells), wide),
            pltpu.VMEM((2, rows + block, cols + block), wide),
            pltpu.VMEM((rows, cols), wide),
            pltpu.VMEM((3, windows, LANES), wide),
            *(pltpu.VMEM(strip, narrow) for strip in strips[1:] + strips),
            pltpu.VMEM((2, 2, RIM, rows), wide),
            pltpu.VMEM((2, 2, cols // LANES, RIM, LANES), wide),
            pltpu.VMEM((2, 2, RIM, rows), wide),
            pltpu.VMEM((4, 2, RIM, LANES), wide),
            pltpu.VMEM(smoothed, wide),
            pltpu.VMEM(smoothed, wide),
            pltpu.SemaphoreType.DMA((STAGES,)),
            pltpu.SemaphoreType.DMA,
            pltpu.SemaphoreType.DMA((4,)),
            pltpu.SemaphoreType.DMA((ROUNDS, 2)),
            pltpu.SemaphoreType.DMA((6,)),
            pltpu.SemaphoreType.DMA((6,)),
            pltpu.SemaphoreType.DMA((ROUNDS, 2, 8 * SIDE)),
            pltpu.SemaphoreType.DMA((ROUNDS, 2, 8 * SIDE)),
            pltpu.SemaphoreType.DMA((3,)),
            pltpu.SemaphoreType.DMA((3,)),
            pltpu.SemaphoreType.DMA((8,)),
            pltpu.SemaphoreType.DMA((8,)),
        ],
        compiler_params=pltpu.CompilerParams(
            collective_id=1, has_side_effects=True, vmem_limit_bytes=GRANT << 20
        ),
        name="step",
    )(
        scan_blocks.T, owner_rows, object_field, amplitudes.reshape(own), probe_field,
        *tables
    )


def solution(mesh):
    in_specs = (
        P(None, "tx", "ty"),
        P(),
        P("tx", "ty", None),
        P(("tx", "ty"), None),
        P(("tx", "ty")),
    )
    out_specs = P(None, "tx", "ty")
    return jax.shard_map(whole_step, mesh=mesh, in_specs=in_specs, out_specs=out_specs, check_vma=False)
```

```python
import functools

import jax
import jax.numpy as jnp
import numpy as np
from jax import lax
from jax.experimental import pallas as pl
from jax.experimental.pallas import tpu as pltpu
from jax.sharding import PartitionSpec as P

STEPS = 4
ROUNDS = 2


KAPPA_SQ = 1.0
TIME_STEP = 0.2
AMPLITUDE_FLOOR = 0.5


def complex_tables(window_cells):
    counter = np.arange(window_cells)
    phases = counter[:, None] * counter[None, :] % window_cells
    angles = phases.astype(np.float32) * np.float32(2.0 * np.pi / window_cells)
    scaling = np.float32(1.0 / np.sqrt(window_cells))
    cosine, sine = (np.cos(angles) * scaling, np.sin(angles) * scaling)
    ahead = np.block([[cosine, sine], [-sine, cosine]])
    conjugate = np.block([[cosine, -sine], [sine, cosine]])
    lines = np.arange(2 * window_cells).reshape(2, 2, ROUNDS, -1)
    split = np.stack([conjugate[:, lines[:, :, number].reshape(-1)] for number in range(ROUNDS)])
    return tuple(jnp.asarray(table, jnp.bfloat16) for table in (ahead, conjugate, split))


def matmul(first, second):
    return jnp.dot(first, second, preferred_element_type=jnp.float32)


LANES = 128
RIM = 8
UNROLL = 6
GRANT = 55
MESH = pl.DeviceIdType.MESH
ONWARD = ((1, 0), (0, 1), (1, 1))
AROUND = ((-1, 0), (1, 0), (0, -1), (0, 1), (-1, -1), (-1, 1), (1, -1), (1, 1))


def flux(real, imag):
    weight = 1.0 / (1.0 + (real * real + imag * imag) * (1.0 / KAPPA_SQ))
    return weight * real, weight * imag


SIDE = 4
STAGES = 3
TAKEN = tuple(
    sorted(
        ((dx, dy) for dx in range(SIDE) for dy in range(SIDE)),
        key=lambda step: (step == (0, 0), 2 not in step, 0 in step),
    )
)


def step_kernel(
    sizes, scan_blocks, owners, field, amplitudes, probe_given, ahead_given, conjugate_given,
    split_given, out, probe, ahead, conjugate, split,
    slots, same, ends, counts, places, spots_of, slots_of, follows, wide_counts,
    extended, sent_rows, got_rows, staged, sent, arrived_first, arrived_second,
    held, passed, passed_again,
    far, phase, sums, grads, inverse, got_counts,
    sent_right, sent_corner, got_down, got_right, got_corner,
    column_rims, got_tops, got_columns, got_corners, first_field, second_field,
    stage_sem, field_sem, table_sem, own_sem, halo_send, halo_recv, send_sem, recv_sem,
    sum_send, sum_recv, rim_send, rim_recv,
):
    n_tx, n_ty = sizes
    cells = probe.shape[1]
    block = cells // 2
    rows, cols = extended.shape[1] - block, extended.shape[2] - block
    spots = cols // block
    windows = rows // block * spots
    row, col = lax.axis_index("tx"), lax.axis_index("ty")
    place = (row // SIDE, lax.rem(row, SIDE))

    def around(step):
        return (lax.rem(row + step[0] + n_tx, n_tx), lax.rem(col + step[1] + n_ty, n_ty))

    def owner_at(half, first, second):
        first, second = lax.rem(first + SIDE, SIDE), lax.rem(second + SIDE, SIDE)
        return first * SIDE + second if half == 0 else second * SIDE + first

    def load(number):
        dx, dy = TAKEN[number]
        home = owner_at(0, place[0] + dx, place[1] + dy)
        slot = number % STAGES
        return pltpu.make_async_copy(
            amplitudes.at[home], staged.at[slot], stage_sem.at[slot]
        )

    take_field = pltpu.make_async_copy(
        field, extended.at[:, pl.ds(0, rows), pl.ds(0, cols)], field_sem
    )
    take_tables = [
        pltpu.make_async_copy(source, target, table_sem.at[number])
        for number, (source, target) in enumerate(
            (
                (probe_given, probe), (ahead_given, ahead), (conjugate_given, conjugate),
                (split_given, split),
            )
        )
    ]
    for number in range(STAGES):
        load(number).start()
    take_field.start()

    barrier = pltpu.get_barrier_semaphore()
    partners = [around(step) for step in AROUND] + [
        (owner_at(half, place[half] + step, place[1 - half]), col)
        for half in range(2)
        for step in (1, -1)
    ]
    for partner in partners:
        pl.semaphore_signal(barrier, inc=1, device_id=partner, device_id_type=MESH)

    def remote(source, target, sems, partner):
        return pltpu.make_async_remote_copy(
            src_ref=source,
            dst_ref=target,
            send_sem=sems[0],
            recv_sem=sems[1],
            device_id=partner,
            device_id_type=MESH,
        )

    depth = block // ROUNDS
    arrived = (arrived_first, arrived_second)
    pair_slots = sent.shape[1]

    def piece(half, kind, first, second, turn_of):
        a, b = place[half], place[1 - half]
        inside = pl.ds(turn_of * depth, depth)
        lines = pl.ds(half * block + turn_of * depth, depth)
        landing = pl.ds(half * depth, depth)
        ring = 0 if kind < 4 else 1
        number = kind * SIDE + (second if ring == 0 else first)
        sems = (send_sem.at[turn_of, half, number], recv_sem.at[turn_of, half, number])
        if ring == 0:
            upward = 3 if (half, turn_of) == (1, 0) else 2
            step = 1 if kind == 0 or (kind > 1 and second < upward) else -1
            partner = owner_at(half, a + step, b)
            if kind == 3:
                source, owner = passed.at[half, second, :, inside], owner_at(half, a - step, b)
            else:
                offset = (1, -1, 2)[kind]
                source = sent.at[owner_at(half, a + offset, b + second), :, lines]
                owner = row
            if kind == 2:
                target = passed.at[half, second, :, inside]
            elif second == 0:
                target = arrived[turn_of].at[owner, :, landing]
            else:
                target = held.at[half, (0, 2, 2, 1)[kind], second - 1, :, inside]
        else:
            step = 1 if kind == 4 or (kind > 5 and first < 2) else -1
            partner = owner_at(half, a, b + step)
            offset = (1, 3, 2)[kind - 4] if kind < 7 else 0
            if kind == 7:
                source = passed_again.at[half, first, :, inside]
                owner = owner_at(half, a - first, b - step)
            else:
                source = (
                    sent.at[owner_at(half, a, b + offset), :, lines]
                    if first == 0
                    else held.at[half, first - 1, offset - 1, :, inside]
                )
                owner = owner_at(half, a - first, b)
            target = (
                passed_again.at[half, first, :, inside]
                if kind == 6
                else arrived[turn_of].at[owner, :, landing]
            )
        return remote(source, target, sems, (partner, col))

    corner = (pl.ds(rows, block), pl.ds(cols, block))
    halos = [
        remote(sent_rows, got_rows, (halo_send.at[0], halo_recv.at[0]), around((-1, 0))),
        remote(
            extended.at[:, pl.ds(0, rows), pl.ds(0, block)],
            extended.at[:, pl.ds(0, rows), pl.ds(cols, block)],
            (halo_send.at[1], halo_recv.at[1]), around((0, -1)),
        ),
        remote(
            extended.at[:, pl.ds(0, block), pl.ds(0, block)],
            extended.at[(slice(None), *corner)],
            (halo_send.at[2], halo_recv.at[2]), around((-1, -1)),
        ),
    ]

    count_copies = [
        remote(
            wide_counts, got_counts.at[number],
            (halo_send.at[3 + number], halo_recv.at[3 + number]), around(step),
        )
        for number, step in enumerate(ONWARD)
    ]

    for number, (dx, dy) in enumerate(TAKEN):
        slot = number % STAGES
        home = owner_at(0, place[0] + dx, place[1] + dy)
        load(number).wait()

        def cast(index, carry):
            sent[home, index] = staged[slot, index].astype(jnp.bfloat16)
            return carry

        lax.fori_loop(0, sent.shape[1], cast, 0)
        if number == 0:
            pl.semaphore_wait(barrier, len(partners))
        if number + STAGES < len(TAKEN):
            load(number + STAGES).start()
        for half, (first, second) in enumerate(((dx, dy), (dy, dx))):
            if first:
                piece(half, (0, 2, 1)[first - 1], None, second, 0).start()
        if number == 4:
            for copy in take_tables:
                copy.start()
            take_field.wait()
            sent_rows[...] = extended[:, :block, :cols].astype(jnp.bfloat16)
        if number == 6:
            for copy in halos:
                copy.start()

    own_copies = [
        pltpu.make_async_copy(
            sent.at[row, :, pl.ds(half * block + turn_of * depth, depth)],
            arrived[turn_of].at[row, :, pl.ds(half * depth, depth)],
            own_sem.at[turn_of, half],
        )
        for turn_of in range(ROUNDS)
        for half in range(2)
    ]
    for copy in own_copies:
        copy.start()

    def forward(number):
        start_row = pl.multiple_of(number // spots * block, block)
        start_col = pl.multiple_of(lax.rem(number, spots) * block, block)
        view = (pl.ds(start_row, cells), pl.ds(start_col, cells))
        window_re, window_im = extended[(0, *view)], extended[(1, *view)]
        probe_re, probe_im = probe[0], probe[1]
        wave_re = (probe_re * window_re - probe_im * window_im).astype(jnp.bfloat16)
        wave_im = (probe_re * window_im + probe_im * window_re).astype(jnp.bfloat16)
        half = matmul(ahead[...], jnp.concatenate([wave_re, wave_im], axis=0)).astype(
            jnp.bfloat16
        )
        waves = matmul(jnp.concatenate([half[:cells], half[cells:]], axis=1), conjugate[...])
        far_re, far_im = waves[:, :cells], waves[:, cells:]
        inverse = jnp.minimum(
            lax.rsqrt(far_re * far_re + far_im * far_im), 1.0 / AMPLITUDE_FLOOR
        )
        far[number, 0] = far_re.astype(jnp.bfloat16)
        far[number, 1] = far_im.astype(jnp.bfloat16)
        phase[number, 0] = (far_re * inverse).astype(jnp.bfloat16)
        phase[number, 1] = (far_im * inverse).astype(jnp.bfloat16)

    def send_far():
        for second in range(SIDE):
            for half in range(2):
                piece(half, 2, None, second, 1).start()

    def send_near():
        for second in (2, 1, 3):
            for kind in range(2):
                for half in range(2):
                    piece(half, kind, None, second, 1).start()

    def send_last():
        for half in range(2):
            for kind in range(2):
                piece(half, kind, None, 0, 1).start()
            for kind in (4, 5):
                piece(half, kind, 0, None, 1).start()

    def relay_first(turn_of):
        for second in range(SIDE):
            for half in range(2):
                piece(half, 2, None, second, turn_of).wait_recv()
                piece(half, 3, None, second, turn_of).start()
        for kind in (6,) if turn_of == ROUNDS - 1 else (6, 4, 5):
            for half in range(2):
                piece(half, kind, 0, None, turn_of).start()

    def turn(first, second, turn_of):
        arrival = (0, 3, 1)[first - 1]
        kind = {1: 4, 2: 6, 3: 5}[second]
        for half in range(2):
            piece(half, arrival, None, second, turn_of).wait_recv()
            piece(half, kind, first, None, turn_of).start()

    def relay_second(first, turn_of):
        for half in range(2):
            piece(half, 6, first, None, turn_of).wait_recv()
            piece(half, 7, first, None, turn_of).start()

    def work_out_tables():
        total = range(owners.shape[0])

        def spot_of(at, carry):
            spots_of[at] = (
                (scan_blocks[0, at] - row * (rows // block)) * spots
                + scan_blocks[1, at] - col * spots
            )
            return carry

        def place_of(at, carry):
            rank, ahead_of, matches = (jnp.zeros((), jnp.int32) for _ in range(3))
            for other in total:
                earlier = other < at
                rank += jnp.where((owners[other] == owners[at]) & earlier, 1, 0)
                ahead_of += jnp.where(spots_of[other] < spots_of[at], 1, 0)
                matches += jnp.where((spots_of[other] == spots_of[at]) & earlier, 1, 0)
            places[at] = ahead_of + matches
            follows[at] = jnp.minimum(matches, 1)
            slots_of[at] = owners[at] * pair_slots + rank
            return carry

        def sorted_at(at, carry):
            slot, joins = (jnp.zeros((), jnp.int32) for _ in range(2))
            for other in total:
                slot += jnp.where(places[other] == at, slots_of[other], 0)
                joins += jnp.where(places[other] == at, follows[other], 0)
            slots[at] = slot
            same[at] = joins
            return carry

        def count_at(at, carry):
            count, up_to = (jnp.zeros((), jnp.int32) for _ in range(2))
            for other in total:
                count += jnp.where(spots_of[other] == at, 1, 0)
                up_to += jnp.where(spots_of[other] <= at, 1, 0)
            counts[at] = count.astype(jnp.float32)
            ends[at] = jnp.maximum(up_to - 1, 0)
            return carry

        lax.fori_loop(0, len(total), spot_of, 0)
        lax.fori_loop(0, len(total), place_of, 0)
        lax.fori_loop(0, len(total), sorted_at, 0)
        lax.fori_loop(0, windows, count_at, 0)
        for number in range(windows):
            wide_counts[number : number + 1, :] = jnp.full((1, LANES), counts[number])
        for copy in count_copies:
            copy.start()

    def take_halos():
        for copy in halos:
            copy.wait()

        for part in range(2):
            extended[part, pl.ds(rows, block), pl.ds(0, cols)] = jnp.where(
                row < n_tx - 1, got_rows[part].astype(jnp.float32), 0.0
            )

        @pl.when(col == n_ty - 1)
        def _():
            extended[:, :, pl.ds(cols, block)] = jnp.zeros_like(extended[:, :, cols:])

        @pl.when(row == n_tx - 1)
        def _():
            extended[(slice(None), *corner)] = jnp.zeros((2, block, block), jnp.float32)

    above, left = (row > 0).astype(jnp.float32), (col > 0).astype(jnp.float32)

    def count_of(block_row, block_col):
        number = block_row % spots * spots + block_col % spots
        if block_row < 0 and block_col < 0:
            return got_counts[2, number : number + 1, :] * (above * left)
        if block_row < 0:
            return got_counts[0, number : number + 1, :] * above
        if block_col < 0:
            return got_counts[1, number : number + 1, :] * left
        return wide_counts[number : number + 1, :]

    def light_up():
        for block_row in range(rows // block):
            for block_col in range(spots):
                light = jnp.ones((block, block), jnp.float32)
                for down in range(2):
                    for right in range(2):
                        part = (pl.ds(down * block, block), pl.ds(right * block, block))
                        power = probe[(0, *part)] ** 2 + probe[(1, *part)] ** 2
                        light += count_of(block_row - down, block_col - right) * power
                spot = (pl.ds(block_row * block, block), pl.ds(block_col * block, block))
                inverse[spot] = 1.0 / light

    inner = spots - 1
    steps = {
        3: [functools.partial(relay_first, 0)],
        5: [functools.partial(turn, 1, 2, 0)],
        6: [send_far],
        7: [functools.partial(turn, 3, 2, 0), take_halos],
        8: [send_near],
        9: [functools.partial(turn, 1, 1, 0)],
        10: [functools.partial(turn, 3, 1, 0)],
        11: [functools.partial(turn, 1, 3, 0)],
        12: [functools.partial(turn, 3, 3, 0)],
        13: [functools.partial(relay_first, 1)],
        14: [functools.partial(turn, 2, 2, 0)],
    }

    for copy in take_tables:
        copy.wait()

    def forward_step(index, carry):
        edge = index - inner * inner
        inside = index < inner * inner
        at_row = jnp.where(inside, index // inner, jnp.where(edge < spots, inner, edge - spots))
        at_col = jnp.where(inside, lax.rem(index, inner), jnp.where(edge < spots, edge, inner))
        forward(at_row * spots + at_col)
        for when, work in steps.items():

            @pl.when(index == when)
            def _(work=work):
                for one in work:
                    one()

        return carry

    lax.fori_loop(0, windows, forward_step, 0)
    work_out_tables()
    for second in (1, 3):
        turn(2, second, 0)
    for first in (0, 1, 3, 2):
        relay_second(first, 0)
    for second in (2, 1, 3):
        for first in (1, 3):
            turn(first, second, 1)
    grads[...] = jnp.zeros_like(grads)
    for second in (2, 1, 3):
        turn(2, second, 1)
    send_last()
    for copy in count_copies:
        copy.wait()
    light_up()
    for copy in own_copies:
        copy.wait()

    across_blocks = [pl.ds(number * block, block) for number in range(spots)]
    ways = [(sent_right, got_right, ONWARD[1]), (sent_corner, got_corner, ONWARD[2])] + [
        (sent_rows.at[:, :, lanes], got_down.at[:, :, lanes], ONWARD[0])
        for lanes in across_blocks
    ]
    sum_copies = [
        remote(source, target, (sum_send.at[number], sum_recv.at[number]), around(step))
        for number, (source, target, step) in enumerate(ways)
    ]

    def round_lines(turn_of):
        return [
            pl.ds(pl.multiple_of(half * block + turn_of * depth, depth), depth)
            for half in range(2)
        ]

    def add_up(turn_of, index, carry):
        slot = slots[index]
        owner, rank = slot // pair_slots, lax.rem(slot, pair_slots)
        for half, lines in enumerate(round_lines(turn_of)):
            before = jnp.where(same[index] > 0, sums[jnp.maximum(index - 1, 0), lines], 0.0)
            plane = arrived[turn_of][owner, rank, pl.ds(half * depth, depth)]
            sums[index, lines] = before + plane.astype(jnp.float32)
        return carry

    def take_round(turn_of):
        for half in range(2):
            for kind in (0, 1, 3):
                piece(half, kind, None, 0, turn_of).wait_recv()
            for kind in (4, 5, 7):
                for first in range(SIDE):
                    piece(half, kind, first, None, turn_of).wait_recv()
        lax.fori_loop(0, sums.shape[0], functools.partial(add_up, turn_of), 0)

    def backward(step, carry):
        turn_of, index = step // windows, lax.rem(step, windows)

        for number in range(ROUNDS):

            @pl.when(step == number * windows)
            def _(number=number):
                take_round(number)

        for when, first in ((2, 0), (4, 1), (7, 3), (10, 2)):

            @pl.when(step == when)
            def _(first=first):
                relay_second(first, 1)

        interior = index - 2 * spots + 1
        edge = interior < 0
        at_row = jnp.where(
            edge, jnp.where(index < spots, inner, index - spots), interior // inner
        )
        at_col = jnp.where(
            edge, jnp.where(index < spots, index, inner), lax.rem(interior, inner)
        )
        number = at_row * spots + at_col

        for part, lanes in enumerate(across_blocks):

            @pl.when(step == windows + part + 1)
            def _(part=part, lanes=lanes):
                sent_rows[:, :, lanes] = grads[:, rows:, lanes].astype(jnp.bfloat16)
                sum_copies[2 + part].start()

        @pl.when(step == windows + spots)
        def _():
            sent_corner[...] = grads[:, rows:, cols:].astype(jnp.bfloat16)
            sum_copies[1].start()

        @pl.when(step == windows + 2 * spots - 1)
        def _():
            sent_right[...] = grads[:, :rows, cols:].astype(jnp.bfloat16)
            sum_copies[0].start()

        count = counts[number]
        used = jnp.minimum(count, 1.0)
        last = ends[number]
        parts = []
        for part in range(2):
            pieces = [
                far[number, part, lines].astype(jnp.float32) * count
                - phase[number, part, lines].astype(jnp.float32) * (sums[last, lines] * used)
                for lines in round_lines(turn_of)
            ]
            parts.append(jnp.concatenate(pieces, axis=0).astype(jnp.bfloat16))
        across = matmul(jnp.concatenate(parts, axis=1), ahead[...]).astype(jnp.bfloat16)
        near = matmul(
            split[turn_of], jnp.concatenate([across[:, :cells], across[:, cells:]], axis=0)
        )
        near_re, near_im = near[:cells], near[cells:]
        probe_re, probe_im = probe[0], probe[1]
        view = (
            pl.ds(pl.multiple_of(at_row * block, block), cells),
            pl.ds(pl.multiple_of(at_col * block, block), cells),
        )
        grads[(0, *view)] += probe_re * near_re + probe_im * near_im
        grads[(1, *view)] += probe_re * near_im - probe_im * near_re
        return carry

    lax.fori_loop(0, ROUNDS * windows, backward, 0)
    strips = cols // LANES

    def refresh(part, strip, start, count):
        lines, lanes = pl.ds(start, count), pl.ds(strip * LANES, LANES)
        updated = (
            extended[part, lines, lanes] - grads[part, lines, lanes] * inverse[lines, lanes]
        )
        first_field[part, strip, pl.ds(2 * RIM + start, count), :] = updated
        return updated

    for copy in sum_copies:
        copy.wait()
    for part in range(2):
        grads[part, :block, :cols] += got_down[part].astype(jnp.float32) * above
        grads[part, :rows, :block] += got_right[part].astype(jnp.float32) * left
        grads[part, :block, :block] += got_corner[part].astype(jnp.float32) * (above * left)
        column_rims[0, part] = refresh(part, 0, 0, rows).T[:RIM]
        column_rims[1, part] = refresh(part, strips - 1, 0, rows).T[LANES - RIM :]
        for strip in range(1, strips - 1):
            for start in (0, rows - RIM):
                refresh(part, strip, start, RIM)

    top, bottom = pl.ds(2 * RIM, RIM), pl.ds(2 * RIM + rows - RIM, RIM)
    main = pl.ds(0, strips)
    rim_copies = [
        remote(source, target, (rim_send.at[number], rim_recv.at[number]), around(AROUND[number]))
        for number, (source, target) in enumerate(
            (
                (first_field.at[:, main, top], got_tops.at[1]),
                (first_field.at[:, main, bottom], got_tops.at[0]),
                (column_rims.at[0], got_columns.at[1]),
                (column_rims.at[1], got_columns.at[0]),
                (first_field.at[:, 0, top], got_corners.at[3]),
                (first_field.at[:, strips - 1, top], got_corners.at[2]),
                (first_field.at[:, 0, bottom], got_corners.at[1]),
                (first_field.at[:, strips - 1, bottom], got_corners.at[0]),
            )
        )
    ]
    for copy in rim_copies:
        copy.start()
    for part in range(2):
        for strip in range(1, strips - 1):
            refresh(part, strip, RIM, rows - 2 * RIM)
    for copy in rim_copies:
        copy.wait()

    has_above, has_left = row > 0, col > 0
    has_below, has_right = row < n_tx - 1, col < n_ty - 1
    lane = lax.broadcasted_iota(jnp.int32, (RIM, LANES), 1)
    sublane = lax.broadcasted_iota(jnp.int32, (RIM, LANES), 0)
    on_right = lane < jnp.where(has_right, RIM, 0)
    on_left = lane >= jnp.where(has_left, LANES - RIM, LANES)
    beside = on_right | on_left
    ends_of_tile = ((0, RIM, has_above), (1, 2 * RIM + rows, has_below))
    for part in range(2):
        for number, start, exists in ends_of_tile:
            corner_cells = jnp.where(
                on_left, got_corners[2 * number, part],
                jnp.where(on_right, got_corners[2 * number + 1, part], 0.0),
            )
            spot = pl.ds(start, RIM)
            for strip in range(strips):
                first_field[part, strip, spot, :] = jnp.where(
                    exists, got_tops[number, part, strip], 0.0
                )
            first_field[part, strips, spot, :] = jnp.where(exists, corner_cells, 0.0)
        sides = jnp.concatenate(
            [
                jnp.where(has_right, got_columns[1, part], 0.0),
                jnp.zeros((LANES - 2 * RIM, rows), jnp.float32),
                jnp.where(has_left, got_columns[0, part], 0.0),
            ],
            axis=0,
        )
        first_field[part, strips, pl.ds(2 * RIM, rows), :] = sides.T

    everywhere = [(part, strip) for strip in range(strips + 1) for part in range(2)]
    blank = jnp.zeros((RIM, LANES), jnp.float32)

    def smooth(source, store, start, stop):
        def shifted(values, amount, edge):
            turned = {key: pltpu.roll(value, amount, axis=1) for key, value in values.items()}
            step = 1 if edge else -1
            return {
                (part, strip): jnp.where(
                    lane == edge, turned[part, (strip + step) % (strips + 1)], turned[part, strip]
                )
                for part, strip in everywhere
            }

        def fluxes(ahead_of, center):
            found = {}
            for strip in range(strips + 1):
                found[0, strip], found[1, strip] = flux(
                    *(ahead_of[part, strip] - center[part, strip] for part in range(2))
                )
            return found

        def chunk(number, earlier):
            start_row = pl.multiple_of((number + 1) * RIM, RIM)
            center, lower = (
                {
                    (part, strip): source[part, strip, pl.ds(start_row + offset, RIM), :]
                    for part, strip in everywhere
                }
                for offset in (0, 1)
            )
            down = fluxes(lower, center)
            right = fluxes(shifted(center, LANES - 1, LANES - 1), center)
            before = shifted(right, 1, 0)
            for at, key in enumerate(everywhere):
                up = jnp.where(
                    sublane == 0,
                    pltpu.roll(earlier[at], 1, axis=0),
                    pltpu.roll(down[key], 1, axis=0),
                )
                value = center[key] + TIME_STEP * ((down[key] - up) + (right[key] - before[key]))
                store(start_row, *key, value)
            return [down[key] for key in everywhere]

        lax.fori_loop(start, stop, chunk, [blank] * len(everywhere), unroll=UNROLL)

    def keep(target):
        def store(start_row, part, strip, value):
            if strip == strips:
                value = jnp.where(beside, value, 0.0)
            target[part, strip, pl.ds(start_row, RIM), :] = value

        return store

    def give(start_row, part, strip, value):
        if strip < strips:
            target = pl.multiple_of(jnp.maximum(start_row - 2 * RIM, 0), RIM)
            out[part, pl.ds(target, RIM), pl.ds(strip * LANES, LANES)] = value

    chunks = rows // RIM + 2
    now, later = first_field, second_field
    for _ in range(STEPS - 1):
        smooth(now, keep(later), 0, chunks)
        for _, start, exists in ends_of_tile:

            @pl.when(jnp.logical_not(exists))
            def _(start=start, later=later):
                later[:, :, pl.ds(start, RIM), :] = jnp.zeros(
                    (2, strips + 1, RIM, LANES), jnp.float32
                )

        now, later = later, now
    smooth(now, give, 0, chunks - 1)

    for turn_of in range(ROUNDS):
        for half in range(2):
            for kind in range(4):
                for second in range(SIDE):
                    piece(half, kind, None, second, turn_of).wait_send()
            for kind in range(4, 8):
                for first in range(SIDE):
                    piece(half, kind, first, None, turn_of).wait_send()


def whole_step(object_field, probe_field, amplitudes, scan_blocks, owner_rows):
    rows, cols = object_field.shape[1:]
    cells = probe_field.shape[1]
    block = cells // 2
    windows = rows // block * (cols // block)
    groups = lax.axis_size("tx")
    slots = amplitudes.shape[0] // groups
    sizes = (groups, lax.axis_size("ty"))
    positions = owner_rows.shape[0]
    tables = complex_tables(cells)
    assert groups == SIDE * SIDE
    vmem = pl.BlockSpec(memory_space=pltpu.VMEM)
    smem = pl.BlockSpec(memory_space=pltpu.SMEM)
    anywhere = pl.BlockSpec(memory_space=pltpu.HBM)
    narrow, wide = jnp.bfloat16, jnp.float32
    own = (groups, slots, cells, cells)
    part = (slots, block, cells)
    strips = [(2, block, cols), (2, rows, block), (2, block, block)]
    smoothed = (2, cols // LANES + 1, rows + 4 * RIM, LANES)
    return pl.pallas_call(
        functools.partial(step_kernel, sizes),
        out_shape=jax.ShapeDtypeStruct(object_field.shape, wide),
        in_specs=[smem] * 2 + [anywhere] * 6,
        out_specs=vmem,
        scratch_shapes=[
            pltpu.VMEM(probe_field.shape, wide),
            *(pltpu.VMEM(table.shape, narrow) for table in tables),
            *(
                pltpu.SMEM((length,), kind)
                for length, kind in (
                    (positions, jnp.int32), (positions, jnp.int32), (windows, jnp.int32),
                    (windows, wide), *((positions, jnp.int32) for _ in range(4)),
                )
            ),
            pltpu.VMEM((windows, LANES), wide),
            pltpu.VMEM((2, rows + block, cols + block), wide),
            pltpu.VMEM((2, block, cols), narrow),
            pltpu.VMEM((2, block, cols), narrow),
            pltpu.VMEM((STAGES, slots, cells, cells), wide),
            pltpu.VMEM(own, narrow),
            *(pltpu.VMEM((groups, slots, cells // ROUNDS, cells), narrow) for _ in range(ROUNDS)),
            pltpu.VMEM((2, SIDE - 1, SIDE - 1, *part), narrow),
            pltpu.VMEM((2, SIDE, *part), narrow),
            pltpu.VMEM((2, SIDE, *part), narrow),
            pltpu.VMEM((windows, 2, cells, cells), narrow),
            pltpu.VMEM((windows, 2, cells, cells), narrow),
            pltpu.VMEM((positions, cells, cells), wide),
            pltpu.VMEM((2, rows + block, cols + block), wide),
            pltpu.VMEM((rows, cols), wide),
            pltpu.VMEM((3, windows, LANES), wide),
            *(pltpu.VMEM(strip, narrow) for strip in strips[1:] + strips),
            pltpu.VMEM((2, 2, RIM, rows), wide),
            pltpu.VMEM((2, 2, cols // LANES, RIM, LANES), wide),
            pltpu.VMEM((2, 2, RIM, rows), wide),
            pltpu.VMEM((4, 2, RIM, LANES), wide),
            pltpu.VMEM(smoothed, wide),
            pltpu.VMEM(smoothed, wide),
            pltpu.SemaphoreType.DMA((STAGES,)),
            pltpu.SemaphoreType.DMA,
            pltpu.SemaphoreType.DMA((4,)),
            pltpu.SemaphoreType.DMA((ROUNDS, 2)),
            pltpu.SemaphoreType.DMA((6,)),
            pltpu.SemaphoreType.DMA((6,)),
            pltpu.SemaphoreType.DMA((ROUNDS, 2, 8 * SIDE)),
            pltpu.SemaphoreType.DMA((ROUNDS, 2, 8 * SIDE)),
            pltpu.SemaphoreType.DMA((2 + cols // block,)),
            pltpu.SemaphoreType.DMA((2 + cols // block,)),
            pltpu.SemaphoreType.DMA((8,)),
            pltpu.SemaphoreType.DMA((8,)),
        ],
        compiler_params=pltpu.CompilerParams(
            collective_id=1, has_side_effects=True, vmem_limit_bytes=GRANT << 20
        ),
        name="step",
    )(
        scan_blocks.T, owner_rows, object_field, amplitudes.reshape(own), probe_field,
        *tables
    )


def solution(mesh):
    in_specs = (
        P(None, "tx", "ty"),
        P(),
        P("tx", "ty", None),
        P(("tx", "ty"), None),
        P(("tx", "ty")),
    )
    out_specs = P(None, "tx", "ty")
    return jax.shard_map(whole_step, mesh=mesh, in_specs=in_specs, out_specs=out_specs, check_vma=False)
```
